32 devices in a mesh: dp: 8 (over y, x, core), mp: 4 (over z).
Axes of the slice: x: 2, y: 2, z: 4, core: 2. Of those that a mesh axis runs over, the one named last changes fastest.
Arguments:
- hidden_in: bfloat16 [4, 2048, 1, 768], P(None, ('dp', 'mp')), may hold values from -6 to 6
- cotangent: bfloat16 [4, 2048, 1, 768], P(None, ('dp', 'mp')), may hold values from -6 to 6
- lengths: int32 [4, 1], replicated, may hold values from 512 to 2048, as said below
- qkv_weight: bfloat16 [3, 768, 768], P(None, 'dp', 'mp'), may hold values from -0.21875 to 0.21875
- out_weight: bfloat16 [768, 768], P('mp', 'dp'), may hold values from -6 to 6
- gate_up_weight: bfloat16 [2, 768, 3072], P(None, 'dp', 'mp'), may hold values from -0.21875 to 0.21875
- down_weight: bfloat16 [3072, 768], P('mp', 'dp'), may hold values from -0.21875 to 0.21875
- norm_gain: bfloat16 [2, 768], P(None, 'dp'), may hold values from 0.5 to 1.5
- norm_bias: bfloat16 [2, 768], P(None, 'dp'), may hold values from -1.796875 to 1.796875
Outputs:
- layer_out: bfloat16 [4, 2048, 1, 768], P(None, ('dp', 'mp'))
- input_grad: float32 [4, 2048, 1, 768], P(None, ('dp', 'mp'))
- qkv_grad: float32 [3, 768, 768], P(None, 'dp', 'mp')
- out_grad: float32 [768, 768], P('mp', 'dp')
- gate_up_grad: float32 [2, 768, 3072], P(None, 'dp', 'mp')
- down_grad: float32 [3072, 768], P('mp', 'dp')
- gain_grad: float32 [2, 768], P(None, 'dp')
- bias_grad: float32 [2, 768], P(None, 'dp')
The draws below stay inside these ranges and needn't reach their ends.
Inputs may be any that keep to these rules, and one draw needn't show every extreme that they name: `lengths`: real slots of each sequence; one sequence has exactly 2048 and one exactly 512 in every draw.
All inputs are finite; a program needn't handle non-finite values.
Results may differ from the reference program's by a relative error of at most 0.029.
Values may be sent and summed in bfloat16 or wider, within the bound.
No kernel may reach another device: no remote copies, remote signals or barrier semaphores. Data moves between devices by JAX's collectives and lax.ppermute only.
A program may use at most 320 MiB of HBM per device.

```python
import jax
import jax.numpy as jnp
from jax import lax

D = 768
HEADS = 12
HEAD_DIM = 64
FF = 3072
MB = 4
SEQS = 1
LENGTH = 2048


def draw_lengths(key, part):
    first_key, second_key = jax.random.split(jax.random.fold_in(key, 11))
    drawn_lengths = jax.random.randint(first_key, (MB * SEQS,), LENGTH // 4, LENGTH + 1)
    shuffle = jax.random.permutation(second_key, MB * SEQS)
    drawn_lengths = drawn_lengths.at[shuffle[0]].set(LENGTH).at[shuffle[1]].set(LENGTH // 4)
    return drawn_lengths.reshape(MB, SEQS).astype(jnp.int32)


def block_levels(stream_key, shape, cuts, low, high):
    loudness = 1.0
    for position, parts in cuts:
        draws = jax.random.uniform(jax.random.fold_in(jax.random.fold_in(stream_key, 6), position), (parts,), jnp.float32, low / len(cuts), high / len(cuts))
        loudness = loudness * jnp.repeat(jnp.exp(draws), shape[position] // parts).reshape((-1,) + (1,) * (len(shape) - 1 - position))
    return loudness


def noise(rng, extent, spread, most, pieces=(), kind=jnp.bfloat16):
    result = spread * jax.random.normal(rng, extent, jnp.float32)
    if pieces:
        result = result * block_levels(rng, extent, pieces, -0.22, 0.18)
    return jnp.clip(result, -most, most).astype(kind)


def setup_inputs(seed: int = 0) -> dict:
    seeds = jax.random.split(jax.random.key(seed), 10)
    hidden_in = noise(seeds[0], (MB, LENGTH, SEQS, D), 1.0, 6.0, ((1, 32),))
    cotangent = noise(seeds[1], (MB, LENGTH, SEQS, D), 1.0, 6.0, ((1, 32),))
    lengths = draw_lengths(jax.random.fold_in(seeds[9], 71), 0)
    qkv_weight = noise(seeds[3], (3, D, D), D ** -0.5, 0.21875, ((1, 8), (2, 4)))
    out_weight = noise(seeds[4], (D, D), (max(1, D * 4 // LENGTH)) ** -0.5, 6.0, ((0, 4), (1, 8)))
    gate_up_weight = noise(seeds[5], (2, D, FF), D ** -0.5, 0.21875, ((1, 8), (2, 4)))
    down_weight = noise(seeds[6], (FF, D), (FF // 4) ** -0.5, 0.21875, ((0, 4), (1, 8)))
    norm_gain = jnp.clip(1.0 + 0.1 * jax.random.normal(seeds[7], (2, D), jnp.float32), 0.5, 1.5).astype(jnp.bfloat16)
    norm_bias = noise(seeds[8], (2, D), 0.3, 1.796875, ((1, 8),))
    return dict(hidden_in=hidden_in, cotangent=cotangent, lengths=lengths, qkv_weight=qkv_weight, out_weight=out_weight, gate_up_weight=gate_up_weight, down_weight=down_weight, norm_gain=norm_gain, norm_bias=norm_bias)


norm_eps = 1e-12
rope_base = 1000.0
masked_score = -1e+30

@jax.custom_vjp
def reduced_precision(v):
    return lax.optimization_barrier(v.astype(jnp.bfloat16)).astype(jnp.float32)

@jax.custom_vjp
def reduced_backward(v):
    return v

def low_keep(v):
    return (reduced_precision(v), None)

def low_pass(kept, grad):
    return (grad,)

def back_keep(v):
    return (v, None)

def back_low(kept, grad):
    return (reduced_precision(grad),)
reduced_precision.defvjp(low_keep, low_pass)
reduced_backward.defvjp(back_keep, back_low)

def rope_tables(positions, half_dim):
    exponent = jnp.arange(half_dim, dtype=jnp.float32) * (1.0 / half_dim)
    inverse = jnp.power(rope_base, -exponent)
    angles = positions[:, None] * inverse[None, :]
    return (jnp.cos(angles), jnp.sin(angles))

def rotate(vectors, cosine, sine_table):
    half_dim = vectors.shape[-1] // 2
    first_half = vectors[..., :half_dim]
    second_half = vectors[..., half_dim:]
    return jnp.concatenate([first_half * cosine - second_half * sine_table, second_half * cosine + first_half * sine_table], axis=-1)

def normalize(residual_stream, gain_row, bias_row):
    center = residual_stream - lax.optimization_barrier(jnp.mean(residual_stream, axis=-1, keepdims=True))
    inv_std = lax.rsqrt(lax.optimization_barrier(jnp.mean(center * center, axis=-1, keepdims=True)) + norm_eps)
    return center * inv_std * gain_row + bias_row

def split_heads(rows):
    return rows.reshape(rows.shape[0], rows.shape[1], HEADS, HEAD_DIM).transpose(0, 2, 1, 3)

def merge_heads(heads):
    return heads.transpose(0, 2, 1, 3).reshape(heads.shape[0], heads.shape[2], HEADS * HEAD_DIM)

def block_layer(residual_stream, query_key_value_matrix, output_matrix, gate_up_matrix, down_matrix, gain_rows, biases, seq_lengths):
    highest_precision = lax.Precision.HIGHEST
    projected_rows = reduced_backward(jnp.einsum('pfr,hrw->hpfw', residual_stream, query_key_value_matrix, precision=highest_precision))
    positions = jnp.arange(LENGTH, dtype=jnp.int32).astype(jnp.float32)
    cosine, sine_table = rope_tables(positions, HEAD_DIM // 2)
    query_heads = reduced_precision(rotate(split_heads(projected_rows[0]), cosine, sine_table))
    key_heads = reduced_precision(rotate(split_heads(projected_rows[1]), cosine, sine_table))
    value_heads = reduced_precision(split_heads(projected_rows[2]))
    key_ok = (jnp.arange(LENGTH, dtype=jnp.int32)[None, :] < seq_lengths[:, None])[:, None, None, :]
    score_scale = HEAD_DIM ** (-0.5)

    def attend(query_block):
        raw_scores = reduced_backward(jnp.einsum('shqd,shkd->shqk', query_block, key_heads, precision=highest_precision))
        scores = jnp.where(key_ok, raw_scores * score_scale, masked_score)
        row_max = lax.optimization_barrier(jnp.max(scores, axis=-1, keepdims=True))
        exp_scores = jnp.exp(scores - row_max)
        probabilities = exp_scores / lax.optimization_barrier(jnp.sum(exp_scores, axis=-1, keepdims=True))
        return jnp.einsum('shqk,shkd->shqd', reduced_precision(probabilities), value_heads, precision=highest_precision)
    query_rows = min(512, LENGTH)
    block_count = LENGTH // query_rows
    grouped = query_heads.reshape(query_heads.shape[0], HEADS, block_count, query_rows, HEAD_DIM).transpose(2, 0, 1, 3, 4)
    attended = lax.map(jax.checkpoint(attend), grouped)
    attended = attended.transpose(1, 2, 0, 3, 4).reshape(query_heads.shape)
    attended_reduced = reduced_precision(reduced_backward(merge_heads(attended)))
    residual_branch = reduced_backward(jnp.einsum('ikj,jb->ikb', attended_reduced, output_matrix, precision=highest_precision))
    attention_normed = normalize(residual_stream + residual_branch, gain_rows[0], biases[0])
    gate_up_rows = reduced_backward(jnp.einsum('nem,wmv->wnev', reduced_precision(attention_normed), gate_up_matrix, precision=highest_precision))
    hidden_rows = reduced_precision(jax.nn.silu(gate_up_rows[0]) * gate_up_rows[1])
    feedforward_output = reduced_backward(jnp.einsum('ikj,jb->ikb', hidden_rows, down_matrix, precision=highest_precision))
    return normalize(attention_normed + feedforward_output, gain_rows[1], biases[1])

def reference(hidden_in, cotangent, lengths, qkv_weight, out_weight, gate_up_weight, down_weight, norm_gain, norm_bias):
    weights = (qkv_weight.astype(jnp.float32), out_weight.astype(jnp.float32), gate_up_weight.astype(jnp.float32), down_weight.astype(jnp.float32), norm_gain.astype(jnp.float32), norm_bias.astype(jnp.float32))

    def one_batch(totals, inputs):
        x_batch, grad_batch, seq_lengths = inputs
        residual_stream = jnp.transpose(x_batch, (1, 0, 2)).astype(jnp.float32)

        def forward(x_float, query_key_value_matrix, output_matrix, gate_up_matrix, down_matrix, gain_rows, biases):
            return block_layer(x_float, query_key_value_matrix, output_matrix, gate_up_matrix, down_matrix, gain_rows, biases, seq_lengths)
        output, pullback = jax.vjp(forward, residual_stream, weights[0], weights[1], weights[2], weights[3], weights[4], weights[5])
        gradients = pullback(jnp.transpose(grad_batch, (1, 0, 2)).astype(jnp.float32))
        totals = tuple((total + gradient for total, gradient in zip(totals, gradients[1:])))
        return (totals, (jnp.transpose(output, (1, 0, 2)).astype(jnp.bfloat16), jnp.transpose(gradients[0], (1, 0, 2))))
    initial = tuple((jnp.zeros(weight.shape, jnp.float32) for weight in weights))
    totals, (outputs, input_grads) = lax.scan(one_batch, initial, (hidden_in, cotangent, lengths))
    return (outputs, input_grads, totals[0], totals[1], totals[2], totals[3], totals[4], totals[5])
```

```python
import functools

import jax
import jax.numpy as jnp
from jax import lax
from jax.experimental import pallas as pl
from jax.experimental.pallas import tpu as pltpu
from jax.sharding import PartitionSpec as P

HEAD_DIM = 64

norm_eps = 1e-12
rope_base = 1000.0
masked_score = -1e30

BF = jnp.bfloat16
F32 = jnp.float32
LANES = 128

CORE, XBIT, YBIT = 1, 2, 4
PIECE = (0, XBIT, YBIT, XBIT | YBIT)
PIECES = PIECE + tuple(j | CORE for j in PIECE)


def swap(value, dp_mask=0, mp_mask=0):
    mp = lax.axis_size("mp")
    count = lax.axis_size("dp") * mp
    mask = dp_mask * mp + mp_mask
    return lax.ppermute(value, ("dp", "mp"), [(i, i ^ mask) for i in range(count)])


def add_low(a, b):
    return (a.astype(F32) + b.astype(F32)).astype(BF)


def add_wide(a, b):
    return a.astype(F32) + b.astype(F32)


def gather_plane(own):
    half = own.shape[0] // 2
    from_x = swap(own, XBIT)
    from_y = swap(own, YBIT)
    low = swap(from_x[:half], YBIT)
    high = swap(from_y[half:], XBIT)
    mine = [own, from_x, from_y, low, high]
    return mine + [swap(piece, CORE) for piece in mine]


def gather_mp(block):
    return jnp.stack([block] + [swap(block, 0, j) for j in range(1, lax.axis_size("mp"))])


def scatter_plane(keep, send, first, second):
    back = swap(send, CORE)
    outgoing = add_low(keep[2:], back[2:])
    staying = add_low(keep[:2], back[:2])
    back = swap(outgoing, first)
    outgoing = add_low(staying[1], back[1])
    own = add_wide(staying[0], back[0])
    return own + swap(outgoing, second).astype(F32)


def order_of(first, second):
    return (0, second, first, first | second)


X_FIRST = order_of(XBIT, YBIT)
Y_FIRST = order_of(YBIT, XBIT)


def params(limit=60 << 20):
    return pltpu.CompilerParams(vmem_limit_bytes=limit)


def cost(flops, size):
    return pl.CostEstimate(flops=int(flops), bytes_accessed=int(size), transcendentals=0)


ANY = pl.BlockSpec(memory_space=pl.ANY)
VM = pl.BlockSpec(memory_space=pltpu.VMEM)


def dot(a, b):
    return lax.dot_general(a, b, (((1,), (0,)), ((), ())), preferred_element_type=F32)


def dot_t(a, b):
    return lax.dot_general(a, b, (((1,), (1,)), ((), ())), preferred_element_type=F32)


def dot_rows(a, b):
    return lax.dot_general(a, b, (((0,), (0,)), ((), ())), preferred_element_type=F32)


def piece_copies(pieces, buffer, sems, plane):
    mine = lax.axis_index("dp")
    copies = []
    for side in range(2):
        a, b, c, low, high = pieces[5 * side : 5 * side + 5]
        half = low.shape[0]
        tail = low.at[plane] if plane < half else high.at[plane - half]
        for k, source in enumerate((a.at[plane], b.at[plane], c.at[plane], tail)):
            rel = PIECE[k] | (CORE if side else 0)
            rows = source.shape[0]
            start = pl.multiple_of((mine ^ rel) * rows, rows)
            copies.append(
                pltpu.make_async_copy(
                    source, buffer.at[pl.ds(start, rows), :], sems.at[4 * side + k]
                )
            )
    return copies


def out_copies(buffer, keep, send, order, sems, rows):
    mine = lax.axis_index("dp")
    copies = []
    for i, rel in enumerate(order):
        for side, target in enumerate((keep, send)):
            start = pl.multiple_of((mine ^ rel ^ side) * rows, rows)
            copies.append(
                pltpu.make_async_copy(
                    buffer.at[pl.ds(start, rows), :], target(i), sems.at[2 * i + side]
                )
            )
    return copies


def start_all(copies):
    for copy in copies:
        copy.start()


def wait_all(copies):
    for copy in copies:
        copy.wait()


def partner(u):
    lane = lax.broadcasted_iota(jnp.int32, u.shape, 1)
    quarter = HEAD_DIM // 2
    return jnp.where(
        lane % HEAD_DIM < quarter,
        pltpu.roll(u, LANES - quarter, 1),
        pltpu.roll(u, quarter, 1),
    )


def low_lanes(shape):
    return lax.broadcasted_iota(jnp.int32, shape, 1) < HEAD_DIM


def kv_kernel(planes, x_ref, tab_ref, *refs):
    pieces, (kv_ref, w, sems) = refs[:10], refs[10:]
    copies = [piece_copies(pieces, w.at[p], sems.at[p], p) for p in range(planes)]
    for group in copies:
        start_all(group)
    x = x_ref[...]
    for p in range(planes):
        wait_all(copies[p])
        y = dot(x, w[p])
        y0, y1, y2 = y[:, :LANES], y[:, LANES : 2 * LANES], y[:, 2 * LANES :]
        base = p * 3 * LANES
        kv_ref[:, base : base + LANES] = (y0 * tab_ref[0] + partner(y0) * tab_ref[1]).astype(BF)
        kv_ref[:, base + LANES : base + 2 * LANES] = (
            y1 * tab_ref[2] + partner(y1) * tab_ref[3]
        ).astype(BF)
        kv_ref[:, base + 2 * LANES : base + 3 * LANES] = y2.astype(BF)


def q_kernel(planes, scale, x_ref, tab_ref, *refs):
    pieces, (q_ref, w, sems) = refs[:10], refs[10:]
    copies = [piece_copies(pieces, w.at[p], sems.at[p], p) for p in range(planes)]
    for group in copies:
        start_all(group)
    x = x_ref[...]
    for p in range(planes):
        wait_all(copies[p])
        y = dot(x, w[p][:, : 2 * LANES])
        y0, y1 = y[:, :LANES], y[:, LANES:]
        low = low_lanes(y1.shape)
        base = p * 2 * LANES
        q0 = y0 * tab_ref[0] + partner(y0) * tab_ref[1]
        q1 = jnp.where(low, y1 * tab_ref[2] + partner(y1) * tab_ref[3], 0.0)
        q_ref[:, base : base + LANES] = (q0 * scale).astype(BF)
        q_ref[:, base + LANES : base + 2 * LANES] = (q1 * scale).astype(BF)


def attend_kernel(q_ref, bias_ref, *refs):
    pieces = refs[:10]
    att_ref, low_ref, lse_ref, s_ref = refs[10:]
    rows = q_ref.shape[0]
    keys = rows

    def block(k, column):
        side, index = divmod(k, 4)
        lanes = slice(column * LANES, (column + 1) * LANES)
        if index < 3:
            return pieces[5 * side + index][:, lanes]
        return jnp.concatenate(
            [pieces[5 * side + 3][:, lanes], pieces[5 * side + 4][:, lanes]], axis=0
        )

    low = low_lanes((rows, LANES))
    lane = lax.broadcasted_iota(jnp.int32, (rows, LANES), 1)
    q0, q1 = q_ref[:, :LANES], q_ref[:, LANES:]
    zero = jnp.zeros_like(q0)
    heads = (
        (jnp.where(low, q0, zero), 0, 2),
        (jnp.where(low, zero, q0), 0, 2),
        (q1, 1, 1),
    )
    stats = jnp.zeros((rows, LANES), F32)
    results = []
    for h, (q, key_column, value_column) in enumerate(heads):
        peak = jnp.full((rows, LANES), -jnp.inf, F32)
        for k in range(8):
            s = dot_t(q, block(k, key_column)) + bias_ref[k : k + 1, :]
            s_ref[:, k * keys : (k + 1) * keys] = s
            for c in range(keys // LANES):
                peak = jnp.maximum(peak, s[:, c * LANES : (c + 1) * LANES])
        top = jnp.max(peak, axis=1, keepdims=True)
        total = jnp.zeros((rows, LANES), F32)
        acc = jnp.zeros((rows, LANES), F32)
        for k in range(8):
            e = jnp.exp(s_ref[:, k * keys : (k + 1) * keys] - top)
            for c in range(keys // LANES):
                total = total + e[:, c * LANES : (c + 1) * LANES]
            acc = acc + dot(e.astype(BF), block(k, value_column))
        total = jnp.sum(total, axis=1, keepdims=True)
        results.append(acc / total)
        stats = jnp.where(lane == h, top + jnp.log(total), stats)
    pair = jnp.where(low, results[0], results[1])
    single = jnp.where(low, 0.0, results[2])
    att_ref[:, :LANES] = single
    att_ref[:, LANES:] = pair
    low_ref[:, :LANES] = single.astype(BF)
    low_ref[:, LANES:] = pair.astype(BF)
    lse_ref[0] = stats.T[:8, :]


def attend_back_kernel(
    order, scale, q_ref, dat_ref, lse_ref, delta_ref, bias_ref, tab_ref, *refs
):
    pieces = refs[:10]
    keep_ref, send_ref, dq_ref = refs[10:]
    rows = q_ref.shape[0]

    def block(k, column):
        side, index = divmod(k, 4)
        lanes = slice(column * LANES, (column + 1) * LANES)
        if index < 3:
            return pieces[5 * side + index][:, lanes]
        return jnp.concatenate(
            [pieces[5 * side + 3][:, lanes], pieces[5 * side + 4][:, lanes]], axis=0
        )

    low = low_lanes((rows, LANES))
    q0, q1 = q_ref[:, :LANES], q_ref[:, LANES:]
    d0, d1 = dat_ref[:, LANES:], dat_ref[:, :LANES]
    zero = jnp.zeros_like(q0)
    heads = (
        (jnp.where(low, q0, zero), jnp.where(low, d0, zero), 0, 2),
        (jnp.where(low, zero, q0), jnp.where(low, zero, d0), 0, 2),
        (q1, d1, 1, 1),
    )
    dq = [jnp.zeros((LANES, rows), F32) for _ in heads]
    for k in range(8):
        side, index = divmod(k, 4)
        target = (keep_ref, send_ref)[side]
        slot = order.index(PIECE[index])
        mask = bias_ref[:, k : k + 1]
        blocks = [block(k, c) for c in range(3)]
        keys_t = [blocks[0].T, blocks[1].T]
        parts = []
        for h, (q, d, key_column, value_column) in enumerate(heads):
            s = dot_t(blocks[key_column], q) + mask
            dp = dot_t(blocks[value_column], d)
            p = jnp.exp(s - lse_ref[0, h : h + 1, :])
            ds = (p * (dp - delta_ref[0, h : h + 1, :])).astype(BF)
            p = p.astype(BF)
            parts.append((dot(ds, q), dot(p, d)))
            dq[h] = dq[h] + dot(keys_t[key_column], ds)
        target[slot, :, :LANES] = (parts[0][0] + parts[1][0]).astype(BF)
        target[slot, :, LANES : 2 * LANES] = (parts[2][0] + parts[2][1]).astype(BF)
        target[slot, :, 2 * LANES :] = (parts[0][1] + parts[1][1]).astype(BF)
    row = lax.broadcasted_iota(jnp.int32, (LANES, rows), 0) < HEAD_DIM
    pair = jnp.where(row, dq[0], dq[1]).T * scale
    single = jnp.where(row, dq[2], 0.0).T * scale
    dq_ref[:, :LANES] = (pair * tab_ref[0] - partner(pair) * tab_ref[1]).astype(BF)
    dq_ref[:, LANES:] = (single * tab_ref[2] - partner(single) * tab_ref[3]).astype(BF)


def center_scale(rows):
    center = rows - jnp.mean(rows, axis=-1, keepdims=True)
    inv = lax.rsqrt(jnp.mean(center * center, axis=-1, keepdims=True) + norm_eps)
    return center * inv, inv


def norm_back(e, scaled, inv):
    return inv * (
        e
        - jnp.mean(e, axis=-1, keepdims=True)
        - scaled * jnp.mean(e * scaled, axis=-1, keepdims=True)
    )


def rows_sum(value):
    return jnp.sum(value, axis=0, keepdims=True)


def forward_kernel(planes, x_ref, cot_ref, att_ref, norm_ref, *refs):
    proj, wide = refs[:10], refs[10:20]
    (
        out_ref,
        dz2_ref,
        dffn_ref,
        flow_ref,
        scaled_ref,
        inv_ref,
        sums_ref,
        gate_ref,
        up_ref,
        wo,
        wf,
        hold,
        wo_sems,
        wf_sems,
        hold_sems,
    ) = refs[20:]
    wo_copies = [piece_copies(proj, wo.at[p], wo_sems.at[p], p) for p in range(planes)]
    wf_copies = [piece_copies(wide, wf.at[p], wf_sems.at[p], p) for p in range(planes)]
    for group in wo_copies + wf_copies:
        start_all(group)
    branch = jnp.zeros(x_ref.shape, F32)
    for p in range(planes):
        wait_all(wo_copies[p])
        branch = branch + dot_t(
            att_ref[:, p * 2 * LANES : (p + 1) * 2 * LANES], wo[p][:, LANES : 3 * LANES]
        )
    gain, bias = norm_ref[0:2, :], norm_ref[2:4, :]
    scaled, inv = center_scale(x_ref[...].astype(F32) + branch)
    scaled_ref[...] = scaled
    inv_ref[...] = jnp.broadcast_to(inv, inv_ref.shape)
    first = scaled * gain[0:1] + bias[0:1]
    flow = first.astype(BF)
    flow_ref[...] = flow
    ffn = jnp.zeros(x_ref.shape, F32)
    width = wf.shape[2] // 3
    saves = []
    for p in range(planes):
        wait_all(wf_copies[p])
        gate = dot(flow, wf[p][:, :width])
        up = dot(flow, wf[p][:, width : 2 * width])
        hold[p, 0] = gate
        hold[p, 1] = up
        for k, target in enumerate((gate_ref, up_ref)):
            copy = pltpu.make_async_copy(hold.at[p, k], target.at[p], hold_sems.at[p, k])
            copy.start()
            saves.append(copy)
        hidden = (gate * jax.nn.sigmoid(gate) * up).astype(BF)
        ffn = ffn + dot_t(hidden, wf[p][:, 2 * width :])
    scaled, inv = center_scale(first + ffn)
    out_ref[...] = (scaled * gain[1:2] + bias[1:2]).astype(BF)
    cot = cot_ref[...].astype(F32)
    dz2 = norm_back(cot * gain[1:2], scaled, inv)
    dz2_ref[...] = dz2
    dffn_ref[...] = dz2.astype(BF)
    sums_ref[...] = jnp.concatenate(
        [rows_sum(cot * scaled), rows_sum(cot), jnp.zeros((6, cot.shape[1]), F32)], axis=0
    )
    wait_all(saves)


def ffn_back_kernel(plane, order, rows, acc_ref, flow_ref, dffn_ref, gate_ref, up_ref, *refs):
    wide = refs[:10]
    dfirst_ref, keep_ref, send_ref, wf, grads, wf_sems, out_sems = refs[10:]
    copies = piece_copies(wide, wf, wf_sems, plane)
    start_all(copies)
    gate, up = gate_ref[0], up_ref[0]
    sig = jax.nn.sigmoid(gate)
    silu = gate * sig
    hidden = (silu * up).astype(BF)
    width = gate.shape[1]
    flow_t = flow_ref[...].T
    dffn = dffn_ref[...]
    grads[2] = dot(dffn.T, hidden).astype(BF)
    outs = []

    def emit(k):
        lanes = slice(k * width, (k + 1) * width)
        group = out_copies(
            grads.at[k],
            lambda i: keep_ref.at[i, :, lanes],
            lambda i: send_ref.at[i, :, lanes],
            order,
            out_sems.at[k],
            rows,
        )
        start_all(group)
        outs.extend(group)

    emit(2)
    wait_all(copies)
    d_hidden = dot(dffn, wf[:, 2 * width :])
    d_up = (d_hidden * silu).astype(BF)
    d_gate = (d_hidden * up * sig * (1.0 + gate * (1.0 - sig))).astype(BF)
    grads[0] = dot(flow_t, d_gate).astype(BF)
    emit(0)
    grads[1] = dot(flow_t, d_up).astype(BF)
    emit(1)
    dfirst_ref[...] = (
        acc_ref[...] + dot_t(d_gate, wf[:, :width]) + dot_t(d_up, wf[:, width : 2 * width])
    )
    wait_all(outs)


def branch_back_kernel(
    planes, rows, dfirst_ref, scaled_ref, inv_ref, norm_ref, att_ref, att_low_ref, *refs
):
    proj = refs[:10]
    (
        dz1_ref,
        dat_ref,
        delta_ref,
        sums_ref,
        keep_x,
        send_x,
        keep_y,
        send_y,
        wo,
        grads,
        wo_sems,
        out_sems,
    ) = refs[10:]
    copies = [piece_copies(proj, wo.at[p], wo_sems.at[p], p) for p in range(planes)]
    for group in copies:
        start_all(group)
    dfirst = dfirst_ref[...]
    scaled = scaled_ref[...]
    sums_ref[...] = jnp.concatenate(
        [rows_sum(dfirst * scaled), rows_sum(dfirst), jnp.zeros((6, dfirst.shape[1]), F32)], axis=0
    )
    dz1 = norm_back(dfirst * norm_ref[0:1, :], scaled, inv_ref[:, 0:1])
    dz1_ref[...] = dz1
    d_branch = dz1.astype(BF)
    branch_t = d_branch.T
    outs = []
    half = planes // 2
    low = low_lanes((dfirst.shape[0], LANES))
    lane = lax.broadcasted_iota(jnp.int32, (dfirst.shape[0], LANES), 1)
    for p in range(planes):
        lanes = slice(p * 2 * LANES, (p + 1) * 2 * LANES)
        grads[p] = dot(branch_t, att_low_ref[:, lanes]).astype(BF)
        keep, send, order = (keep_x, send_x, X_FIRST) if p < half else (keep_y, send_y, Y_FIRST)
        group = out_copies(
            grads.at[p],
            lambda i: keep.at[i, p % half],
            lambda i: send.at[i, p % half],
            order,
            out_sems.at[p],
            rows,
        )
        start_all(group)
        outs.extend(group)
        wait_all(copies[p])
        d = dot(d_branch, wo[p][:, LANES : 3 * LANES])
        single = jnp.where(low, 0.0, d[:, :LANES]).astype(BF)
        pair = d[:, LANES:].astype(BF)
        dat_ref[:, p * 2 * LANES : p * 2 * LANES + LANES] = single
        dat_ref[:, p * 2 * LANES + LANES : (p + 1) * 2 * LANES] = pair
        both = pair.astype(F32) * att_ref[:, p * 2 * LANES + LANES : (p + 1) * 2 * LANES]
        alone = single.astype(F32) * att_ref[:, p * 2 * LANES : p * 2 * LANES + LANES]
        zero = jnp.zeros_like(both)
        stats = zero
        for h, part in enumerate((jnp.where(low, both, zero), jnp.where(low, zero, both), alone)):
            stats = jnp.where(lane == h, jnp.sum(part, axis=1, keepdims=True), stats)
        delta_ref[p] = stats.T[:8, :]
    wait_all(outs)


def project_back_kernel(planes, columns, used, rows, mode, x_ref, d_ref, acc_ref, tab_ref, *refs):
    pieces = refs[:10]
    din_ref, keep_x, send_x, keep_y, send_y, w, grads, w_sems, out_sems = refs[10:]
    copies = [piece_copies(pieces, w.at[p], w_sems.at[p], p) for p in range(planes)]
    for group in copies:
        start_all(group)
    x_t = x_ref[...].T
    total = acc_ref[...]
    outs = []
    half = planes // 2
    for p in range(planes):
        base = p * used
        if mode:
            d0 = d_ref[:, base : base + LANES].astype(F32)
            d1 = d_ref[:, base + LANES : base + 2 * LANES].astype(F32)
            d2 = d_ref[:, base + 2 * LANES : base + 3 * LANES].astype(F32)
            d = jnp.concatenate(
                [
                    (d0 * tab_ref[0] - partner(d0) * tab_ref[1]).astype(BF),
                    (d1 * tab_ref[2] - partner(d1) * tab_ref[3]).astype(BF),
                    d2.astype(BF),
                ],
                axis=1,
            )
        else:
            d = d_ref[:, base : base + used]
        grads[p] = dot(x_t, d).astype(BF)
        keep, send, order = (keep_x, send_x, X_FIRST) if p < half else (keep_y, send_y, Y_FIRST)
        group = out_copies(
            grads.at[p],
            lambda i: keep.at[i, p % half],
            lambda i: send.at[i, p % half],
            order,
            out_sems.at[p],
            rows,
        )
        start_all(group)
        outs.extend(group)
        wait_all(copies[p])
        total = total + dot_t(d, w[p][:, :used])
    din_ref[...] = total.astype(din_ref.dtype)
    wait_all(outs)


def sds(shape, dtype):
    return jax.ShapeDtypeStruct(shape, dtype)


def plane_body(
    hidden_in,
    cotangent,
    lengths,
    qkv_weight,
    out_weight,
    gate_up_weight,
    down_weight,
    norm_gain,
    norm_bias,
):
    planes = lax.axis_size("mp")
    group = lax.axis_size("dp")
    dp, mp = lax.axis_index("dp"), lax.axis_index("mp")
    part = hidden_in.shape[1]
    width = hidden_in.shape[3]
    rows = part * planes
    slab = qkv_weight.shape[1]
    ff = gate_up_weight.shape[2]
    scale = HEAD_DIM ** (-0.5)
    mine = mp ^ jnp.arange(planes, dtype=jnp.int32)

    def exchange_in(array):
        array = array.reshape(array.shape[0], part, width)
        blocks = [lax.dynamic_index_in_dim(array, mine[j], 0, keepdims=False) for j in range(planes)]
        return [blocks[0]] + [swap(blocks[j], 0, j) for j in range(1, planes)]

    def exchange_out(blocks):
        got = jnp.stack([blocks[0]] + [swap(blocks[j], 0, j) for j in range(1, planes)])
        return jnp.stack(
            [lax.dynamic_index_in_dim(got, mine[m], 0, keepdims=False) for m in range(planes)]
        )

    q_w, k_w, v_w = qkv_weight[0], qkv_weight[1], qkv_weight[2]
    o_w = out_weight.T
    two = 2 * HEAD_DIM
    kv_own = jnp.concatenate([k_w[:, :two], k_w[:, two:], v_w[:, two:], v_w[:, :two]], axis=1)
    qo_own = jnp.concatenate([q_w[:, :two], q_w[:, two:], o_w[:, two:], o_w[:, :two]], axis=1)
    ffn_own = jnp.concatenate([gate_up_weight[0], gate_up_weight[1], down_weight.T], axis=1)

    x_parts = exchange_in(hidden_in)
    kv_w = gather_plane(gather_mp(kv_own))
    x = jnp.concatenate(x_parts, axis=0)
    qo_w = gather_plane(gather_mp(qo_own))
    ffn_w = gather_plane(gather_mp(ffn_own))
    cot = jnp.concatenate(exchange_in(cotangent), axis=0)

    norm_own = jnp.concatenate([norm_gain, norm_bias, jnp.zeros((4, slab), BF)], axis=0)
    norms = lax.dynamic_update_slice(
        jnp.zeros((8, width), F32), norm_own.astype(F32), (0, dp * slab)
    )
    for mask in (CORE, XBIT, YBIT):
        norms = norms + swap(norms, mask)

    within = (mine[:, None] * part + jnp.arange(part, dtype=jnp.int32)[None, :]).reshape(rows)
    positions = (dp * rows + within).astype(F32)
    half = HEAD_DIM // 2
    exponent = jnp.arange(half, dtype=F32) * (1.0 / half)
    angles = positions[:, None] * jnp.power(rope_base, -exponent)[None, :]
    cosine, sine = jnp.cos(angles), jnp.sin(angles)
    cos_head = jnp.concatenate([cosine, cosine], axis=1)
    sin_head = jnp.concatenate([-sine, sine], axis=1)
    one, none = jnp.ones_like(cos_head), jnp.zeros_like(cos_head)
    cat = lambda a, b: jnp.concatenate([a, b], axis=1)
    tables = jnp.stack(
        [cat(cos_head, cos_head), cat(sin_head, sin_head), cat(cos_head, one), cat(sin_head, none)]
    )
    length = lax.dynamic_index_in_dim(lengths.reshape(-1), mp, 0, keepdims=False)
    piece_base = (dp ^ jnp.array(PIECES, dtype=jnp.int32)) * rows
    key_pos = piece_base[:, None] + within[None, :]
    bias = jnp.where(key_pos < length, 0.0, masked_score).astype(F32)
    bias_t = bias.T

    w_size = planes * group * slab * 3 * LANES * 2
    dma = pltpu.SemaphoreType.DMA
    kv = pl.pallas_call(
        functools.partial(kv_kernel, planes),
        out_shape=sds((rows, planes * 3 * LANES), BF),
        in_specs=[VM, VM] + [ANY] * 10,
        out_specs=VM,
        scratch_shapes=[pltpu.VMEM((planes, width, 3 * LANES), BF), dma((planes, 8))],
        compiler_params=params(),
        cost_estimate=cost(2 * rows * width * planes * 3 * LANES, w_size),
        name="kv_project",
    )(x, tables, *kv_w)

    split = rows // 2
    kv_x, kv_y = swap(kv, XBIT), swap(kv, YBIT)
    kv_low, kv_high = swap(kv_x[:split], YBIT), swap(kv_y[split:], XBIT)
    kv_mine = [kv, kv_x, kv_y, kv_low, kv_high]
    kv_all = kv_mine + [swap(piece, CORE) for piece in kv_mine]

    q = pl.pallas_call(
        functools.partial(q_kernel, planes, scale),
        out_shape=sds((rows, planes * 2 * LANES), BF),
        in_specs=[VM, VM] + [ANY] * 10,
        out_specs=VM,
        scratch_shapes=[pltpu.VMEM((planes, width, 3 * LANES), BF), dma((planes, 8))],
        compiler_params=params(),
        cost_estimate=cost(2 * rows * width * planes * 2 * LANES, w_size),
        name="q_project",
    )(x, tables, *qo_w)

    def kv_specs(base):
        full = pl.BlockSpec((rows, 3 * LANES), lambda i: (0, i + base))
        part_spec = pl.BlockSpec((split, 3 * LANES), lambda i: (0, i + base))
        return [full, full, full, part_spec, part_spec] * 2

    seq = rows * group
    heads = planes * 3
    att, att_low, lse = pl.pallas_call(
        attend_kernel,
        grid=(planes,),
        out_shape=(
            sds((rows, planes * 2 * LANES), F32),
            sds((rows, planes * 2 * LANES), BF),
            sds((planes, 8, rows), F32),
        ),
        in_specs=[
            pl.BlockSpec((rows, 2 * LANES), lambda i: (0, i)),
            pl.BlockSpec((8, rows), lambda i: (0, 0)),
        ]
        + kv_specs(0),
        out_specs=(
            pl.BlockSpec((rows, 2 * LANES), lambda i: (0, i)),
            pl.BlockSpec((rows, 2 * LANES), lambda i: (0, i)),
            pl.BlockSpec((1, 8, rows), lambda i: (i, 0, 0)),
        ),
        scratch_shapes=[pltpu.VMEM((rows, seq), F32)],
        compiler_params=params(),
        cost_estimate=cost(16 * rows * seq * LANES * heads, seq * 3 * LANES * planes * 2),
        name="attend",
    )(q, bias, *kv_all)

    ffn_size = planes * group * slab * 3 * ff * 2
    layer_out, dz2, dffn, flow, scaled, inv, sums_two, gate, up = pl.pallas_call(
        functools.partial(forward_kernel, planes),
        out_shape=(
            sds((rows, width), BF),
            sds((rows, width), F32),
            sds((rows, width), BF),
            sds((rows, width), BF),
            sds((rows, width), F32),
            sds((rows, LANES), F32),
            sds((8, width), F32),
            sds((planes, rows, ff), F32),
            sds((planes, rows, ff), F32),
        ),
        in_specs=[VM] * 4 + [ANY] * 20,
        out_specs=(VM,) * 7 + (ANY, ANY),
        scratch_shapes=[
            pltpu.VMEM((planes, width, 3 * LANES), BF),
            pltpu.VMEM((planes, width, 3 * ff), BF),
            pltpu.VMEM((planes, 2, rows, ff), F32),
            dma((planes, 8)),
            dma((planes, 8)),
            dma((planes, 2)),
        ],
        compiler_params=params(),
        cost_estimate=cost(6 * rows * width * planes * ff, ffn_size),
        name="forward",
    )(x, cot, att_low, norms, *qo_w, *ffn_w)

    dfirst = dz2
    ffn_sums = {}
    for p in reversed(range(planes)):
        order = X_FIRST if p % 2 else Y_FIRST
        gate_spec = pl.BlockSpec((1, rows, ff), functools.partial(lambda p, i: (p, 0, 0), p))
        whole = pl.BlockSpec((rows, width), lambda i: (0, 0))
        dfirst, keep, send = pl.pallas_call(
            functools.partial(ffn_back_kernel, p, order, slab),
            grid=(1,),
            out_shape=(
                sds((rows, width), F32),
                sds((4, slab, 3 * ff), BF),
                sds((4, slab, 3 * ff), BF),
            ),
            in_specs=[whole, whole, whole, gate_spec, gate_spec] + [ANY] * 10,
            out_specs=(whole, ANY, ANY),
            scratch_shapes=[
                pltpu.VMEM((width, 3 * ff), BF),
                pltpu.VMEM((3, width, ff), BF),
                dma((8,)),
                dma((3, 8)),
            ],
            compiler_params=params(),
            cost_estimate=cost(12 * rows * width * ff, 2 * ffn_size // planes),
            name="ffn_back",
        )(dfirst, flow, dffn, gate, up, *ffn_w)
        first, second = (XBIT, YBIT) if p % 2 else (YBIT, XBIT)
        ffn_sums[p] = scatter_plane(keep, send, first, second)
        if p:
            ffn_sums[p] = swap(ffn_sums[p].astype(BF), 0, p).astype(F32)
    ffn_grad = sum(ffn_sums[p] for p in range(planes))

    pair = planes // 2
    grad_shape = lambda columns: sds((4, pair, slab, columns), BF)
    dz1, dat, delta, sums_one, keep_x, send_x, keep_y, send_y = pl.pallas_call(
        functools.partial(branch_back_kernel, planes, slab),
        out_shape=(
            sds((rows, width), F32),
            sds((rows, planes * 2 * LANES), BF),
            sds((planes, 8, rows), F32),
            sds((8, width), F32),
        )
        + (grad_shape(2 * LANES),) * 4,
        in_specs=[VM] * 6 + [ANY] * 10,
        out_specs=(VM,) * 4 + (ANY,) * 4,
        scratch_shapes=[
            pltpu.VMEM((planes, width, 3 * LANES), BF),
            pltpu.VMEM((planes, width, 2 * LANES), BF),
            dma((planes, 8)),
            dma((planes, 8)),
        ],
        compiler_params=params(),
        cost_estimate=cost(4 * rows * width * planes * 2 * LANES, 2 * w_size),
        name="branch_back",
    )(dfirst, scaled, inv, norms, att, att_low, *qo_w)

    def scatter_all(keep_x, send_x, keep_y, send_y):
        sum_x = scatter_plane(keep_x, send_x, XBIT, YBIT)
        sum_y = scatter_plane(keep_y, send_y, YBIT, XBIT)
        blocks = [sum_x[k] for k in range(pair)] + [sum_y[k] for k in range(pair)]
        total = blocks[0]
        for j in range(1, planes):
            total = total + swap(blocks[j].astype(BF), 0, j).astype(F32)
        return total

    o_grad = scatter_all(keep_x, send_x, keep_y, send_y)

    sums = jnp.concatenate([sums_one[0:1], sums_two[0:1], sums_one[1:2], sums_two[1:2]], axis=0)
    sums = jnp.concatenate([sums, jnp.zeros((4, width), F32)], axis=0)
    for mask in (CORE, XBIT, YBIT):
        sums = sums + swap(sums, mask)
    for mask in range(planes.bit_length() - 1):
        sums = sums + swap(sums, 0, 1 << mask)
    sums = lax.dynamic_slice_in_dim(sums, dp * slab, slab, 1)

    dq_parts, dkv_parts = [], []
    for call in range(2):
        first, second = ((XBIT, YBIT), (YBIT, XBIT))[call]
        order = order_of(first, second)
        base = call * pair
        at = functools.partial(lambda base, i: (0, i + base), base)
        stat = pl.BlockSpec((1, 8, rows), functools.partial(lambda base, i: (i + base, 0, 0), base))
        keep, send, dq = pl.pallas_call(
            functools.partial(attend_back_kernel, order, scale),
            grid=(pair,),
            out_shape=(
                sds((4, rows, pair * 3 * LANES), BF),
                sds((4, rows, pair * 3 * LANES), BF),
                sds((rows, pair * 2 * LANES), BF),
            ),
            in_specs=[
                pl.BlockSpec((rows, 2 * LANES), at),
                pl.BlockSpec((rows, 2 * LANES), at),
                stat,
                stat,
                pl.BlockSpec((rows, 8), lambda i: (0, 0)),
                pl.BlockSpec((4, rows, LANES), lambda i: (0, 0, 0)),
            ]
            + kv_specs(base),
            out_specs=(
                pl.BlockSpec((4, rows, 3 * LANES), lambda i: (0, 0, i)),
                pl.BlockSpec((4, rows, 3 * LANES), lambda i: (0, 0, i)),
                pl.BlockSpec((rows, 2 * LANES), lambda i: (0, i)),
            ),
            compiler_params=params(),
            cost_estimate=cost(
                40 * rows * seq * LANES * heads // 2, seq * 3 * LANES * planes * 2
            ),
            name="attend_back",
        )(q, dat, lse, delta, bias_t, tables, *kv_all)
        dkv_parts.append(scatter_plane(keep, send, first, second))
        dq_parts.append(dq)
    dq = jnp.concatenate(dq_parts, axis=1)
    dkv = jnp.concatenate(dkv_parts, axis=1)

    def project_back(d, acc, pieces, used, mode, out_type):
        columns = 3 * LANES
        return pl.pallas_call(
            functools.partial(project_back_kernel, planes, columns, used, slab, mode),
            out_shape=(sds((rows, width), out_type),) + (grad_shape(used),) * 4,
            in_specs=[VM] * 4 + [ANY] * 10,
            out_specs=(VM,) + (ANY,) * 4,
            scratch_shapes=[
                pltpu.VMEM((planes, width, columns), BF),
                pltpu.VMEM((planes, width, used), BF),
                dma((planes, 8)),
                dma((planes, 8)),
            ],
            compiler_params=params(),
            cost_estimate=cost(4 * rows * width * planes * used, 2 * w_size),
            name="project_back",
        )(x, d, acc, tables, *pieces)

    din, *q_parts = project_back(dq, dz1, qo_w, 2 * LANES, False, F32)
    q_grad = scatter_all(*q_parts)
    din, *kv_parts = project_back(dkv, din, kv_w, 3 * LANES, True, BF)
    input_grad = exchange_out([din[j * part : (j + 1) * part] for j in range(planes)])
    kv_grad = scatter_all(*kv_parts)

    layer_rows = exchange_out([layer_out[j * part : (j + 1) * part] for j in range(planes)])
    shape = hidden_in.shape
    qkv_grad = jnp.stack(
        [
            q_grad[:, : 3 * HEAD_DIM],
            kv_grad[:, : 3 * HEAD_DIM],
            jnp.concatenate([kv_grad[:, 2 * LANES :], kv_grad[:, 3 * HEAD_DIM : 2 * LANES]], axis=1),
        ]
    )
    out_grad = jnp.concatenate([o_grad[:, LANES:], o_grad[:, HEAD_DIM:LANES]], axis=1).T
    return (
        layer_rows.reshape(shape),
        input_grad.reshape(shape).astype(F32),
        qkv_grad,
        out_grad,
        jnp.stack([ffn_grad[:, :ff], ffn_grad[:, ff : 2 * ff]]),
        ffn_grad[:, 2 * ff :].T,
        sums[0:2],
        sums[2:4],
    )


def rope_tables(positions, half_dim):
    exponent = jnp.arange(half_dim, dtype=jnp.float32) * (1.0 / half_dim)
    inverse = jnp.power(rope_base, -exponent)
    angles = positions[:, None] * inverse[None, :]
    return (jnp.cos(angles), jnp.sin(angles))


def rotate(vectors, cosine, sine_table):
    half_dim = vectors.shape[-1] // 2
    first_half = vectors[..., :half_dim]
    second_half = vectors[..., half_dim:]
    return jnp.concatenate(
        [
            first_half * cosine - second_half * sine_table,
            second_half * cosine + first_half * sine_table,
        ],
        axis=-1,
    )


def rotate_back(gradient, cosine, sine_table):
    half_dim = gradient.shape[-1] // 2
    first_half = gradient[..., :half_dim]
    second_half = gradient[..., half_dim:]
    return jnp.concatenate(
        [
            first_half * cosine + second_half * sine_table,
            second_half * cosine - first_half * sine_table,
        ],
        axis=-1,
    )


def normalize(residual_stream, gain_row, bias_row):
    center = residual_stream - jnp.mean(residual_stream, axis=-1, keepdims=True)
    inv_std = lax.rsqrt(jnp.mean(center * center, axis=-1, keepdims=True) + norm_eps)
    scaled = center * inv_std
    return (scaled * gain_row + bias_row, scaled, inv_std)


def normalize_back(upstream, scaled, inv_std, gain_row):
    d_scaled = upstream * gain_row
    d_stream = inv_std * (
        d_scaled
        - jnp.mean(d_scaled, axis=-1, keepdims=True)
        - scaled * jnp.mean(d_scaled * scaled, axis=-1, keepdims=True)
    )
    return (d_stream, jnp.sum(upstream * scaled, axis=(0, 1)), jnp.sum(upstream, axis=(0, 1)))


def split_heads(rows, head_dim):
    return rows.reshape(
        rows.shape[0], rows.shape[1], rows.shape[2] // head_dim, head_dim
    ).transpose(1, 2, 0, 3)


def merge_heads(heads):
    return heads.transpose(2, 0, 1, 3).reshape(
        heads.shape[2], heads.shape[0], heads.shape[1] * heads.shape[3]
    )


def score_grads(
    query_part, grad_part, lse_part, delta_part, key_part, value_part, mask_part, score_scale
):
    scores = (
        jnp.einsum("shqd,shkd->shqk", query_part, key_part, preferred_element_type=jnp.float32)
        * score_scale
    )
    prob_full = jnp.where(mask_part, jnp.exp(scores - lse_part[..., None]), 0.0)
    d_probs = jnp.einsum(
        "shqd,shkd->shqk", grad_part, value_part, preferred_element_type=jnp.float32
    )
    d_scores = (prob_full * (d_probs - delta_part[..., None]) * score_scale).astype(jnp.bfloat16)
    return (d_scores, prob_full.astype(jnp.bfloat16))


def body(
    hidden_in,
    cotangent,
    lengths,
    qkv_weight,
    out_weight,
    gate_up_weight,
    down_weight,
    norm_gain,
    norm_bias,
):
    query_key_value_matrix, output_matrix, gate_up_matrix, down_matrix, gain_rows, bias_rows = (
        lax.all_gather(qkv_weight, "dp", axis=1, tiled=True),
        lax.all_gather(out_weight, "dp", axis=1, tiled=True),
        lax.all_gather(gate_up_weight, "dp", axis=1, tiled=True),
        lax.all_gather(down_weight, "dp", axis=1, tiled=True),
        lax.all_gather(norm_gain, "dp", axis=1, tiled=True),
        lax.all_gather(norm_bias, "dp", axis=1, tiled=True),
    )
    gain_rows = gain_rows.astype(jnp.float32)
    bias_rows = bias_rows.astype(jnp.float32)
    group_size = lax.axis_size("dp")
    group_rank = lax.axis_index("dp")
    model_rank = lax.axis_index("mp")
    local_rows = hidden_in.shape[1]
    slots = local_rows * lax.axis_size("mp")
    seq_total = slots * group_size
    head_dim = HEAD_DIM
    score_scale = head_dim ** (-0.5)
    span = min(group_size, 8)
    block_keys = slots * span
    key_blocks = group_size // span
    own_first = group_rank * slots
    positions = (own_first + jnp.arange(slots, dtype=jnp.int32)).astype(jnp.float32)
    cosine, sine_table = rope_tables(positions, head_dim // 2)
    acc_qkv = jnp.zeros(query_key_value_matrix.shape, jnp.float32)
    acc_out = jnp.zeros(output_matrix.shape, jnp.float32)
    acc_gate_up = jnp.zeros(gate_up_matrix.shape, jnp.float32)
    acc_down = jnp.zeros(down_matrix.shape, jnp.float32)
    acc_gain = jnp.zeros(gain_rows.shape, jnp.float32)
    acc_bias = jnp.zeros(bias_rows.shape, jnp.float32)
    layer_rows = []
    input_rows = []
    for micro_step in range(hidden_in.shape[0]):
        x_rows, grad_rows = (
            lax.all_gather(hidden_in[micro_step], "mp", axis=0, tiled=True),
            lax.all_gather(cotangent[micro_step], "mp", axis=0, tiled=True),
        )
        seq_lengths = lengths[micro_step]

        def allowed_keys(first_row, row_count):
            key_pos = first_row + jnp.arange(row_count, dtype=jnp.int32)
            return (key_pos[None, :] < seq_lengths[:, None])[:, None, None, :]

        projected_rows = jnp.einsum(
            "rsd,cde->rsce", x_rows, query_key_value_matrix, preferred_element_type=jnp.float32
        )
        q_heads = rotate(split_heads(projected_rows[:, :, 0], head_dim), cosine, sine_table).astype(
            jnp.bfloat16
        )
        k_heads = rotate(split_heads(projected_rows[:, :, 1], head_dim), cosine, sine_table).astype(
            jnp.bfloat16
        )
        v_heads = split_heads(projected_rows[:, :, 2], head_dim).astype(jnp.bfloat16)
        head_shape = q_heads.shape
        buffer_shape = (head_shape[0], head_shape[1], seq_total, head_shape[3])
        forward_first_row = jnp.int32(0)
        run_max = jnp.full(head_shape[:3], masked_score, jnp.float32)
        key_part = lax.all_gather(k_heads, "dp", axis=2, tiled=True)
        value_part = lax.all_gather(v_heads, "dp", axis=2, tiled=True)
        forward_row_count = key_part.shape[2]
        forward_key_buffer = key_part
        forward_value_buffer = value_part
        old_max = run_max
        allowed = allowed_keys(forward_first_row, forward_row_count)
        scores = (
            jnp.einsum("shqd,shkd->shqk", q_heads, key_part, preferred_element_type=jnp.float32)
            * score_scale
        )
        scores = jnp.where(allowed, scores, masked_score)
        new_max = jnp.maximum(old_max, jnp.max(scores, axis=-1))
        weights_block = jnp.where(allowed, jnp.exp(scores - new_max[..., None]), 0.0)
        new_sum = jnp.sum(weights_block, axis=-1)
        new_acc = jnp.einsum(
            "shqk,shkd->shqd",
            weights_block.astype(jnp.bfloat16),
            value_part,
            preferred_element_type=jnp.float32,
        )
        run_max = new_max
        key_buffer = forward_key_buffer
        value_buffer = forward_value_buffer
        lse = run_max + jnp.log(new_sum)
        attended = new_acc / new_sum[..., None]
        attended_reduced = merge_heads(attended).astype(jnp.bfloat16)
        residual_branch = lax.psum(
            jnp.einsum(
                "rsf,fd->rsd", attended_reduced, output_matrix, preferred_element_type=jnp.float32
            ).astype(jnp.bfloat16),
            "mp",
        ).astype(jnp.float32)
        attention_normed, scaled_one, inv_std_one = normalize(
            x_rows.astype(jnp.float32) + residual_branch, gain_rows[0], bias_rows[0]
        )
        first_low = attention_normed.astype(jnp.bfloat16)
        gate_up_rows = jnp.einsum(
            "rsd,cdf->rscf", first_low, gate_up_matrix, preferred_element_type=jnp.float32
        )
        gate_part = gate_up_rows[:, :, 0]
        up_part = gate_up_rows[:, :, 1]
        sigmoid_gate = jax.nn.sigmoid(gate_part)
        silu_gate = gate_part * sigmoid_gate
        hidden_rows = (silu_gate * up_part).astype(jnp.bfloat16)
        feedforward_output = lax.psum(
            jnp.einsum(
                "rsf,fd->rsd", hidden_rows, down_matrix, preferred_element_type=jnp.float32
            ).astype(jnp.bfloat16),
            "mp",
        ).astype(jnp.float32)
        output, scaled_two, inv_std_two = normalize(
            attention_normed + feedforward_output, gain_rows[1], bias_rows[1]
        )
        layer_rows.append(
            lax.dynamic_slice_in_dim(output, model_rank * local_rows, local_rows, 0).astype(
                jnp.bfloat16
            )
        )
        d_z2, gain_two, bias_two = normalize_back(
            grad_rows.astype(jnp.float32), scaled_two, inv_std_two, gain_rows[1]
        )
        d_ffn = d_z2.astype(jnp.bfloat16)
        acc_down = acc_down + jnp.einsum(
            "rsf,rsd->fd", hidden_rows, d_ffn, preferred_element_type=jnp.float32
        )
        d_hidden = jnp.einsum("rsd,fd->rsf", d_ffn, down_matrix, preferred_element_type=jnp.float32)
        d_gate = d_hidden * up_part * sigmoid_gate * (1.0 + gate_part * (1.0 - sigmoid_gate))
        d_up = d_hidden * silu_gate
        d_gate_up = jnp.stack([d_gate, d_up], axis=2).astype(jnp.bfloat16)
        acc_gate_up = acc_gate_up + jnp.einsum(
            "rsd,rscf->cdf", first_low, d_gate_up, preferred_element_type=jnp.float32
        )
        d_first = (
            lax.psum(
                jnp.einsum(
                    "rscf,cdf->rsd", d_gate_up, gate_up_matrix, preferred_element_type=jnp.float32
                ).astype(jnp.bfloat16),
                "mp",
            ).astype(jnp.float32)
            + d_z2
        )
        d_z1, gain_one, bias_one = normalize_back(d_first, scaled_one, inv_std_one, gain_rows[0])
        acc_gain = acc_gain + jnp.stack([gain_one, gain_two])
        acc_bias = acc_bias + jnp.stack([bias_one, bias_two])
        d_branch = d_z1.astype(jnp.bfloat16)
        acc_out = acc_out + jnp.einsum(
            "rsf,rsd->fd", attended_reduced, d_branch, preferred_element_type=jnp.float32
        )
        d_attended = split_heads(
            jnp.einsum("rsd,fd->rsf", d_branch, output_matrix, preferred_element_type=jnp.float32),
            head_dim,
        ).astype(jnp.bfloat16)
        delta = jnp.sum(d_attended.astype(jnp.float32) * attended, axis=-1)
        zero_heads = jnp.zeros(head_shape, jnp.float32)

        def query_block(step_index, partial_sums):
            first_row = step_index * block_keys
            key_part = lax.dynamic_slice_in_dim(key_buffer, first_row, block_keys, 2)
            value_part = lax.dynamic_slice_in_dim(value_buffer, first_row, block_keys, 2)
            d_scores, prob_block = score_grads(
                q_heads,
                d_attended,
                lse,
                delta,
                key_part,
                value_part,
                allowed_keys(first_row, block_keys),
                score_scale,
            )
            d_query = partial_sums[0] + jnp.einsum(
                "shqk,shkd->shqd", d_scores, key_part, preferred_element_type=jnp.float32
            )
            key_total = lax.dynamic_update_slice_in_dim(
                partial_sums[1],
                jnp.einsum(
                    "shqk,shqd->shkd", d_scores, q_heads, preferred_element_type=jnp.float32
                ),
                first_row,
                2,
            )
            value_total = lax.dynamic_update_slice_in_dim(
                partial_sums[2],
                jnp.einsum(
                    "shqk,shqd->shkd", prob_block, d_attended, preferred_element_type=jnp.float32
                ),
                first_row,
                2,
            )
            return (d_query, key_total, value_total)

        zero_keys = jnp.zeros(buffer_shape, jnp.float32)
        d_query, key_total, value_total = lax.fori_loop(
            0, key_blocks, query_block, (zero_heads, zero_keys, zero_keys)
        )
        d_key, d_value = (
            lax.psum_scatter(key_total, "dp", scatter_dimension=2, tiled=True),
            lax.psum_scatter(value_total, "dp", scatter_dimension=2, tiled=True),
        )
        d_projected = jnp.stack(
            [
                merge_heads(rotate_back(d_query, cosine, sine_table)),
                merge_heads(rotate_back(d_key, cosine, sine_table)),
                merge_heads(d_value),
            ],
            axis=2,
        ).astype(jnp.bfloat16)
        acc_qkv = acc_qkv + jnp.einsum(
            "rsd,rsce->cde", x_rows, d_projected, preferred_element_type=jnp.float32
        )
        d_input = lax.psum_scatter(
            jnp.einsum(
                "rsce,cde->rsd",
                d_projected,
                query_key_value_matrix,
                preferred_element_type=jnp.float32,
            ).astype(jnp.bfloat16),
            "mp",
            scatter_dimension=0,
            tiled=True,
        ).astype(jnp.float32)
        input_rows.append(
            d_input + lax.dynamic_slice_in_dim(d_z1, model_rank * local_rows, local_rows, 0)
        )
    qkv_grad, out_grad, gate_up_grad, down_grad, gain_grad, bias_grad = (
        lax.psum_scatter(acc_qkv, "dp", scatter_dimension=1, tiled=True),
        lax.psum_scatter(acc_out, "dp", scatter_dimension=1, tiled=True),
        lax.psum_scatter(acc_gate_up, "dp", scatter_dimension=1, tiled=True),
        lax.psum_scatter(acc_down, "dp", scatter_dimension=1, tiled=True),
        lax.psum_scatter(acc_gain, "dp", scatter_dimension=1, tiled=True),
        lax.psum_scatter(acc_bias, "dp", scatter_dimension=1, tiled=True),
    )
    return (
        jnp.stack(layer_rows),
        jnp.stack(input_rows),
        qkv_grad,
        out_grad,
        gate_up_grad,
        down_grad,
        gain_grad,
        bias_grad,
    )


def solution(mesh):
    rows_of = dict(mesh.shape)
    by_plane = rows_of == {"dp": 8, "mp": 4}
    return jax.shard_map(
        plane_body if by_plane else body,
        mesh=mesh,
        in_specs=(
            P(None, ("dp", "mp"), None, None),
            P(None, ("dp", "mp"), None, None),
            P(),
            P(None, "dp", "mp"),
            P("mp", "dp"),
            P(None, "dp", "mp"),
            P("mp", "dp"),
            P(None, "dp"),
            P(None, "dp"),
        ),
        out_specs=(
            P(None, ("dp", "mp"), None, None),
            P(None, ("dp", "mp"), None, None),
            P(None, "dp", "mp"),
            P("mp", "dp"),
            P(None, "dp", "mp"),
            P("mp", "dp"),
            P(None, "dp"),
            P(None, "dp"),
        ),
        check_vma=False,
    )
```

```python
import functools

import jax
import jax.numpy as jnp
from jax import lax
from jax.experimental import pallas as pl
from jax.experimental.pallas import tpu as pltpu
from jax.sharding import PartitionSpec as P

HEAD_DIM = 64

norm_eps = 1e-12
rope_base = 1000.0
masked_score = -1e30

BF = jnp.bfloat16
F32 = jnp.float32
LANES = 128

CORE, XBIT, YBIT = 1, 2, 4
BOTH = XBIT | YBIT


def permute(value, dp_mask, mp_mask=0):
    mp = lax.axis_size("mp")
    count = lax.axis_size("dp") * mp
    pairs = [(i, i ^ (dp_mask((i // mp) & CORE) * mp + mp_mask)) for i in range(count)]
    return lax.ppermute(value, ("dp", "mp"), pairs)


def swap(value, dp_mask=0, mp_mask=0):
    return permute(value, lambda core: dp_mask, mp_mask)


def first_mask(core):
    return XBIT + core * (YBIT - XBIT)


def second_mask(core):
    return YBIT + core * (XBIT - YBIT)


def to_first(value):
    return permute(value, first_mask)


def to_second(value):
    return permute(value, second_mask)


def to_core(value):
    return swap(value, CORE)


def gathered_masks(core):
    first, second = first_mask(core), second_mask(core)
    return (0, first, second, BOTH, CORE, CORE ^ second, CORE ^ first, CORE ^ BOTH)


def kept_masks(core):
    first, second = first_mask(core), second_mask(core)
    return (0, second, first, BOTH), (CORE, CORE ^ first, CORE ^ second, CORE ^ BOTH)


SLOTS = (0, 2, 1, 3)


def add_low(a, b):
    return (a.astype(F32) + b.astype(F32)).astype(BF)


def add_wide(a, b):
    return a.astype(F32) + b.astype(F32)


def fence(*values):
    return lax.optimization_barrier(values)


class Scatter:
    def __init__(self, keep, send=None):
        self.keep, self.go, self.stage = keep, send, 0
        if send is None:
            self.keep, self.go, self.stage = keep[:2], keep[2:], 1

    def send(self):
        self.back = (to_core, to_first, to_second)[self.stage](self.go)

    def fold(self):
        back = self.back
        self.stage += 1
        if self.stage == 1:
            self.keep, self.go = add_low(self.keep[:2], back[:2]), add_low(self.keep[2:], back[2:])
        elif self.stage == 2:
            self.go = add_low(self.keep[1], back[1])
            self.keep = add_low(self.keep[0], back[0])

    def total(self):
        return add_low(self.keep, self.back)


class Hop:
    def __init__(self, value, dp_mask=0, mp_mask=0):
        self.go, self.masks = value, (dp_mask, mp_mask)

    def send(self):
        self.back = swap(self.go, *self.masks)

    def fold(self):
        self.got = self.back


class Sum(Hop):
    def fold(self):
        self.got = self.go + self.back


def tick(carry, waits, starts):
    arrived = fence(carry, [w.back for w in waits])
    for w, back in zip(waits, arrived[1]):
        w.back = back
        w.fold()
    starts = starts() if callable(starts) else starts
    ready = fence(arrived[0], [t.go for t in starts])
    for t, go in zip(starts, ready[1]):
        t.go = go
        t.send()
    return ready[0]


def params(limit=60 << 20):
    return pltpu.CompilerParams(vmem_limit_bytes=limit)


def cost(flops, size):
    del flops, size
    return pl.CostEstimate(flops=1, bytes_accessed=1, transcendentals=0)


ANY = pl.BlockSpec(memory_space=pl.ANY)
VM = pl.BlockSpec(memory_space=pltpu.VMEM)


def dot(a, b):
    return lax.dot_general(a, b, (((1,), (0,)), ((), ())), preferred_element_type=F32)


def dot_t(a, b):
    return lax.dot_general(a, b, (((1,), (1,)), ((), ())), preferred_element_type=F32)


def dot_rows(a, b):
    return lax.dot_general(a, b, (((0,), (0,)), ((), ())), preferred_element_type=F32)


def piece_copies(pieces, buffer, sems, plane):
    mine = lax.axis_index("dp")
    masks = gathered_masks(mine & CORE)
    copies = []
    for k, piece in enumerate(pieces):
        rows = piece.shape[1]
        start = pl.multiple_of((mine ^ masks[k]) * rows, rows)
        copies.append(
            pltpu.make_async_copy(
                piece.at[plane], buffer.at[pl.ds(start, rows), :], sems.at[k]
            )
        )
    return copies


def ffn_copies(pieces, plane, wide, narrow, sems):
    mine = lax.axis_index("dp")
    masks = gathered_masks(mine & CORE)
    inner = wide.shape[1]
    copies = []
    for k, piece in enumerate(pieces):
        for core in range(2):
            rows = piece.shape[2]
            start = pl.multiple_of((mine ^ masks[k] ^ core) * rows, rows)
            source = piece.at[plane, core]
            for i, (target, lanes) in enumerate(
                ((wide, slice(0, inner)), (narrow, slice(inner, piece.shape[3])))
            ):
                copies.append(
                    pltpu.make_async_copy(
                        source.at[:, lanes],
                        target.at[pl.ds(start, rows), :],
                        sems.at[i, 2 * k + core],
                    )
                )
    return copies


def out_copies(buffer, keep, send, sems, rows):
    mine = lax.axis_index("dp")
    copies = []
    for side, (target, masks) in enumerate(zip((keep, send), kept_masks(mine & CORE))):
        for i, mask in enumerate(masks):
            start = pl.multiple_of((mine ^ mask) * rows, rows)
            copies.append(
                pltpu.make_async_copy(
                    buffer.at[pl.ds(start, rows), :], target(i), sems.at[4 * side + i]
                )
            )
    return copies


def chip_copies(buffer, keep, sems, rows):
    mine = lax.axis_index("dp")
    copies = []
    for i, mask in enumerate(kept_masks(mine & CORE)[0]):
        for core in range(2):
            start = pl.multiple_of((mine ^ mask ^ core) * rows, rows)
            copies.append(
                pltpu.make_async_copy(
                    buffer.at[pl.ds(start, rows), :], keep(i, core), sems.at[2 * i + core]
                )
            )
    return copies


def start_all(copies):
    for copy in copies:
        copy.start()


def wait_all(copies):
    for copy in copies:
        copy.wait()


def partner(u):
    lane = lax.broadcasted_iota(jnp.int32, u.shape, 1)
    quarter = HEAD_DIM // 2
    return jnp.where(
        lane % HEAD_DIM < quarter,
        pltpu.roll(u, LANES - quarter, 1),
        pltpu.roll(u, quarter, 1),
    )


def low_lanes(shape):
    return lax.broadcasted_iota(jnp.int32, shape, 1) < HEAD_DIM


def kv_kernel(planes, x_ref, tab_ref, *refs):
    pieces, (kv_ref, w, sems) = refs[:8], refs[8:]
    copies = [piece_copies(pieces, w.at[p], sems.at[p], p) for p in range(planes)]
    for group in copies:
        start_all(group)
    x = x_ref[...]
    for p in range(planes):
        wait_all(copies[p])
        y = dot(x, w[p][:, : 3 * LANES])
        y0, y1, y2 = y[:, :LANES], y[:, LANES : 2 * LANES], y[:, 2 * LANES :]
        base = p * 3 * LANES
        kv_ref[:, base : base + LANES] = (y0 * tab_ref[0] + partner(y0) * tab_ref[1]).astype(BF)
        kv_ref[:, base + LANES : base + 2 * LANES] = (
            y1 * tab_ref[2] + partner(y1) * tab_ref[3]
        ).astype(BF)
        kv_ref[:, base + 2 * LANES : base + 3 * LANES] = y2.astype(BF)


def q_kernel(planes, scale, x_ref, tab_ref, *refs):
    pieces, (q_ref, w, sems) = refs[:8], refs[8:]
    copies = [piece_copies(pieces, w.at[p], sems.at[p], p) for p in range(planes)]
    for group in copies:
        start_all(group)
    x = x_ref[...]
    for p in range(planes):
        wait_all(copies[p])
        y = dot(x, w[p][:, 3 * LANES : 5 * LANES])
        y0, y1 = y[:, :LANES], y[:, LANES:]
        low = low_lanes(y1.shape)
        base = p * 2 * LANES
        q0 = y0 * tab_ref[0] + partner(y0) * tab_ref[1]
        q1 = jnp.where(low, y1 * tab_ref[2] + partner(y1) * tab_ref[3], 0.0)
        q_ref[:, base : base + LANES] = (q0 * scale).astype(BF)
        q_ref[:, base + LANES : base + 2 * LANES] = (q1 * scale).astype(BF)


def attend_kernel(q_ref, bias_ref, *refs):
    pieces = refs[:8]
    att_ref, low_ref, lse_ref, s_ref = refs[8:]
    rows = q_ref.shape[0]
    keys = rows

    def block(k, column):
        return pieces[k][:, column * LANES : (column + 1) * LANES]

    low = low_lanes((rows, LANES))
    lane = lax.broadcasted_iota(jnp.int32, (rows, LANES), 1)
    q0, q1 = q_ref[:, :LANES], q_ref[:, LANES:]
    zero = jnp.zeros_like(q0)
    heads = (
        (jnp.where(low, q0, zero), 0, 2),
        (jnp.where(low, zero, q0), 0, 2),
        (q1, 1, 1),
    )
    stats = jnp.zeros((rows, LANES), F32)
    results = []
    for h, (q, key_column, value_column) in enumerate(heads):
        peak = jnp.full((rows, LANES), -jnp.inf, F32)
        for k in range(8):
            s = dot_t(q, block(k, key_column)) + bias_ref[k : k + 1, :]
            s_ref[:, k * keys : (k + 1) * keys] = s
            for c in range(keys // LANES):
                peak = jnp.maximum(peak, s[:, c * LANES : (c + 1) * LANES])
        top = jnp.max(peak, axis=1, keepdims=True)
        total = jnp.zeros((rows, LANES), F32)
        acc = jnp.zeros((rows, LANES), F32)
        for k in range(8):
            e = jnp.exp(s_ref[:, k * keys : (k + 1) * keys] - top)
            for c in range(keys // LANES):
                total = total + e[:, c * LANES : (c + 1) * LANES]
            acc = acc + dot(e.astype(BF), block(k, value_column))
        total = jnp.sum(total, axis=1, keepdims=True)
        results.append(acc / total)
        stats = jnp.where(lane == h, top + jnp.log(total), stats)
    pair = jnp.where(low, results[0], results[1])
    single = jnp.where(low, 0.0, results[2])
    att_ref[:, :LANES] = single
    att_ref[:, LANES:] = pair
    low_ref[:, :LANES] = single.astype(BF)
    low_ref[:, LANES:] = pair.astype(BF)
    lse_ref[0] = stats.T[:8, :]


def attend_back_kernel(
    scale, q_ref, dat_ref, lse_ref, delta_ref, bias_ref, tab_ref, *refs
):
    pieces = refs[:8]
    keep_ref, send_ref, dq_ref = refs[8:]
    rows = q_ref.shape[0]

    def block(k, column):
        return pieces[k][:, column * LANES : (column + 1) * LANES]

    low = low_lanes((rows, LANES))
    q0, q1 = q_ref[:, :LANES], q_ref[:, LANES:]
    d0, d1 = dat_ref[:, LANES:], dat_ref[:, :LANES]
    zero = jnp.zeros_like(q0)
    heads = (
        (jnp.where(low, q0, zero), jnp.where(low, d0, zero), 0, 2),
        (jnp.where(low, zero, q0), jnp.where(low, zero, d0), 0, 2),
        (q1, d1, 1, 1),
    )
    dq = [jnp.zeros((LANES, rows), F32) for _ in heads]
    for k in range(8):
        side, index = divmod(k, 4)
        target = (keep_ref, send_ref)[side]
        slot = SLOTS[index]
        mask = bias_ref[:, k : k + 1]
        blocks = [block(k, c) for c in range(3)]
        keys_t = [blocks[0].T, blocks[1].T]
        parts = []
        for h, (q, d, key_column, value_column) in enumerate(heads):
            s = dot_t(blocks[key_column], q) + mask
            dp = dot_t(blocks[value_column], d)
            p = jnp.exp(s - lse_ref[0, h : h + 1, :])
            ds = (p * (dp - delta_ref[0, h : h + 1, :])).astype(BF)
            p = p.astype(BF)
            parts.append((dot(ds, q), dot(p, d)))
            dq[h] = dq[h] + dot(keys_t[key_column], ds)
        target[slot, :, :LANES] = (parts[0][0] + parts[1][0]).astype(BF)
        target[slot, :, LANES : 2 * LANES] = (parts[2][0] + parts[2][1]).astype(BF)
        target[slot, :, 2 * LANES :] = (parts[0][1] + parts[1][1]).astype(BF)
    row = lax.broadcasted_iota(jnp.int32, (LANES, rows), 0) < HEAD_DIM
    pair = jnp.where(row, dq[0], dq[1]).T * scale
    single = jnp.where(row, dq[2], 0.0).T * scale
    dq_ref[:, :LANES] = (pair * tab_ref[0] - partner(pair) * tab_ref[1]).astype(BF)
    dq_ref[:, LANES:] = (single * tab_ref[2] - partner(single) * tab_ref[3]).astype(BF)


def center_scale(rows):
    center = rows - jnp.mean(rows, axis=-1, keepdims=True)
    inv = lax.rsqrt(jnp.mean(center * center, axis=-1, keepdims=True) + norm_eps)
    return center * inv, inv


def norm_back(e, scaled, inv):
    return inv * (
        e
        - jnp.mean(e, axis=-1, keepdims=True)
        - scaled * jnp.mean(e * scaled, axis=-1, keepdims=True)
    )


def rows_sum(value):
    return jnp.sum(value, axis=0, keepdims=True)


def mix_kernel(planes, x_ref, att_ref, norm_ref, *refs):
    pieces = refs[:8]
    flow_ref, first_ref, scaled_ref, inv_ref, w, sems = refs[8:]
    copies = [piece_copies(pieces, w.at[p], sems.at[p], p) for p in range(planes)]
    for group in copies:
        start_all(group)
    total = x_ref[...].astype(F32)
    for p in range(planes):
        wait_all(copies[p])
        total = total + dot_t(
            att_ref[:, p * 2 * LANES : (p + 1) * 2 * LANES], w[p][:, 4 * LANES : 6 * LANES]
        )
    scaled, inv = center_scale(total)
    scaled_ref[...] = scaled
    inv_ref[...] = jnp.broadcast_to(inv, inv_ref.shape)
    first = scaled * norm_ref[0:1, :] + norm_ref[2:3, :]
    first_ref[...] = first
    flow_ref[...] = first.astype(BF)


def ffn_kernel(planes, own_ref, other_ref, *refs):
    wide = (refs[:4], refs[4:8])
    ffn_ref, send_ref, gate_ref, up_ref, wgu, wd, hold, flow, sems, hold_sems = refs[8:]
    half = planes // 2
    rows = own_ref.shape[0]
    copies = [
        ffn_copies(wide[p // half], p % half, wgu.at[p], wd.at[p], sems.at[p])
        for p in range(planes)
    ]
    for group in copies:
        start_all(group)
    flow[:rows, :] = own_ref[...]
    flow[rows:, :] = other_ref[...]
    total = jnp.zeros(flow.shape, F32)
    inner = wd.shape[2]
    saves = []
    for p in range(planes):
        wait_all(copies[p])
        both = dot(flow[...], wgu[p])
        gate, up = both[:, :inner], both[:, inner:]
        hold[p, 0] = gate
        hold[p, 1] = up
        for k, target in enumerate((gate_ref, up_ref)):
            copy = pltpu.make_async_copy(hold.at[p, k], target.at[p], hold_sems.at[p, k])
            copy.start()
            saves.append(copy)
        hidden = (gate * jax.nn.sigmoid(gate) * up).astype(BF)
        total = total + dot_t(hidden, wd[p])
    ffn_ref[...] = total[:rows]
    send_ref[...] = total[rows:].astype(BF)
    wait_all(saves)


def close_kernel(ffn_ref, back_ref, first_ref, cot_ref, norm_ref, out_ref, dz2_ref, dffn_ref, sums_ref):
    gain, bias = norm_ref[1:2, :], norm_ref[3:4, :]
    scaled, inv = center_scale(first_ref[...] + (ffn_ref[...] + back_ref[...].astype(F32)))
    out_ref[...] = (scaled * gain + bias).astype(BF)
    cot = cot_ref[...].astype(F32)
    dz2 = norm_back(cot * gain, scaled, inv)
    dz2_ref[...] = dz2
    dffn_ref[...] = dz2.astype(BF)
    sums_ref[...] = jnp.concatenate(
        [rows_sum(cot * scaled), rows_sum(cot), jnp.zeros((6, cot.shape[1]), F32)], axis=0
    )


def ffn_back_kernel(slab, has_acc, *refs):
    if has_acc:
        acc_ref, refs = refs[0], refs[1:]
    flow_own, flow_other, dffn_own, dffn_other, gate_ref, up_ref = refs[:6]
    pieces, refs = refs[6:10], refs[10:]
    dfirst_ref, send_ref, keep_ref, wgu, wd, flow, dffn, hidden, grads, sems, out_sems = refs
    rows = flow_own.shape[0]
    count = gate_ref.shape[0]
    inner = gate_ref.shape[2]
    copies = []
    for p in range(count):
        group = ffn_copies(
            pieces, p, wgu.at[p], wd.at[:, p * inner : (p + 1) * inner], sems.at[p]
        )
        start_all(group)
        copies.extend(group)
    flow[:rows, :] = flow_own[...]
    flow[rows:, :] = flow_other[...]
    dffn[:rows, :] = dffn_own[...]
    dffn[rows:, :] = dffn_other[...]
    for p in range(count):
        gate = gate_ref[p]
        hidden[:, p * inner : (p + 1) * inner] = (
            gate * jax.nn.sigmoid(gate) * up_ref[p]
        ).astype(BF)
    down = dot(dffn[...].T, hidden[...])
    for p in range(count):
        grads[p, :, 2 * inner :] = down[:, p * inner : (p + 1) * inner].astype(BF)
    wait_all(copies)
    d_hidden = dot(dffn[...], wd[...])
    flow_t = flow[...].T
    total = acc_ref[...] if has_acc else jnp.zeros(flow.shape, F32)
    outs = []
    for p in range(count):
        gate, up = gate_ref[p], up_ref[p]
        d = d_hidden[:, p * inner : (p + 1) * inner]
        sig = jax.nn.sigmoid(gate)
        d_gate = (d * up * sig * (1.0 + gate * (1.0 - sig))).astype(BF)
        d_up = (d * (gate * sig)).astype(BF)
        both = jnp.concatenate([d_gate, d_up], axis=1)
        grads[p, :, : 2 * inner] = dot(flow_t, both).astype(BF)
        group = chip_copies(
            grads.at[p], lambda i, core: keep_ref.at[i, p, core], out_sems.at[p], slab
        )
        start_all(group)
        outs.extend(group)
        total = total + dot_t(both, wgu[p])
    dfirst_ref[...] = total
    send_ref[...] = total[rows:].astype(BF)
    wait_all(outs)


def branch_back_kernel(
    planes, dfirst_ref, back_ref, dz2_ref, scaled_ref, inv_ref, norm_ref, two_ref, att_ref, *refs
):
    pieces = refs[:8]
    dz1_ref, dat_ref, delta_ref, sums_ref, w, sems = refs[8:]
    copies = [piece_copies(pieces, w.at[p], sems.at[p], p) for p in range(planes)]
    for group in copies:
        start_all(group)
    dfirst = dfirst_ref[...] + back_ref[...].astype(F32) + dz2_ref[...]
    scaled = scaled_ref[...]
    two = two_ref[...]
    sums_ref[...] = jnp.concatenate(
        [
            rows_sum(dfirst * scaled),
            two[0:1],
            rows_sum(dfirst),
            two[1:2],
            jnp.zeros((4, dfirst.shape[1]), F32),
        ],
        axis=0,
    )
    dz1 = norm_back(dfirst * norm_ref[0:1, :], scaled, inv_ref[:, 0:1])
    dz1_ref[...] = dz1
    d_branch = dz1.astype(BF)
    low = low_lanes((dfirst.shape[0], LANES))
    lane = lax.broadcasted_iota(jnp.int32, (dfirst.shape[0], LANES), 1)
    for p in range(planes):
        wait_all(copies[p])
        d = dot(d_branch, w[p][:, 4 * LANES : 6 * LANES])
        single = jnp.where(low, 0.0, d[:, :LANES]).astype(BF)
        pair = d[:, LANES:].astype(BF)
        dat_ref[:, p * 2 * LANES : p * 2 * LANES + LANES] = single
        dat_ref[:, p * 2 * LANES + LANES : (p + 1) * 2 * LANES] = pair
        both = pair.astype(F32) * att_ref[:, p * 2 * LANES + LANES : (p + 1) * 2 * LANES]
        alone = single.astype(F32) * att_ref[:, p * 2 * LANES : p * 2 * LANES + LANES]
        zero = jnp.zeros_like(both)
        stats = zero
        for h, part in enumerate((jnp.where(low, both, zero), jnp.where(low, zero, both), alone)):
            stats = jnp.where(lane == h, jnp.sum(part, axis=1, keepdims=True), stats)
        delta_ref[p] = stats.T[:8, :]


def query_back_kernel(planes, slab, x_ref, low_dq_ref, high_dq_ref, dz1_ref, low_ref, *refs):
    pieces = refs[:8]
    din_ref, keep_ref, send_ref, w, grads, sems, out_sems = refs[8:]
    half = planes // 2
    copies = [piece_copies(pieces, w.at[p], sems.at[p], p) for p in range(planes)]
    for group in copies:
        start_all(group)
    x_t = x_ref[...].T
    total = dz1_ref[...]
    branch_t = total.astype(BF).T
    outs = []
    for p in range(planes):
        at = (p % half) * 2 * LANES
        d = (low_dq_ref, high_dq_ref)[p // half][:, at : at + 2 * LANES]
        query = dot(x_t, d)
        output = dot(branch_t, low_ref[:, p * 2 * LANES : (p + 1) * 2 * LANES])
        grads[p, :, :LANES] = query[:, :LANES].astype(BF)
        grads[p, :, LANES : 2 * LANES] = (query[:, LANES:] + output[:, :LANES]).astype(BF)
        grads[p, :, 2 * LANES :] = output[:, LANES:].astype(BF)
        group = out_copies(
            grads.at[p],
            lambda i: keep_ref.at[i, p],
            lambda i: send_ref.at[i, p],
            out_sems.at[p],
            slab,
        )
        start_all(group)
        outs.extend(group)
        wait_all(copies[p])
        total = total + dot_t(d, w[p][:, 3 * LANES : 5 * LANES])
    din_ref[...] = total
    wait_all(outs)


def kv_back_kernel(base, count, slab, x_ref, acc_ref, tab_ref, keep_d_ref, back_d_ref, *refs):
    pieces = refs[:8]
    din_ref, keep_ref, send_ref, w, grads, sems, out_sems = refs[8:]
    copies = [piece_copies(pieces, w.at[p], sems.at[p], base + p) for p in range(count)]
    for group in copies:
        start_all(group)
    x_t = x_ref[...].T
    total = acc_ref[...]
    outs = []
    for p in range(count):
        lanes = slice(p * 3 * LANES, (p + 1) * 3 * LANES)
        d = keep_d_ref[:, lanes].astype(F32) + back_d_ref[:, lanes].astype(F32)
        d0, d1, d2 = d[:, :LANES], d[:, LANES : 2 * LANES], d[:, 2 * LANES :]
        d = jnp.concatenate(
            [
                (d0 * tab_ref[0] - partner(d0) * tab_ref[1]).astype(BF),
                (d1 * tab_ref[2] - partner(d1) * tab_ref[3]).astype(BF),
                d2.astype(BF),
            ],
            axis=1,
        )
        grads[p] = dot(x_t, d).astype(BF)
        group = out_copies(
            grads.at[p],
            lambda i: keep_ref.at[i, p],
            lambda i: send_ref.at[i, p],
            out_sems.at[p],
            slab,
        )
        start_all(group)
        outs.extend(group)
        wait_all(copies[p])
        total = total + dot_t(d, w[p][:, : 3 * LANES])
    din_ref[...] = total.astype(din_ref.dtype)
    wait_all(outs)


def sds(shape, dtype):
    return jax.ShapeDtypeStruct(shape, dtype)


def plane_body(
    hidden_in,
    cotangent,
    lengths,
    qkv_weight,
    out_weight,
    gate_up_weight,
    down_weight,
    norm_gain,
    norm_bias,
):
    planes = lax.axis_size("mp")
    pair = planes // 2
    group = lax.axis_size("dp")
    dp, mp = lax.axis_index("dp"), lax.axis_index("mp")
    core = dp & CORE
    part = hidden_in.shape[1]
    width = hidden_in.shape[3]
    rows = part * planes
    slab = qkv_weight.shape[1]
    inner = gate_up_weight.shape[2] // 2
    scale = HEAD_DIM ** (-0.5)
    mine = mp ^ jnp.arange(planes, dtype=jnp.int32)
    others = range(1, planes)

    def blocks_of(array):
        array = array.reshape(array.shape[0], part, width)
        return [lax.dynamic_index_in_dim(array, mine[j], 0, keepdims=False) for j in range(planes)]

    q_w, k_w, v_w = qkv_weight[0], qkv_weight[1], qkv_weight[2]
    o_w, d_w = out_weight.T, down_weight.T
    two = 2 * HEAD_DIM
    own = jnp.concatenate(
        [k_w[:, :two], k_w[:, two:], v_w[:, two:], v_w[:, :two]]
        + [q_w[:, :two], q_w[:, two:], o_w[:, two:], o_w[:, :two]],
        axis=1,
    )
    x_blocks, cot_blocks = blocks_of(hidden_in), blocks_of(cotangent)

    def half_of(index):
        take = lambda w: lax.dynamic_slice_in_dim(w, index * inner, inner, 1)
        return jnp.concatenate([take(gate_up_weight[0]), take(gate_up_weight[1]), take(d_w)], axis=1)

    ffn_mine, ffn_give = half_of(core), half_of(1 - core)
    norm_own = jnp.concatenate([norm_gain, norm_bias, jnp.zeros((4, slab), BF)], axis=0)
    norms = lax.dynamic_update_slice(
        jnp.zeros((8, width), F32), norm_own.astype(F32), (0, dp * slab)
    )

    z = [swap(own, 0, j) for j in others]
    ffn_get = to_core(ffn_give)
    norm_back_ = swap(norms, CORE)
    z, ffn_get, norm_back_, x_blocks = fence(z, ffn_get, norm_back_, x_blocks)
    norms = norms + norm_back_
    w_four = jnp.stack([own] + z)
    ffn_own = jnp.stack([ffn_mine, ffn_get])
    x_give = jnp.stack([x_blocks[1], x_blocks[3]])
    w_first, w_second = to_first(w_four), to_second(w_four)
    f_one = swap(ffn_own, 0, 1)
    x_got = swap(x_give, 0, 1)
    norm_back_ = swap(norms, XBIT)
    w_first, w_second, x_got, norm_back_, f_one, ffn_own, w_four = fence(
        w_first, w_second, x_got, norm_back_, f_one, ffn_own, w_four
    )
    norms = norms + norm_back_
    w_diag = to_second(w_first)
    low = [jnp.stack([ffn_own, f_one])]
    low.append(to_first(low[0]))
    x_far = swap(jnp.stack([x_blocks[2], x_got[1]]), 0, 2)
    w_core = [to_core(w_four), to_core(w_first)]
    w_diag, w_core, w_second, x_far, ffn_own, norms = fence(
        w_diag, w_core, w_second, x_far, ffn_own, norms
    )
    w_core += [to_core(w_second), to_core(w_diag)]
    f_two = swap(ffn_own, 0, 2)
    norm_back_ = swap(norms, YBIT)
    x = jnp.concatenate([x_blocks[0], x_got[0], x_far[0], x_far[1]], axis=0)
    w_core, low[0], x = fence(w_core, low[0], x)
    weights = [w_four, w_first, w_second, w_diag] + w_core
    low.append(to_second(low[0]))

    within = (mine[:, None] * part + jnp.arange(part, dtype=jnp.int32)[None, :]).reshape(rows)
    positions = (dp * rows + within).astype(F32)
    half = HEAD_DIM // 2
    exponent = jnp.arange(half, dtype=F32) * (1.0 / half)
    angles = positions[:, None] * jnp.power(rope_base, -exponent)[None, :]
    cosine, sine = jnp.cos(angles), jnp.sin(angles)
    cos_head = jnp.concatenate([cosine, cosine], axis=1)
    sin_head = jnp.concatenate([-sine, sine], axis=1)
    one, none = jnp.ones_like(cos_head), jnp.zeros_like(cos_head)
    cat = lambda a, b: jnp.concatenate([a, b], axis=1)
    tables = jnp.stack(
        [cat(cos_head, cos_head), cat(sin_head, sin_head), cat(cos_head, one), cat(sin_head, none)]
    )
    length = lax.dynamic_index_in_dim(lengths.reshape(-1), mp, 0, keepdims=False)
    piece_base = (dp ^ jnp.stack([jnp.int32(0) + m for m in gathered_masks(core)])) * rows
    key_pos = piece_base[:, None] + within[None, :]
    bias = jnp.where(key_pos < length, 0.0, masked_score).astype(F32)
    bias_t = bias.T

    dma = pltpu.SemaphoreType.DMA
    w_scratch = [pltpu.VMEM((planes, width, 6 * LANES), BF), dma((planes, 8))]

    def project(kernel, columns, name):
        return pl.pallas_call(
            kernel,
            out_shape=sds((rows, planes * columns), BF),
            in_specs=[VM, VM] + [ANY] * 8,
            out_specs=VM,
            scratch_shapes=w_scratch,
            compiler_params=params(),
            cost_estimate=cost(1, 1),
            name=name,
        )(x, tables, *weights)

    kv = project(functools.partial(kv_kernel, planes), 3 * LANES, "kv_project")
    kv, low[2], norm_back_, f_two, low[1], f_one, bias, bias_t = fence(
        kv, low[2], norm_back_, f_two, low[1], f_one, bias, bias_t
    )
    norms = norms + norm_back_
    keys = [kv, to_first(kv), to_second(kv)]
    key_core = [to_core(kv)]
    f_three = swap(f_one, 0, 2)
    q = project(functools.partial(q_kernel, planes, scale), 2 * LANES, "q_project")
    q, keys[1], keys[2], key_core, low[1], f_three, cot_blocks = fence(
        q, keys[1], keys[2], key_core, low[1], f_three, cot_blocks
    )
    keys.append(to_second(keys[1]))
    low.append(to_second(low[1]))
    high = [jnp.stack([f_two, f_three])]
    high.append(to_first(high[0]))
    key_core += [to_core(keys[1]), to_core(keys[2])]
    keys[3], key_core, low[3], cot_blocks, high[0] = fence(
        keys[3], key_core, low[3], cot_blocks, high[0]
    )
    key_core.append(to_core(keys[3]))
    high.append(to_second(high[0]))
    cot_got = swap(jnp.stack([cot_blocks[1], cot_blocks[3]]), 0, 1)
    key_core, high[1], cot_got, cot_blocks = fence(key_core, high[1], cot_got, cot_blocks)
    kv_all = keys + key_core
    high.append(to_second(high[1]))
    cot_far = swap(jnp.stack([cot_blocks[2], cot_got[1]]), 0, 2)

    at_spec = lambda base, columns: pl.BlockSpec((rows, columns), lambda i: (0, i + base))
    seq = rows * group
    att, att_low, lse = pl.pallas_call(
        attend_kernel,
        grid=(planes,),
        out_shape=(
            sds((rows, planes * 2 * LANES), F32),
            sds((rows, planes * 2 * LANES), BF),
            sds((planes, 8, rows), F32),
        ),
        in_specs=[at_spec(0, 2 * LANES), pl.BlockSpec((8, rows), lambda i: (0, 0))]
        + [at_spec(0, 3 * LANES)] * 8,
        out_specs=(
            at_spec(0, 2 * LANES),
            at_spec(0, 2 * LANES),
            pl.BlockSpec((1, 8, rows), lambda i: (i, 0, 0)),
        ),
        scratch_shapes=[pltpu.VMEM((rows, seq), F32)],
        compiler_params=params(),
        cost_estimate=cost(1, 1),
        name="attend",
    )(q, bias, *kv_all)
    act = lambda dtype: sds((rows, width), dtype)
    flow, first, scaled, inv = pl.pallas_call(
        functools.partial(mix_kernel, planes),
        out_shape=(act(BF), act(F32), act(F32), sds((rows, LANES), F32)),
        in_specs=[VM] * 3 + [ANY] * 8,
        out_specs=(VM,) * 4,
        scratch_shapes=w_scratch,
        compiler_params=params(),
        cost_estimate=cost(1, 1),
        name="mix",
    )(x, att_low, norms, *weights)
    flow_other = to_core(flow)
    flow, high[2], high[3], cot_got, cot_far, flow_other = fence(
        flow, high[2], high[3], cot_got, cot_far, flow_other
    )
    cot = jnp.concatenate([cot_blocks[0], cot_got[0], cot_far[0], cot_far[1]], axis=0)

    saved = sds((planes, 2 * rows, inner), F32)
    ffn, give, gate, up = pl.pallas_call(
        functools.partial(ffn_kernel, planes),
        out_shape=(act(F32), act(BF), saved, saved),
        in_specs=[VM] * 2 + [ANY] * 8,
        out_specs=(VM, VM, ANY, ANY),
        scratch_shapes=[
            pltpu.VMEM((planes, width, 2 * inner), BF),
            pltpu.VMEM((planes, width, inner), BF),
            pltpu.VMEM((planes, 2, 2 * rows, inner), F32),
            pltpu.VMEM((2 * rows, width), BF),
            dma((planes, 2, 8)),
            dma((planes, 2)),
        ],
        compiler_params=params(),
        cost_estimate=cost(1, 1),
        name="ffn",
    )(flow, flow_other, *low, *high)
    layer_out, dz2, dffn, sums_two = pl.pallas_call(
        close_kernel,
        out_shape=(act(BF), act(F32), act(BF), sds((8, width), F32)),
        in_specs=[VM] * 5,
        out_specs=(VM,) * 4,
        compiler_params=params(),
        cost_estimate=cost(1, 1),
        name="close",
    )(ffn, to_core(give), first, cot, norms)
    dffn_other = to_core(dffn)

    def ffn_back(pieces, base, acc):
        block = pl.BlockSpec((pair, 2 * rows, inner), lambda i: (base, 0, 0))
        whole = lambda count: pl.BlockSpec((count * rows, width), lambda i: (0, 0))
        return pl.pallas_call(
            functools.partial(ffn_back_kernel, slab, acc is not None),
            grid=(1,),
            out_shape=(
                sds((2 * rows, width), F32),
                act(BF),
                sds((4, pair, 2, slab, 3 * inner), BF),
            ),
            in_specs=[whole(2)] * (acc is not None) + [whole(1)] * 4 + [block] * 2 + [ANY] * 4,
            out_specs=(whole(2), whole(1), ANY),
            scratch_shapes=[
                pltpu.VMEM((pair, width, 2 * inner), BF),
                pltpu.VMEM((width, pair * inner), BF),
                pltpu.VMEM((2 * rows, width), BF),
                pltpu.VMEM((2 * rows, width), BF),
                pltpu.VMEM((2 * rows, pair * inner), BF),
                pltpu.VMEM((pair, width, 3 * inner), BF),
                dma((pair, 2, 8)),
                dma((pair, 8)),
            ],
            compiler_params=params(),
            cost_estimate=cost(1, 1),
            name="ffn_back",
        )(*([] if acc is None else [acc]), flow, flow_other, dffn, dffn_other, gate, up, *pieces)

    def attend_back(base, q, dat):
        stat = pl.BlockSpec((1, 8, rows), lambda i: (i + base, 0, 0))
        keep_spec = pl.BlockSpec((4, rows, 3 * LANES), lambda i: (0, 0, i))
        return pl.pallas_call(
            functools.partial(attend_back_kernel, scale),
            grid=(pair,),
            out_shape=(
                sds((4, rows, pair * 3 * LANES), BF),
                sds((4, rows, pair * 3 * LANES), BF),
                sds((rows, pair * 2 * LANES), BF),
            ),
            in_specs=[
                at_spec(base, 2 * LANES),
                at_spec(base, 2 * LANES),
                stat,
                stat,
                pl.BlockSpec((rows, 8), lambda i: (0, 0)),
                pl.BlockSpec((4, rows, LANES), lambda i: (0, 0, 0)),
            ]
            + [at_spec(base, 3 * LANES)] * 8,
            out_specs=(keep_spec, keep_spec, at_spec(0, 2 * LANES)),
            compiler_params=params(),
            cost_estimate=cost(1, 1),
            name="attend_back",
        )(q, dat, lse, delta, bias_t, tables, *kv_all)

    out_blocks = [layer_out[j * part : (j + 1) * part] for j in range(planes)]
    near_out = Hop(jnp.stack([out_blocks[1], out_blocks[3]]), 0, 1)
    dfirst, _, keep = ffn_back(high, 1, None)
    high_sum = Scatter(keep)
    dfirst = tick(dfirst, [], [high_sum, near_out])
    dfirst, give, keep = ffn_back(low, 0, dfirst)
    low_sum = Scatter(keep)
    give_hop = Hop(give, CORE)
    dfirst = tick(dfirst, [near_out], [give_hop])
    far_out = Hop(jnp.stack([out_blocks[2], near_out.got[1]]), 0, 2)
    dfirst = tick(dfirst, [give_hop, high_sum], [high_sum, low_sum, far_out])
    dz1, dat, delta, sums = pl.pallas_call(
        functools.partial(branch_back_kernel, planes),
        grid=(1,),
        out_shape=(
            act(F32),
            sds((rows, planes * 2 * LANES), BF),
            sds((planes, 8, rows), F32),
            sds((8, width), F32),
        ),
        in_specs=[pl.BlockSpec((rows, width), lambda i: (0, 0))] + [VM] * 7 + [ANY] * 8,
        out_specs=(VM,) * 4,
        scratch_shapes=w_scratch,
        compiler_params=params(),
        cost_estimate=cost(1, 1),
        name="branch_back",
    )(dfirst, give_hop.got, dz2, scaled, inv, norms, sums_two, att, *weights)

    stages = [Sum(sums, CORE)]

    def next_sum(dp_mask, mp_mask=0):
        stages.append(Sum(stages[-1].got, dp_mask, mp_mask))
        return stages[-1]

    dat = tick(dat, [far_out], [stages[0]])
    keep, send, high_dq = attend_back(pair, q, dat)
    high_keys = Scatter(keep, send)
    dat, high_dq = fence(dat, high_dq)
    far = {}

    def hop_to_two(k):
        far[k] = Hop(high_total[k], 0, 2)
        return far[k]

    arrived = fence(dat, high_sum.back)
    dat, high_sum.back = arrived
    high_total = high_sum.total()
    dat = tick(
        dat,
        [low_sum, stages[0]],
        lambda: [hop_to_two(0), low_sum, high_keys, next_sum(XBIT)],
    )
    keep, send, low_dq = attend_back(0, q, dat)
    low_keys = Scatter(keep, send)
    low_dq, low_sum.back = fence(low_dq, low_sum.back)
    low_total = low_sum.total()
    low_dq = tick(
        low_dq,
        [far[0], high_keys, stages[1]],
        lambda: [hop_to_two(1), high_keys, low_keys, next_sum(YBIT)],
    )

    def grads_shape(count):
        return sds((4, count, slab, 3 * LANES), BF)

    din, keep, send = pl.pallas_call(
        functools.partial(query_back_kernel, planes, slab),
        out_shape=(act(F32), grads_shape(planes), grads_shape(planes)),
        in_specs=[VM] * 5 + [ANY] * 8,
        out_specs=(VM, ANY, ANY),
        scratch_shapes=[
            pltpu.VMEM((planes, width, 6 * LANES), BF),
            pltpu.VMEM((planes, width, 3 * LANES), BF),
            dma((planes, 8)),
            dma((planes, 8)),
        ],
        compiler_params=params(),
        cost_estimate=cost(1, 1),
        name="query_back",
    )(x, low_dq, high_dq, dz1, att_low, *weights)
    queries = Scatter(keep, send)
    din = tick(
        din,
        [high_keys, low_keys, stages[2]],
        lambda: [high_keys, low_keys, queries, next_sum(0, 1)],
    )

    def kv_back(base, sum_, din, out_type):
        din, keep, send = pl.pallas_call(
            functools.partial(kv_back_kernel, base, pair, slab),
            out_shape=(act(out_type), grads_shape(pair), grads_shape(pair)),
            in_specs=[VM] * 5 + [ANY] * 8,
            out_specs=(VM, ANY, ANY),
            scratch_shapes=[
                pltpu.VMEM((pair, width, 6 * LANES), BF),
                pltpu.VMEM((pair, width, 3 * LANES), BF),
                dma((pair, 8)),
                dma((pair, 8)),
            ],
            compiler_params=params(),
            cost_estimate=cost(1, 1),
            name="kv_back",
        )(x, din, tables, sum_.keep, sum_.back, *weights)
        return din, Scatter(keep, send)

    din, far[1].back = fence(din, far[1].back)
    near_total = add_low(low_total, jnp.stack([far[0].got, far[1].back]))
    near = Hop(near_total[1], 0, 1)
    din, high_keys.back = fence(din, high_keys.back)
    din, high_w = kv_back(pair, high_keys, din, F32)
    din = tick(
        din,
        [low_keys, queries, stages[3]],
        lambda: [low_keys, queries, high_w, near, next_sum(0, 2)],
    )
    din, near.back = fence(din, near.back)
    ffn_sum = near_total[0].astype(F32) + near.back.astype(F32)
    last_hop = Hop(ffn_sum[1].astype(BF), CORE)
    din = tick(din, [queries, high_w], lambda: [queries, high_w, last_hop])
    din, low_keys.back = fence(din, low_keys.back)
    din, low_w = kv_back(0, low_keys, din, BF)
    din = tick(din, [high_w, last_hop, stages[4]], lambda: [low_w, high_w])
    mine_sum, other_sum = ffn_sum[0], last_hop.got.astype(F32)
    even, odd = jnp.where(core == 0, mine_sum, other_sum), jnp.where(core == 0, other_sum, mine_sum)
    join = lambda k: cat(even[:, k * inner : (k + 1) * inner], odd[:, k * inner : (k + 1) * inner])
    gate_up_grad = jnp.stack([join(0), join(1)])
    down_grad = join(2).T
    din_blocks = [din[j * part : (j + 1) * part] for j in range(planes)]
    near_din = Hop(jnp.stack([din_blocks[1], din_blocks[3]]), 0, 1)
    carry, queries.back = fence(din, queries.back)
    q_total = queries.total()
    q_far = Hop(q_total[pair:], 0, 2)
    carry = tick(carry, [low_w], lambda: [low_w, near_din, q_far])
    carry, high_w.back = fence(carry, high_w.back)
    v_far = Hop(high_w.total(), 0, 2)
    far_din = None

    def more():
        nonlocal far_din
        far_din = Hop(jnp.stack([din_blocks[2], near_din.got[1]]), 0, 2)
        return far_din

    q_pair = None

    def q_more():
        nonlocal q_pair
        q_pair = add_low(q_total[:pair], q_far.got)
        return Hop(q_pair[1], 0, 1)

    q_near = None

    def starts():
        nonlocal q_near
        q_near = q_more()
        return [low_w, v_far, more(), q_near]

    carry = tick(carry, [low_w, near_din, q_far], starts)
    carry, low_w.back, v_far.back = fence(carry, low_w.back, v_far.back)
    v_pair = add_low(low_w.total(), v_far.back)
    v_near = Hop(v_pair[1], 0, 1)
    carry = tick(carry, [far_din, q_near], [v_near])
    carry = tick(carry, [v_near], [])
    qo_grad = add_wide(q_pair[0], q_near.got)
    kv_grad = add_wide(v_pair[0], v_near.got)

    def in_order(own, near_hop, far_hop):
        got = jnp.stack([own, near_hop.got[0], far_hop.got[0], far_hop.got[1]])
        return jnp.stack(
            [lax.dynamic_index_in_dim(got, mine[m], 0, keepdims=False) for m in range(planes)]
        )

    layer_rows = in_order(out_blocks[0], near_out, far_out)
    input_grad = in_order(din_blocks[0], near_din, far_din)
    sums = lax.dynamic_slice_in_dim(stages[4].got, dp * slab, slab, 1)
    shape = hidden_in.shape
    heads = 3 * HEAD_DIM
    qkv_grad = jnp.stack(
        [
            qo_grad[:, :heads],
            kv_grad[:, :heads],
            cat(kv_grad[:, 2 * LANES :], kv_grad[:, heads : 2 * LANES]),
        ]
    )
    out_grad = cat(qo_grad[:, 2 * LANES :], qo_grad[:, heads : 2 * LANES]).T
    return (
        layer_rows.reshape(shape),
        input_grad.reshape(shape).astype(F32),
        qkv_grad,
        out_grad,
        gate_up_grad,
        down_grad,
        sums[0:2],
        sums[2:4],
    )


def rope_tables(positions, half_dim):
    exponent = jnp.arange(half_dim, dtype=jnp.float32) * (1.0 / half_dim)
    inverse = jnp.power(rope_base, -exponent)
    angles = positions[:, None] * inverse[None, :]
    return (jnp.cos(angles), jnp.sin(angles))


def rotate(vectors, cosine, sine_table):
    half_dim = vectors.shape[-1] // 2
    first_half = vectors[..., :half_dim]
    second_half = vectors[..., half_dim:]
    return jnp.concatenate(
        [
            first_half * cosine - second_half * sine_table,
            second_half * cosine + first_half * sine_table,
        ],
        axis=-1,
    )


def rotate_back(gradient, cosine, sine_table):
    half_dim = gradient.shape[-1] // 2
    first_half = gradient[..., :half_dim]
    second_half = gradient[..., half_dim:]
    return jnp.concatenate(
        [
            first_half * cosine + second_half * sine_table,
            second_half * cosine - first_half * sine_table,
        ],
        axis=-1,
    )


def normalize(residual_stream, gain_row, bias_row):
    center = residual_stream - jnp.mean(residual_stream, axis=-1, keepdims=True)
    inv_std = lax.rsqrt(jnp.mean(center * center, axis=-1, keepdims=True) + norm_eps)
    scaled = center * inv_std
    return (scaled * gain_row + bias_row, scaled, inv_std)


def normalize_back(upstream, scaled, inv_std, gain_row):
    d_scaled = upstream * gain_row
    d_stream = inv_std * (
        d_scaled
        - jnp.mean(d_scaled, axis=-1, keepdims=True)
        - scaled * jnp.mean(d_scaled * scaled, axis=-1, keepdims=True)
    )
    return (d_stream, jnp.sum(upstream * scaled, axis=(0, 1)), jnp.sum(upstream, axis=(0, 1)))


def split_heads(rows, head_dim):
    return rows.reshape(
        rows.shape[0], rows.shape[1], rows.shape[2] // head_dim, head_dim
    ).transpose(1, 2, 0, 3)


def merge_heads(heads):
    return heads.transpose(2, 0, 1, 3).reshape(
        heads.shape[2], heads.shape[0], heads.shape[1] * heads.shape[3]
    )


def score_grads(
    query_part, grad_part, lse_part, delta_part, key_part, value_part, mask_part, score_scale
):
    scores = (
        jnp.einsum("shqd,shkd->shqk", query_part, key_part, preferred_element_type=jnp.float32)
        * score_scale
    )
    prob_full = jnp.where(mask_part, jnp.exp(scores - lse_part[..., None]), 0.0)
    d_probs = jnp.einsum(
        "shqd,shkd->shqk", grad_part, value_part, preferred_element_type=jnp.float32
    )
    d_scores = (prob_full * (d_probs - delta_part[..., None]) * score_scale).astype(jnp.bfloat16)
    return (d_scores, prob_full.astype(jnp.bfloat16))


def body(
    hidden_in,
    cotangent,
    lengths,
    qkv_weight,
    out_weight,
    gate_up_weight,
    down_weight,
    norm_gain,
    norm_bias,
):
    query_key_value_matrix, output_matrix, gate_up_matrix, down_matrix, gain_rows, bias_rows = (
        lax.all_gather(qkv_weight, "dp", axis=1, tiled=True),
        lax.all_gather(out_weight, "dp", axis=1, tiled=True),
        lax.all_gather(gate_up_weight, "dp", axis=1, tiled=True),
        lax.all_gather(down_weight, "dp", axis=1, tiled=True),
        lax.all_gather(norm_gain, "dp", axis=1, tiled=True),
        lax.all_gather(norm_bias, "dp", axis=1, tiled=True),
    )
    gain_rows = gain_rows.astype(jnp.float32)
    bias_rows = bias_rows.astype(jnp.float32)
    group_size = lax.axis_size("dp")
    group_rank = lax.axis_index("dp")
    model_rank = lax.axis_index("mp")
    local_rows = hidden_in.shape[1]
    slots = local_rows * lax.axis_size("mp")
    seq_total = slots * group_size
    head_dim = HEAD_DIM
    score_scale = head_dim ** (-0.5)
    span = min(group_size, 8)
    block_keys = slots * span
    key_blocks = group_size // span
    own_first = group_rank * slots
    positions = (own_first + jnp.arange(slots, dtype=jnp.int32)).astype(jnp.float32)
    cosine, sine_table = rope_tables(positions, head_dim // 2)
    acc_qkv = jnp.zeros(query_key_value_matrix.shape, jnp.float32)
    acc_out = jnp.zeros(output_matrix.shape, jnp.float32)
    acc_gate_up = jnp.zeros(gate_up_matrix.shape, jnp.float32)
    acc_down = jnp.zeros(down_matrix.shape, jnp.float32)
    acc_gain = jnp.zeros(gain_rows.shape, jnp.float32)
    acc_bias = jnp.zeros(bias_rows.shape, jnp.float32)
    layer_rows = []
    input_rows = []
    for micro_step in range(hidden_in.shape[0]):
        x_rows, grad_rows = (
            lax.all_gather(hidden_in[micro_step], "mp", axis=0, tiled=True),
            lax.all_gather(cotangent[micro_step], "mp", axis=0, tiled=True),
        )
        seq_lengths = lengths[micro_step]

        def allowed_keys(first_row, row_count):
            key_pos = first_row + jnp.arange(row_count, dtype=jnp.int32)
            return (key_pos[None, :] < seq_lengths[:, None])[:, None, None, :]

        projected_rows = jnp.einsum(
            "rsd,cde->rsce", x_rows, query_key_value_matrix, preferred_element_type=jnp.float32
        )
        q_heads = rotate(split_heads(projected_rows[:, :, 0], head_dim), cosine, sine_table).astype(
            jnp.bfloat16
        )
        k_heads = rotate(split_heads(projected_rows[:, :, 1], head_dim), cosine, sine_table).astype(
            jnp.bfloat16
        )
        v_heads = split_heads(projected_rows[:, :, 2], head_dim).astype(jnp.bfloat16)
        head_shape = q_heads.shape
        buffer_shape = (head_shape[0], head_shape[1], seq_total, head_shape[3])
        forward_first_row = jnp.int32(0)
        run_max = jnp.full(head_shape[:3], masked_score, jnp.float32)
        key_part = lax.all_gather(k_heads, "dp", axis=2, tiled=True)
        value_part = lax.all_gather(v_heads, "dp", axis=2, tiled=True)
        forward_row_count = key_part.shape[2]
        forward_key_buffer = key_part
        forward_value_buffer = value_part
        old_max = run_max
        allowed = allowed_keys(forward_first_row, forward_row_count)
        scores = (
            jnp.einsum("shqd,shkd->shqk", q_heads, key_part, preferred_element_type=jnp.float32)
            * score_scale
        )
        scores = jnp.where(allowed, scores, masked_score)
        new_max = jnp.maximum(old_max, jnp.max(scores, axis=-1))
        weights_block = jnp.where(allowed, jnp.exp(scores - new_max[..., None]), 0.0)
        new_sum = jnp.sum(weights_block, axis=-1)
        new_acc = jnp.einsum(
            "shqk,shkd->shqd",
            weights_block.astype(jnp.bfloat16),
            value_part,
            preferred_element_type=jnp.float32,
        )
        run_max = new_max
        key_buffer = forward_key_buffer
        value_buffer = forward_value_buffer
        lse = run_max + jnp.log(new_sum)
        attended = new_acc / new_sum[..., None]
        attended_reduced = merge_heads(attended).astype(jnp.bfloat16)
        residual_branch = lax.psum(
            jnp.einsum(
                "rsf,fd->rsd", attended_reduced, output_matrix, preferred_element_type=jnp.float32
            ).astype(jnp.bfloat16),
            "mp",
        ).astype(jnp.float32)
        attention_normed, scaled_one, inv_std_one = normalize(
            x_rows.astype(jnp.float32) + residual_branch, gain_rows[0], bias_rows[0]
        )
        first_low = attention_normed.astype(jnp.bfloat16)
        gate_up_rows = jnp.einsum(
            "rsd,cdf->rscf", first_low, gate_up_matrix, preferred_element_type=jnp.float32
        )
        gate_part = gate_up_rows[:, :, 0]
        up_part = gate_up_rows[:, :, 1]
        sigmoid_gate = jax.nn.sigmoid(gate_part)
        silu_gate = gate_part * sigmoid_gate
        hidden_rows = (silu_gate * up_part).astype(jnp.bfloat16)
        feedforward_output = lax.psum(
            jnp.einsum(
                "rsf,fd->rsd", hidden_rows, down_matrix, preferred_element_type=jnp.float32
            ).astype(jnp.bfloat16),
            "mp",
        ).astype(jnp.float32)
        output, scaled_two, inv_std_two = normalize(
            attention_normed + feedforward_output, gain_rows[1], bias_rows[1]
        )
        layer_rows.append(
            lax.dynamic_slice_in_dim(output, model_rank * local_rows, local_rows, 0).astype(
                jnp.bfloat16
            )
        )
        d_z2, gain_two, bias_two = normalize_back(
            grad_rows.astype(jnp.float32), scaled_two, inv_std_two, gain_rows[1]
        )
        d_ffn = d_z2.astype(jnp.bfloat16)
        acc_down = acc_down + jnp.einsum(
            "rsf,rsd->fd", hidden_rows, d_ffn, preferred_element_type=jnp.float32
        )
        d_hidden = jnp.einsum("rsd,fd->rsf", d_ffn, down_matrix, preferred_element_type=jnp.float32)
        d_gate = d_hidden * up_part * sigmoid_gate * (1.0 + gate_part * (1.0 - sigmoid_gate))
        d_up = d_hidden * silu_gate
        d_gate_up = jnp.stack([d_gate, d_up], axis=2).astype(jnp.bfloat16)
        acc_gate_up = acc_gate_up + jnp.einsum(
            "rsd,rscf->cdf", first_low, d_gate_up, preferred_element_type=jnp.float32
        )
        d_first = (
            lax.psum(
                jnp.einsum(
                    "rscf,cdf->rsd", d_gate_up, gate_up_matrix, preferred_element_type=jnp.float32
                ).astype(jnp.bfloat16),
                "mp",
            ).astype(jnp.float32)
            + d_z2
        )
        d_z1, gain_one, bias_one = normalize_back(d_first, scaled_one, inv_std_one, gain_rows[0])
        acc_gain = acc_gain + jnp.stack([gain_one, gain_two])
        acc_bias = acc_bias + jnp.stack([bias_one, bias_two])
        d_branch = d_z1.astype(jnp.bfloat16)
        acc_out = acc_out + jnp.einsum(
            "rsf,rsd->fd", attended_reduced, d_branch, preferred_element_type=jnp.float32
        )
        d_attended = split_heads(
            jnp.einsum("rsd,fd->rsf", d_branch, output_matrix, preferred_element_type=jnp.float32),
            head_dim,
        ).astype(jnp.bfloat16)
        delta = jnp.sum(d_attended.astype(jnp.float32) * attended, axis=-1)
        zero_heads = jnp.zeros(head_shape, jnp.float32)

        def query_block(step_index, partial_sums):
            first_row = step_index * block_keys
            key_part = lax.dynamic_slice_in_dim(key_buffer, first_row, block_keys, 2)
            value_part = lax.dynamic_slice_in_dim(value_buffer, first_row, block_keys, 2)
            d_scores, prob_block = score_grads(
                q_heads,
                d_attended,
                lse,
                delta,
                key_part,
                value_part,
                allowed_keys(first_row, block_keys),
                score_scale,
            )
            d_query = partial_sums[0] + jnp.einsum(
                "shqk,shkd->shqd", d_scores, key_part, preferred_element_type=jnp.float32
            )
            key_total = lax.dynamic_update_slice_in_dim(
                partial_sums[1],
                jnp.einsum(
                    "shqk,shqd->shkd", d_scores, q_heads, preferred_element_type=jnp.float32
                ),
                first_row,
                2,
            )
            value_total = lax.dynamic_update_slice_in_dim(
                partial_sums[2],
                jnp.einsum(
                    "shqk,shqd->shkd", prob_block, d_attended, preferred_element_type=jnp.float32
                ),
                first_row,
                2,
            )
            return (d_query, key_total, value_total)

        zero_keys = jnp.zeros(buffer_shape, jnp.float32)
        d_query, key_total, value_total = lax.fori_loop(
            0, key_blocks, query_block, (zero_heads, zero_keys, zero_keys)
        )
        d_key, d_value = (
            lax.psum_scatter(key_total, "dp", scatter_dimension=2, tiled=True),
            lax.psum_scatter(value_total, "dp", scatter_dimension=2, tiled=True),
        )
        d_projected = jnp.stack(
            [
                merge_heads(rotate_back(d_query, cosine, sine_table)),
                merge_heads(rotate_back(d_key, cosine, sine_table)),
                merge_heads(d_value),
            ],
            axis=2,
        ).astype(jnp.bfloat16)
        acc_qkv = acc_qkv + jnp.einsum(
            "rsd,rsce->cde", x_rows, d_projected, preferred_element_type=jnp.float32
        )
        d_input = lax.psum_scatter(
            jnp.einsum(
                "rsce,cde->rsd",
                d_projected,
                query_key_value_matrix,
                preferred_element_type=jnp.float32,
            ).astype(jnp.bfloat16),
            "mp",
            scatter_dimension=0,
            tiled=True,
        ).astype(jnp.float32)
        input_rows.append(
            d_input + lax.dynamic_slice_in_dim(d_z1, model_rank * local_rows, local_rows, 0)
        )
    qkv_grad, out_grad, gate_up_grad, down_grad, gain_grad, bias_grad = (
        lax.psum_scatter(acc_qkv, "dp", scatter_dimension=1, tiled=True),
        lax.psum_scatter(acc_out, "dp", scatter_dimension=1, tiled=True),
        lax.psum_scatter(acc_gate_up, "dp", scatter_dimension=1, tiled=True),
        lax.psum_scatter(acc_down, "dp", scatter_dimension=1, tiled=True),
        lax.psum_scatter(acc_gain, "dp", scatter_dimension=1, tiled=True),
        lax.psum_scatter(acc_bias, "dp", scatter_dimension=1, tiled=True),
    )
    return (
        jnp.stack(layer_rows),
        jnp.stack(input_rows),
        qkv_grad,
        out_grad,
        gate_up_grad,
        down_grad,
        gain_grad,
        bias_grad,
    )


def solution(mesh):
    rows_of = dict(mesh.shape)
    by_plane = rows_of == {"dp": 8, "mp": 4}
    return jax.shard_map(
        plane_body if by_plane else body,
        mesh=mesh,
        in_specs=(
            P(None, ("dp", "mp"), None, None),
            P(None, ("dp", "mp"), None, None),
            P(),
            P(None, "dp", "mp"),
            P("mp", "dp"),
            P(None, "dp", "mp"),
            P("mp", "dp"),
            P(None, "dp"),
            P(None, "dp"),
        ),
        out_specs=(
            P(None, ("dp", "mp"), None, None),
            P(None, ("dp", "mp"), None, None),
            P(None, "dp", "mp"),
            P("mp", "dp"),
            P(None, "dp", "mp"),
            P("mp", "dp"),
            P(None, "dp"),
            P(None, "dp"),
        ),
        check_vma=False,
    )
```

```python
import functools

import jax
import jax.numpy as jnp
from jax import lax
from jax.experimental import pallas as pl
from jax.experimental.pallas import tpu as pltpu
from jax.sharding import PartitionSpec as P

HEAD_DIM = 64

norm_eps = 1e-12
rope_base = 1000.0
masked_score = -1e30

BF = jnp.bfloat16
F32 = jnp.float32
LANES = 128

CORE, XBIT, YBIT = 1, 2, 4
BOTH = XBIT | YBIT


def permute(value, dp_mask, mp_mask=0):
    mp = lax.axis_size("mp")
    count = lax.axis_size("dp") * mp
    pairs = [(i, i ^ (dp_mask((i // mp) & CORE) * mp + mp_mask)) for i in range(count)]
    return lax.ppermute(value, ("dp", "mp"), pairs)


def swap(value, dp_mask=0, mp_mask=0):
    return permute(value, lambda core: dp_mask, mp_mask)


def first_mask(core):
    return XBIT + core * (YBIT - XBIT)


def second_mask(core):
    return YBIT + core * (XBIT - YBIT)


def to_first(value):
    return permute(value, first_mask)


def to_second(value):
    return permute(value, second_mask)


def to_core(value):
    return swap(value, CORE)


def gathered_masks(core):
    first, second = first_mask(core), second_mask(core)
    return (0, first, second, BOTH, CORE, CORE ^ second, CORE ^ first, CORE ^ BOTH)


def kept_masks(core):
    first, second = first_mask(core), second_mask(core)
    return (0, second, first, BOTH), (CORE, CORE ^ first, CORE ^ second, CORE ^ BOTH)


SLOTS = (0, 2, 1, 3)


def add_low(a, b):
    return (a.astype(F32) + b.astype(F32)).astype(BF)


def add_wide(a, b):
    return a.astype(F32) + b.astype(F32)


def fence(*values):
    return lax.optimization_barrier(values)


class Scatter:
    def __init__(self, keep, send, stage=0):
        self.keep, self.go, self.stage = keep, send, stage

    def send(self):
        self.back = (to_core, to_first, to_second)[self.stage](self.go)

    def fold(self):
        back = self.back
        self.stage += 1
        if self.stage == 1:
            self.keep, self.go = add_low(self.keep[:2], back[:2]), add_low(self.keep[2:], back[2:])
        elif self.stage == 2:
            self.go = add_low(self.keep[1], back[1])
            self.keep = add_low(self.keep[0], back[0])

    def total(self):
        return add_low(self.keep, self.back)


class Hop:
    def __init__(self, value, dp_mask=0, mp_mask=0):
        self.go, self.masks = value, (dp_mask, mp_mask)

    def send(self):
        self.back = swap(self.go, *self.masks)

    def fold(self):
        self.got = self.back


class Sum(Hop):
    def fold(self):
        self.got = self.go + self.back


def tick(carry, waits, starts):
    arrived = fence(carry, [w.back for w in waits])
    for w, back in zip(waits, arrived[1]):
        w.back = back
        w.fold()
    starts = starts() if callable(starts) else starts
    ready = fence(arrived[0], [t.go for t in starts])
    for t, go in zip(starts, ready[1]):
        t.go = go
        t.send()
    return ready[0]


def params(limit=60 << 20):
    return pltpu.CompilerParams(vmem_limit_bytes=limit)


def cost(flops, size):
    del flops, size
    return pl.CostEstimate(flops=1, bytes_accessed=1, transcendentals=0)


ANY = pl.BlockSpec(memory_space=pl.ANY)
VM = pl.BlockSpec(memory_space=pltpu.VMEM)


def dot(a, b):
    return lax.dot_general(a, b, (((1,), (0,)), ((), ())), preferred_element_type=F32)


def dot_t(a, b):
    return lax.dot_general(a, b, (((1,), (1,)), ((), ())), preferred_element_type=F32)


def dot_rows(a, b):
    return lax.dot_general(a, b, (((0,), (0,)), ((), ())), preferred_element_type=F32)


def piece_copies(pieces, buffer, sems, plane):
    mine = lax.axis_index("dp")
    masks = gathered_masks(mine & CORE)
    copies = []
    for k, piece in enumerate(pieces):
        rows = buffer.shape[0] // len(pieces)
        start = pl.multiple_of((mine ^ masks[k]) * rows, rows)
        copies.append(
            pltpu.make_async_copy(
                piece.at[pl.ds(plane * rows, rows), :], buffer.at[pl.ds(start, rows), :], sems.at[k]
            )
        )
    return copies


def ffn_copies(pieces, plane, wide, narrow, sems):
    mine = lax.axis_index("dp")
    masks = gathered_masks(mine & CORE)
    inner = wide.shape[1]
    copies = []
    for k, piece in enumerate(pieces):
        for core in range(2):
            rows = piece.shape[2]
            start = pl.multiple_of((mine ^ masks[k] ^ core) * rows, rows)
            source = piece.at[plane, core]
            for i, (target, lanes) in enumerate(
                ((wide, slice(0, inner)), (narrow, slice(inner, piece.shape[3])))
            ):
                copies.append(
                    pltpu.make_async_copy(
                        source.at[:, lanes],
                        target.at[pl.ds(start, rows), :],
                        sems.at[i, 2 * k + core],
                    )
                )
    return copies


def out_copies(buffer, keep, send, sems, rows):
    mine = lax.axis_index("dp")
    copies = []
    for side, (target, masks) in enumerate(zip((keep, send), kept_masks(mine & CORE))):
        for i, mask in enumerate(masks):
            start = pl.multiple_of((mine ^ mask) * rows, rows)
            copies.append(
                pltpu.make_async_copy(
                    buffer.at[pl.ds(start, rows), :], target(i), sems.at[4 * side + i]
                )
            )
    return copies


def chip_copies(buffer, keep, sems, rows):
    mine = lax.axis_index("dp")
    copies = []
    for i, mask in enumerate(kept_masks(mine & CORE)[0]):
        for core in range(2):
            start = pl.multiple_of((mine ^ mask ^ core) * rows, rows)
            copies.append(
                pltpu.make_async_copy(
                    buffer.at[pl.ds(start, rows), :], keep(i, core), sems.at[2 * i + core]
                )
            )
    return copies


def start_all(copies):
    for copy in copies:
        copy.start()


def wait_all(copies):
    for copy in copies:
        copy.wait()


def partner(u):
    lane = lax.broadcasted_iota(jnp.int32, u.shape, 1)
    quarter = HEAD_DIM // 2
    return jnp.where(
        lane % HEAD_DIM < quarter,
        pltpu.roll(u, LANES - quarter, 1),
        pltpu.roll(u, quarter, 1),
    )


def low_lanes(shape):
    return lax.broadcasted_iota(jnp.int32, shape, 1) < HEAD_DIM


def kv_kernel(planes, x_ref, tab_ref, *refs):
    pieces, (kv_ref, w, sems) = refs[:8], refs[8:]
    copies = [piece_copies(pieces, w.at[p], sems.at[p], p) for p in range(planes)]
    for group in copies:
        start_all(group)
    x = x_ref[...]
    for p in range(planes):
        wait_all(copies[p])
        y = dot(x, w[p][:, : 3 * LANES])
        y0, y1, y2 = y[:, :LANES], y[:, LANES : 2 * LANES], y[:, 2 * LANES :]
        base = p * 3 * LANES
        kv_ref[:, base : base + LANES] = (y0 * tab_ref[0] + partner(y0) * tab_ref[1]).astype(BF)
        kv_ref[:, base + LANES : base + 2 * LANES] = (
            y1 * tab_ref[2] + partner(y1) * tab_ref[3]
        ).astype(BF)
        kv_ref[:, base + 2 * LANES : base + 3 * LANES] = y2.astype(BF)


def q_kernel(planes, scale, x_ref, tab_ref, *refs):
    pieces, (q_ref, w, sems) = refs[:8], refs[8:]
    copies = [piece_copies(pieces, w.at[p], sems.at[p], p) for p in range(planes)]
    for group in copies:
        start_all(group)
    x = x_ref[...]
    for p in range(planes):
        wait_all(copies[p])
        y = dot(x, w[p][:, 3 * LANES : 5 * LANES])
        y0, y1 = y[:, :LANES], y[:, LANES:]
        low = low_lanes(y1.shape)
        base = p * 2 * LANES
        q0 = y0 * tab_ref[0] + partner(y0) * tab_ref[1]
        q1 = jnp.where(low, y1 * tab_ref[2] + partner(y1) * tab_ref[3], 0.0)
        q_ref[:, base : base + LANES] = (q0 * scale).astype(BF)
        q_ref[:, base + LANES : base + 2 * LANES] = (q1 * scale).astype(BF)


def attend_kernel(q_ref, bias_ref, *refs):
    pieces = refs[:8]
    att_ref, low_ref, lse_ref, s_ref = refs[8:]
    rows = q_ref.shape[0]
    keys = rows

    def block(k, column):
        return pieces[k][:, column * LANES : (column + 1) * LANES]

    low = low_lanes((rows, LANES))
    lane = lax.broadcasted_iota(jnp.int32, (rows, LANES), 1)
    q0, q1 = q_ref[:, :LANES], q_ref[:, LANES:]
    zero = jnp.zeros_like(q0)
    heads = (
        (jnp.where(low, q0, zero), 0, 2),
        (jnp.where(low, zero, q0), 0, 2),
        (q1, 1, 1),
    )
    stats = jnp.zeros((rows, LANES), F32)
    results = []
    for h, (q, key_column, value_column) in enumerate(heads):
        peak = jnp.full((rows, LANES), -jnp.inf, F32)
        for k in range(8):
            s = dot_t(q, block(k, key_column)) + bias_ref[k : k + 1, :]
            s_ref[:, k * keys : (k + 1) * keys] = s
            for c in range(keys // LANES):
                peak = jnp.maximum(peak, s[:, c * LANES : (c + 1) * LANES])
        top = jnp.max(peak, axis=1, keepdims=True)
        total = jnp.zeros((rows, LANES), F32)
        acc = jnp.zeros((rows, LANES), F32)
        for k in range(8):
            e = jnp.exp(s_ref[:, k * keys : (k + 1) * keys] - top)
            for c in range(keys // LANES):
                total = total + e[:, c * LANES : (c + 1) * LANES]
            acc = acc + dot(e.astype(BF), block(k, value_column))
        total = jnp.sum(total, axis=1, keepdims=True)
        results.append(acc / total)
        stats = jnp.where(lane == h, top + jnp.log(total), stats)
    pair = jnp.where(low, results[0], results[1])
    single = jnp.where(low, 0.0, results[2])
    att_ref[:, :LANES] = single
    att_ref[:, LANES:] = pair
    low_ref[:, :LANES] = single.astype(BF)
    low_ref[:, LANES:] = pair.astype(BF)
    lse_ref[0] = stats.T[:8, :]


def attend_back_kernel(
    scale, q_ref, dat_ref, lse_ref, delta_ref, bias_ref, tab_ref, *refs
):
    pieces = refs[:8]
    keep_ref, send_ref, dq_ref = refs[8:]
    rows = q_ref.shape[0]

    def block(k, column):
        return pieces[k][:, column * LANES : (column + 1) * LANES]

    low = low_lanes((rows, LANES))
    q0, q1 = q_ref[:, :LANES], q_ref[:, LANES:]
    d0, d1 = dat_ref[:, LANES:], dat_ref[:, :LANES]
    zero = jnp.zeros_like(q0)
    heads = (
        (jnp.where(low, q0, zero), jnp.where(low, d0, zero), 0, 2),
        (jnp.where(low, zero, q0), jnp.where(low, zero, d0), 0, 2),
        (q1, d1, 1, 1),
    )
    dq = [jnp.zeros((LANES, rows), F32) for _ in heads]
    for k in range(8):
        side, index = divmod(k, 4)
        target = (keep_ref, send_ref)[side]
        slot = SLOTS[index]
        mask = bias_ref[:, k : k + 1]
        blocks = [block(k, c) for c in range(3)]
        keys_t = [blocks[0].T, blocks[1].T]
        parts = []
        for h, (q, d, key_column, value_column) in enumerate(heads):
            s = dot_t(blocks[key_column], q) + mask
            dp = dot_t(blocks[value_column], d)
            p = jnp.exp(s - lse_ref[0, h : h + 1, :])
            ds = (p * (dp - delta_ref[0, h : h + 1, :])).astype(BF)
            p = p.astype(BF)
            parts.append((dot(ds, q), dot(p, d)))
            dq[h] = dq[h] + dot(keys_t[key_column], ds)
        target[slot, :, :LANES] = (parts[0][0] + parts[1][0]).astype(BF)
        target[slot, :, LANES : 2 * LANES] = (parts[2][0] + parts[2][1]).astype(BF)
        target[slot, :, 2 * LANES :] = (parts[0][1] + parts[1][1]).astype(BF)
    row = lax.broadcasted_iota(jnp.int32, (LANES, rows), 0) < HEAD_DIM
    pair = jnp.where(row, dq[0], dq[1]).T * scale
    single = jnp.where(row, dq[2], 0.0).T * scale
    dq_ref[:, :LANES] = (pair * tab_ref[0] - partner(pair) * tab_ref[1]).astype(BF)
    dq_ref[:, LANES:] = (single * tab_ref[2] - partner(single) * tab_ref[3]).astype(BF)


def center_scale(rows):
    center = rows - jnp.mean(rows, axis=-1, keepdims=True)
    inv = lax.rsqrt(jnp.mean(center * center, axis=-1, keepdims=True) + norm_eps)
    return center * inv, inv


def norm_back(e, scaled, inv):
    return inv * (
        e
        - jnp.mean(e, axis=-1, keepdims=True)
        - scaled * jnp.mean(e * scaled, axis=-1, keepdims=True)
    )


def rows_sum(value):
    return jnp.sum(value, axis=0, keepdims=True)


def mix_kernel(planes, x_ref, att_ref, norm_ref, *refs):
    pieces = refs[:8]
    flow_ref, first_ref, scaled_ref, inv_ref, w, sems = refs[8:]
    copies = [piece_copies(pieces, w.at[p], sems.at[p], p) for p in range(planes)]
    for group in copies:
        start_all(group)
    total = x_ref[...].astype(F32)
    for p in range(planes):
        wait_all(copies[p])
        total = total + dot_t(
            att_ref[:, p * 2 * LANES : (p + 1) * 2 * LANES], w[p][:, 4 * LANES : 6 * LANES]
        )
    scaled, inv = center_scale(total)
    scaled_ref[...] = scaled
    inv_ref[...] = jnp.broadcast_to(inv, inv_ref.shape)
    first = scaled * norm_ref[0:1, :] + norm_ref[2:3, :]
    first_ref[...] = first
    flow_ref[...] = first.astype(BF)


def ffn_kernel(planes, own_ref, other_ref, *refs):
    wide = (refs[:4], refs[4:8])
    ffn_ref, send_ref, wgu, wd, flow, sems = refs[8:]
    half = planes // 2
    rows = own_ref.shape[0]
    copies = [
        ffn_copies(wide[p // half], p % half, wgu.at[p], wd.at[p], sems.at[p])
        for p in range(planes)
    ]
    for group in copies:
        start_all(group)
    flow[:rows, :] = own_ref[...]
    flow[rows:, :] = other_ref[...]
    total = jnp.zeros(flow.shape, F32)
    inner = wd.shape[2]
    for p in range(planes):
        wait_all(copies[p])
        both = dot(flow[...], wgu[p])
        gate, up = both[:, :inner], both[:, inner:]
        hidden = (gate * jax.nn.sigmoid(gate) * up).astype(BF)
        total = total + dot_t(hidden, wd[p])
    ffn_ref[...] = total[:rows]
    send_ref[...] = total[rows:].astype(BF)


def close_kernel(ffn_ref, back_ref, first_ref, cot_ref, norm_ref, out_ref, dz2_ref, dffn_ref, sums_ref):
    gain, bias = norm_ref[1:2, :], norm_ref[3:4, :]
    scaled, inv = center_scale(first_ref[...] + (ffn_ref[...] + back_ref[...].astype(F32)))
    out_ref[...] = (scaled * gain + bias).astype(BF)
    cot = cot_ref[...].astype(F32)
    dz2 = norm_back(cot * gain, scaled, inv)
    dz2_ref[...] = dz2
    dffn_ref[...] = dz2.astype(BF)
    sums_ref[...] = jnp.concatenate(
        [rows_sum(cot * scaled), rows_sum(cot), jnp.zeros((6, cot.shape[1]), F32)], axis=0
    )


def ffn_back_kernel(slab, *refs):
    acc_ref, refs = refs[0], refs[1:]
    flow_own, flow_other, dffn_own, dffn_other = refs[:4]
    pieces, refs = refs[4:8], refs[8:]
    dfirst_ref, send_ref, keep_ref, go_ref, wgu, wd, flow, dffn, both_ref, hidden, grads, sems, out_sems = refs
    rows = flow_own.shape[0]
    count = wgu.shape[0]
    inner = wgu.shape[2] // 2
    copies = []
    for p in range(count):
        group = ffn_copies(
            pieces, p, wgu.at[p], wd.at[:, p * inner : (p + 1) * inner], sems.at[p]
        )
        start_all(group)
        copies.extend(group)
    flow[:rows, :] = flow_own[...]
    flow[rows:, :] = flow_other[...]
    dffn[:rows, :] = dffn_own[...]
    dffn[rows:, :] = dffn_other[...]
    wait_all(copies)
    for p in range(count):
        both = dot(flow[...], wgu[p])
        both_ref[p] = both
        gate, up = both[:, :inner], both[:, inner:]
        hidden[:, p * inner : (p + 1) * inner] = (gate * jax.nn.sigmoid(gate) * up).astype(BF)
    down = dot(dffn[...].T, hidden[...])
    for p in range(count):
        grads[p, :, 2 * inner :] = down[:, p * inner : (p + 1) * inner].astype(BF)
    d_hidden = dot(dffn[...], wd[...])
    flow_t = flow[...].T
    total = acc_ref[...]
    outs = []
    for p in range(count):
        gate, up = both_ref[p][:, :inner], both_ref[p][:, inner:]
        d = d_hidden[:, p * inner : (p + 1) * inner]
        sig = jax.nn.sigmoid(gate)
        d_gate = (d * up * sig * (1.0 + gate * (1.0 - sig))).astype(BF)
        d_up = (d * (gate * sig)).astype(BF)
        both = jnp.concatenate([d_gate, d_up], axis=1)
        grads[p, :, : 2 * inner] = dot(flow_t, both).astype(BF)
        group = chip_copies(
            grads.at[p],
            lambda i, core: (keep_ref, go_ref)[i // 2].at[i % 2, p, core],
            out_sems.at[p],
            slab,
        )
        start_all(group)
        outs.extend(group)
        total = total + dot_t(both, wgu[p])
    dfirst_ref[...] = total
    send_ref[...] = total[rows:].astype(BF)
    wait_all(outs)


def branch_back_kernel(
    planes, dfirst_ref, back_ref, dz2_ref, scaled_ref, inv_ref, norm_ref, two_ref, att_ref, *refs
):
    pieces = refs[:8]
    dz1_ref, dat_ref, delta_ref, sums_ref, w, sems = refs[8:]
    copies = [piece_copies(pieces, w.at[p], sems.at[p], p) for p in range(planes)]
    for group in copies:
        start_all(group)
    dfirst = dfirst_ref[...] + back_ref[...].astype(F32) + dz2_ref[...]
    scaled = scaled_ref[...]
    two = two_ref[...]
    sums_ref[...] = jnp.concatenate(
        [
            rows_sum(dfirst * scaled),
            two[0:1],
            rows_sum(dfirst),
            two[1:2],
            jnp.zeros((4, dfirst.shape[1]), F32),
        ],
        axis=0,
    )
    dz1 = norm_back(dfirst * norm_ref[0:1, :], scaled, inv_ref[:, 0:1])
    dz1_ref[...] = dz1
    d_branch = dz1.astype(BF)
    low = low_lanes((dfirst.shape[0], LANES))
    lane = lax.broadcasted_iota(jnp.int32, (dfirst.shape[0], LANES), 1)
    for p in range(planes):
        wait_all(copies[p])
        d = dot(d_branch, w[p][:, 4 * LANES : 6 * LANES])
        single = jnp.where(low, 0.0, d[:, :LANES]).astype(BF)
        pair = d[:, LANES:].astype(BF)
        dat_ref[:, p * 2 * LANES : p * 2 * LANES + LANES] = single
        dat_ref[:, p * 2 * LANES + LANES : (p + 1) * 2 * LANES] = pair
        both = pair.astype(F32) * att_ref[:, p * 2 * LANES + LANES : (p + 1) * 2 * LANES]
        alone = single.astype(F32) * att_ref[:, p * 2 * LANES : p * 2 * LANES + LANES]
        zero = jnp.zeros_like(both)
        stats = zero
        for h, part in enumerate((jnp.where(low, both, zero), jnp.where(low, zero, both), alone)):
            stats = jnp.where(lane == h, jnp.sum(part, axis=1, keepdims=True), stats)
        delta_ref[p] = stats.T[:8, :]


def query_back_kernel(planes, slab, x_ref, low_dq_ref, high_dq_ref, dz1_ref, low_ref, *refs):
    pieces = refs[:8]
    din_ref, keep_ref, send_ref, w, grads, sems, out_sems = refs[8:]
    half = planes // 2
    copies = [piece_copies(pieces, w.at[p], sems.at[p], p) for p in range(planes)]
    for group in copies:
        start_all(group)
    x_t = x_ref[...].T
    total = dz1_ref[...]
    branch_t = total.astype(BF).T
    outs = []
    for p in range(planes):
        at = (p % half) * 2 * LANES
        d = (low_dq_ref, high_dq_ref)[p // half][:, at : at + 2 * LANES]
        query = dot(x_t, d)
        output = dot(branch_t, low_ref[:, p * 2 * LANES : (p + 1) * 2 * LANES])
        grads[p, :, :LANES] = query[:, :LANES].astype(BF)
        grads[p, :, LANES : 2 * LANES] = (query[:, LANES:] + output[:, :LANES]).astype(BF)
        grads[p, :, 2 * LANES :] = output[:, LANES:].astype(BF)
        group = out_copies(
            grads.at[p],
            lambda i: keep_ref.at[i, p],
            lambda i: send_ref.at[i, p],
            out_sems.at[p],
            slab,
        )
        start_all(group)
        outs.extend(group)
        wait_all(copies[p])
        total = total + dot_t(d, w[p][:, 3 * LANES : 5 * LANES])
    din_ref[...] = total
    wait_all(outs)


def kv_back_kernel(base, count, slab, x_ref, acc_ref, tab_ref, keep_d_ref, back_d_ref, *refs):
    pieces = refs[:8]
    din_ref, keep_ref, send_ref, w, grads, sems, out_sems = refs[8:]
    copies = [piece_copies(pieces, w.at[p], sems.at[p], base + p) for p in range(count)]
    for group in copies:
        start_all(group)
    x_t = x_ref[...].T
    total = acc_ref[...]
    outs = []
    for p in range(count):
        lanes = slice(p * 3 * LANES, (p + 1) * 3 * LANES)
        d = keep_d_ref[:, lanes].astype(F32) + back_d_ref[:, lanes].astype(F32)
        d0, d1, d2 = d[:, :LANES], d[:, LANES : 2 * LANES], d[:, 2 * LANES :]
        d = jnp.concatenate(
            [
                (d0 * tab_ref[0] - partner(d0) * tab_ref[1]).astype(BF),
                (d1 * tab_ref[2] - partner(d1) * tab_ref[3]).astype(BF),
                d2.astype(BF),
            ],
            axis=1,
        )
        grads[p] = dot(x_t, d).astype(BF)
        group = out_copies(
            grads.at[p],
            lambda i: keep_ref.at[i, p],
            lambda i: send_ref.at[i, p],
            out_sems.at[p],
            slab,
        )
        start_all(group)
        outs.extend(group)
        wait_all(copies[p])
        total = total + dot_t(d, w[p][:, : 3 * LANES])
    din_ref[...] = total.astype(din_ref.dtype)
    wait_all(outs)


def sds(shape, dtype):
    return jax.ShapeDtypeStruct(shape, dtype)


def plane_body(
    hidden_in,
    cotangent,
    lengths,
    qkv_weight,
    out_weight,
    gate_up_weight,
    down_weight,
    norm_gain,
    norm_bias,
):
    planes = lax.axis_size("mp")
    pair = planes // 2
    group = lax.axis_size("dp")
    dp, mp = lax.axis_index("dp"), lax.axis_index("mp")
    core = dp & CORE
    part = hidden_in.shape[1]
    width = hidden_in.shape[3]
    rows = part * planes
    slab = qkv_weight.shape[1]
    inner = gate_up_weight.shape[2] // 2
    scale = HEAD_DIM ** (-0.5)
    mine = mp ^ jnp.arange(planes, dtype=jnp.int32)
    others = range(1, planes)

    def blocks_of(array):
        array = array.reshape(array.shape[0], part, width)
        return [lax.dynamic_index_in_dim(array, mine[j], 0, keepdims=False) for j in range(planes)]

    q_w, k_w, v_w = qkv_weight[0], qkv_weight[1], qkv_weight[2]
    o_w, d_w = out_weight.T, down_weight.T
    two = 2 * HEAD_DIM
    own = jnp.concatenate(
        [k_w[:, :two], k_w[:, two:], v_w[:, two:], v_w[:, :two]]
        + [q_w[:, :two], q_w[:, two:], o_w[:, two:], o_w[:, :two]],
        axis=1,
    )
    x_blocks, cot_blocks = blocks_of(hidden_in), blocks_of(cotangent)

    def half_of(index):
        take = lambda w: lax.dynamic_slice_in_dim(w, index * inner, inner, 1)
        return jnp.concatenate([take(gate_up_weight[0]), take(gate_up_weight[1]), take(d_w)], axis=1)

    ffn_mine, ffn_give = half_of(core), half_of(1 - core)
    norm_own = jnp.concatenate([norm_gain, norm_bias, jnp.zeros((12, slab), BF)], axis=0)
    norm_rows = lax.dynamic_update_slice(jnp.zeros((16, width), BF), norm_own, (0, dp * slab))

    z = [swap(own, 0, j) for j in others]
    ffn_get = to_core(ffn_give)
    z, ffn_get, x_blocks = fence(z, ffn_get, x_blocks)
    w_four = jnp.concatenate([own] + z + [norm_rows], axis=0)
    ffn_own = jnp.stack([ffn_mine, ffn_get])
    w_first, w_second = to_first(w_four), to_second(w_four)
    x_got = swap(jnp.stack([x_blocks[1], x_blocks[3]]), 0, 1)
    f_one = swap(ffn_own, 0, 1)
    f_two = [swap(ffn_mine, 0, 2)]
    w_first, w_second, x_got, f_one, f_two, ffn_get, ffn_own, w_four = fence(
        w_first, w_second, x_got, f_one, f_two, ffn_get, ffn_own, w_four
    )
    w_diag = to_second(w_first)
    w_core = [to_core(w_four), to_core(w_first)]
    low = [jnp.stack([ffn_own, f_one])]
    low.append(to_first(low[0]))
    x_far = swap(jnp.stack([x_blocks[2], x_got[1]]), 0, 2)
    w_diag, w_core, w_second, x_far, ffn_get, f_one, low[0] = fence(
        w_diag, w_core, w_second, x_far, ffn_get, f_one, low[0]
    )
    x = jnp.concatenate([x_blocks[0], x_got[0], x_far[0], x_far[1]], axis=0)
    w_core += [to_core(w_second), to_core(w_diag)]
    f_two.append(swap(ffn_get, 0, 2))
    low.append(to_second(low[0]))
    weights = [w_four, w_first, w_second, w_diag] + w_core
    norms = sum(w[planes * slab : planes * slab + 8].astype(F32) for w in weights)

    within = (mine[:, None] * part + jnp.arange(part, dtype=jnp.int32)[None, :]).reshape(rows)
    positions = (dp * rows + within).astype(F32)
    half = HEAD_DIM // 2
    exponent = jnp.arange(half, dtype=F32) * (1.0 / half)
    angles = positions[:, None] * jnp.power(rope_base, -exponent)[None, :]
    cosine, sine = jnp.cos(angles), jnp.sin(angles)
    cos_head = jnp.concatenate([cosine, cosine], axis=1)
    sin_head = jnp.concatenate([-sine, sine], axis=1)
    one, none = jnp.ones_like(cos_head), jnp.zeros_like(cos_head)
    cat = lambda a, b: jnp.concatenate([a, b], axis=1)
    tables = jnp.stack(
        [cat(cos_head, cos_head), cat(sin_head, sin_head), cat(cos_head, one), cat(sin_head, none)]
    )
    length = lax.dynamic_index_in_dim(lengths.reshape(-1), mp, 0, keepdims=False)
    piece_base = (dp ^ jnp.stack([jnp.int32(0) + m for m in gathered_masks(core)])) * rows
    key_pos = piece_base[:, None] + within[None, :]
    bias = jnp.where(key_pos < length, 0.0, masked_score).astype(F32)
    bias_t = bias.T

    dma = pltpu.SemaphoreType.DMA
    w_scratch = [pltpu.VMEM((planes, width, 6 * LANES), BF), dma((planes, 8))]

    def project(kernel, columns, name):
        return pl.pallas_call(
            kernel,
            out_shape=sds((rows, planes * columns), BF),
            in_specs=[VM, VM] + [ANY] * 8,
            out_specs=VM,
            scratch_shapes=w_scratch,
            compiler_params=params(),
            cost_estimate=cost(1, 1),
            name=name,
        )(x, tables, *weights)

    kv = project(functools.partial(kv_kernel, planes), 3 * LANES, "kv_project")
    kv, low, f_one, f_two, bias, bias_t = fence(kv, low, f_one, f_two, bias, bias_t)
    keys = [kv, to_first(kv), to_second(kv)]
    key_core = [to_core(kv)]
    low.append(to_second(low[1]))
    f_three = swap(f_one, 0, 2)
    q = project(functools.partial(q_kernel, planes, scale), 2 * LANES, "q_project")
    q, key_core, keys[1], keys[2], f_three, low[3] = fence(
        q, key_core, keys[1], keys[2], f_three, low[3]
    )
    keys.append(to_second(keys[1]))
    key_core += [to_core(keys[1]), to_core(keys[2])]
    high = [jnp.stack([jnp.stack(f_two), f_three])]
    keys[3], key_core, cot_blocks, high = fence(keys[3], key_core, cot_blocks, high)
    key_core.append(to_core(keys[3]))
    high += [to_first(high[0]), to_second(high[0])]
    cot_got = swap(jnp.stack([cot_blocks[1], cot_blocks[3]]), 0, 1)
    kv_all = keys + key_core

    at_spec = lambda base, columns: pl.BlockSpec((rows, columns), lambda i: (0, i + base))
    seq = rows * group
    att, att_low, lse = pl.pallas_call(
        attend_kernel,
        grid=(planes,),
        out_shape=(
            sds((rows, planes * 2 * LANES), F32),
            sds((rows, planes * 2 * LANES), BF),
            sds((planes, 8, rows), F32),
        ),
        in_specs=[at_spec(0, 2 * LANES), pl.BlockSpec((8, rows), lambda i: (0, 0))]
        + [at_spec(0, 3 * LANES)] * 8,
        out_specs=(
            at_spec(0, 2 * LANES),
            at_spec(0, 2 * LANES),
            pl.BlockSpec((1, 8, rows), lambda i: (i, 0, 0)),
        ),
        scratch_shapes=[pltpu.VMEM((rows, seq), F32)],
        compiler_params=params(),
        cost_estimate=cost(1, 1),
        name="attend",
    )(q, bias, *kv_all)
    act = lambda dtype: sds((rows, width), dtype)
    att_low, high[1], cot_got, cot_blocks = fence(att_low, high[1], cot_got, cot_blocks)
    high.append(to_second(high[1]))
    cot_far = swap(jnp.stack([cot_blocks[2], cot_got[1]]), 0, 2)
    flow, first, scaled, inv = pl.pallas_call(
        functools.partial(mix_kernel, planes),
        out_shape=(act(BF), act(F32), act(F32), sds((rows, LANES), F32)),
        in_specs=[VM] * 3 + [ANY] * 8,
        out_specs=(VM,) * 4,
        scratch_shapes=w_scratch,
        compiler_params=params(),
        cost_estimate=cost(1, 1),
        name="mix",
    )(x, att_low, norms, *weights)
    flow_other = to_core(flow)

    ffn, give = pl.pallas_call(
        functools.partial(ffn_kernel, planes),
        out_shape=(act(F32), act(BF)),
        in_specs=[VM] * 2 + [ANY] * 8,
        out_specs=(VM, VM),
        scratch_shapes=[
            pltpu.VMEM((planes, width, 2 * inner), BF),
            pltpu.VMEM((planes, width, inner), BF),
            pltpu.VMEM((2 * rows, width), BF),
            dma((planes, 2, 8)),
        ],
        compiler_params=params(),
        cost_estimate=cost(1, 1),
        name="ffn",
    )(flow, flow_other, *low, *high)
    ffn, cot_far = fence(ffn, cot_far)
    cot = jnp.concatenate([cot_blocks[0], cot_got[0], cot_far[0], cot_far[1]], axis=0)
    layer_out, dz2, dffn, sums_two = pl.pallas_call(
        close_kernel,
        out_shape=(act(BF), act(F32), act(BF), sds((8, width), F32)),
        in_specs=[VM] * 5,
        out_specs=(VM,) * 4,
        compiler_params=params(),
        cost_estimate=cost(1, 1),
        name="close",
    )(ffn, to_core(give), first, cot, norms)
    dffn_other = to_core(dffn)

    def ffn_back(pieces, acc):
        whole = lambda count: pl.BlockSpec((count * rows, width), lambda i: (0, 0))
        return pl.pallas_call(
            functools.partial(ffn_back_kernel, slab),
            grid=(1,),
            out_shape=(
                sds((2 * rows, width), F32),
                act(BF),
                sds((2, pair, 2, slab, 3 * inner), BF),
                sds((2, pair, 2, slab, 3 * inner), BF),
            ),
            in_specs=[whole(2)] + [whole(1)] * 4 + [ANY] * 4,
            out_specs=(whole(2), whole(1), ANY, ANY),
            scratch_shapes=[
                pltpu.VMEM((pair, width, 2 * inner), BF),
                pltpu.VMEM((width, pair * inner), BF),
                pltpu.VMEM((2 * rows, width), BF),
                pltpu.VMEM((2 * rows, width), BF),
                pltpu.VMEM((pair, 2 * rows, 2 * inner), F32),
                pltpu.VMEM((2 * rows, pair * inner), BF),
                pltpu.VMEM((pair, width, 3 * inner), BF),
                dma((pair, 2, 8)),
                dma((pair, 8)),
            ],
            compiler_params=params(),
            cost_estimate=cost(1, 1),
            name="ffn_back",
        )(acc, flow, flow_other, dffn, dffn_other, *pieces)

    def attend_back(base, q, dat):
        stat = pl.BlockSpec((1, 8, rows), lambda i: (i + base, 0, 0))
        keep_spec = pl.BlockSpec((4, rows, 3 * LANES), lambda i: (0, 0, i))
        return pl.pallas_call(
            functools.partial(attend_back_kernel, scale),
            grid=(pair,),
            out_shape=(
                sds((4, rows, pair * 3 * LANES), BF),
                sds((4, rows, pair * 3 * LANES), BF),
                sds((rows, pair * 2 * LANES), BF),
            ),
            in_specs=[
                at_spec(base, 2 * LANES),
                at_spec(base, 2 * LANES),
                stat,
                stat,
                pl.BlockSpec((rows, 8), lambda i: (0, 0)),
                pl.BlockSpec((4, rows, LANES), lambda i: (0, 0, 0)),
            ]
            + [at_spec(base, 3 * LANES)] * 8,
            out_specs=(keep_spec, keep_spec, at_spec(0, 2 * LANES)),
            compiler_params=params(),
            cost_estimate=cost(1, 1),
            name="attend_back",
        )(q, dat, lse, delta, bias_t, tables, *kv_all)

    out_blocks = [layer_out[j * part : (j + 1) * part] for j in range(planes)]
    near_out = Hop(jnp.stack([out_blocks[1], out_blocks[3]]), 0, 1)
    dfirst, _, keep, go = ffn_back(high, jnp.zeros((2 * rows, width), F32))
    high_sum = Scatter(keep, go, 1)
    dfirst = tick(dfirst, [], [high_sum, near_out])
    dfirst, give, keep, go = ffn_back(low, dfirst)
    low_sum = Scatter(keep, go, 1)
    give_hop = Hop(give, CORE)
    dfirst = tick(dfirst, [near_out], [give_hop, low_sum])
    dfirst = tick(dfirst, [give_hop], [])
    dz1, dat, delta, sums = pl.pallas_call(
        functools.partial(branch_back_kernel, planes),
        grid=(1,),
        out_shape=(
            act(F32),
            sds((rows, planes * 2 * LANES), BF),
            sds((planes, 8, rows), F32),
            sds((8, width), F32),
        ),
        in_specs=[pl.BlockSpec((rows, width), lambda i: (0, 0))] + [VM] * 7 + [ANY] * 8,
        out_specs=(VM,) * 4,
        scratch_shapes=w_scratch,
        compiler_params=params(),
        cost_estimate=cost(1, 1),
        name="branch_back",
    )(dfirst, give_hop.got, dz2, scaled, inv, norms, sums_two, att, *weights)

    stages = [Sum(sums, CORE)]

    def next_sum(dp_mask, mp_mask=0):
        stages.append(Sum(stages[-1].got, dp_mask, mp_mask))
        return stages[-1]

    far_out = Hop(jnp.stack([out_blocks[2], near_out.got[1]]), 0, 2)
    dat = tick(dat, [high_sum], [high_sum, stages[0], far_out])
    keep, send, high_dq = attend_back(pair, q, dat)
    high_keys = Scatter(keep, send)
    dat, high_dq = fence(dat, high_dq)
    dat = tick(
        dat, [stages[0], far_out, low_sum], lambda: [high_keys, low_sum, next_sum(XBIT)]
    )
    keep, send, low_dq = attend_back(0, q, dat)
    low_keys = Scatter(keep, send)
    low_dq = tick(low_dq, [high_keys, stages[1]], lambda: [high_keys, low_keys, next_sum(YBIT)])
    low_dq, high_sum.back, low_sum.back = fence(low_dq, high_sum.back, low_sum.back)
    high_total, low_total = high_sum.total(), low_sum.total()
    far = [Hop(high_total[k], 0, 2 + k) for k in range(2)]
    near = Hop(low_total[1], 0, 1)
    low_dq = tick(low_dq, [], [far[0], near])

    def grads_shape(count):
        return sds((4, count, slab, 3 * LANES), BF)

    din, keep, send = pl.pallas_call(
        functools.partial(query_back_kernel, planes, slab),
        out_shape=(act(F32), grads_shape(planes), grads_shape(planes)),
        in_specs=[VM] * 5 + [ANY] * 8,
        out_specs=(VM, ANY, ANY),
        scratch_shapes=[
            pltpu.VMEM((planes, width, 6 * LANES), BF),
            pltpu.VMEM((planes, width, 3 * LANES), BF),
            dma((planes, 8)),
            dma((planes, 8)),
        ],
        compiler_params=params(),
        cost_estimate=cost(1, 1),
        name="query_back",
    )(x, low_dq, high_dq, dz1, att_low, *weights)
    queries = Scatter(keep, send)
    din = tick(din, [high_keys], [high_keys])
    din = tick(din, [low_keys, stages[2], near], [queries])
    din, high_keys.back = fence(din, high_keys.back)
    din = tick(din, [], [low_keys])

    def kv_back(base, sum_, din, out_type):
        din, keep, send = pl.pallas_call(
            functools.partial(kv_back_kernel, base, pair, slab),
            out_shape=(act(out_type), grads_shape(pair), grads_shape(pair)),
            in_specs=[VM] * 5 + [ANY] * 8,
            out_specs=(VM, ANY, ANY),
            scratch_shapes=[
                pltpu.VMEM((pair, width, 6 * LANES), BF),
                pltpu.VMEM((pair, width, 3 * LANES), BF),
                dma((pair, 8)),
                dma((pair, 8)),
            ],
            compiler_params=params(),
            cost_estimate=cost(1, 1),
            name="kv_back",
        )(x, din, tables, sum_.keep, sum_.back, *weights)
        return din, Scatter(keep, send)

    din, high_w = kv_back(pair, high_keys, din, F32)
    din = tick(din, [low_keys], [low_keys, high_w])
    din = tick(din, [queries, far[0]], [far[1]])
    din = tick(din, [high_w], [])
    din, low_keys.back = fence(din, low_keys.back)
    din = tick(din, [], [queries, high_w])
    din, low_w = kv_back(0, low_keys, din, BF)
    din_blocks = [din[j * part : (j + 1) * part] for j in range(planes)]
    near_din = Hop(jnp.stack([din_blocks[1], din_blocks[3]]), 0, 1)
    carry = tick(din, [far[1]], [low_w, near_din])
    carry = tick(carry, [low_w, high_w, near_din], [low_w, high_w])
    far_din = Hop(jnp.stack([din_blocks[2], near_din.got[1]]), 0, 2)
    carry = tick(carry, [queries], [queries, far_din])
    ffn_sum = low_total[0].astype(F32) + near.got.astype(F32)
    ffn_sum = ffn_sum + far[0].got.astype(F32) + far[1].got.astype(F32)
    last_hop = Hop(ffn_sum[1].astype(BF), CORE)
    carry, high_w.back = fence(carry, high_w.back)
    v_high = high_w.total()
    v_hops = [Hop(v_high[k], 0, 2 + k) for k in range(2)]
    carry = tick(carry, [low_w, far_din], [low_w] + v_hops)
    norm_sums = lax.dynamic_slice_in_dim(stages[2].got, dp * slab, slab, 1)
    rider = jnp.pad(norm_sums.astype(BF), ((0, 8), (0, 3 * LANES - slab)))
    carry, queries.back = fence(carry, queries.back)
    q_total = jnp.concatenate(
        [queries.total(), jnp.broadcast_to(rider, (planes,) + rider.shape)], axis=1
    )
    q_hops = [Hop(q_total[j], 0, j) for j in others]
    carry = tick(carry, [], q_hops[:2])
    carry, low_w.back = fence(carry, low_w.back)
    v_low = low_w.total()
    v_near = Hop(v_low[1], 0, 1)
    carry = tick(carry, [q_hops[0]] + v_hops[:1], [v_near, q_hops[2], last_hop])
    carry = tick(carry, [v_near, last_hop] + v_hops[1:] + q_hops[1:], [])
    mine_sum, other_sum = ffn_sum[0], last_hop.got.astype(F32)
    even, odd = jnp.where(core == 0, mine_sum, other_sum), jnp.where(core == 0, other_sum, mine_sum)
    join = lambda k: cat(even[:, k * inner : (k + 1) * inner], odd[:, k * inner : (k + 1) * inner])
    gate_up_grad = jnp.stack([join(0), join(1)])
    down_grad = join(2).T
    wide = lambda values: sum(value.astype(F32) for value in values)
    q_all = wide([q_total[0]] + [hop.got for hop in q_hops])
    qo_grad, sums = q_all[:slab], q_all[slab:, :slab]
    kv_grad = wide([v_low[0]] + [hop.got for hop in [v_near] + v_hops])

    def in_order(own, near_hop, far_hop):
        got = jnp.stack([own, near_hop.got[0], far_hop.got[0], far_hop.got[1]])
        return jnp.stack(
            [lax.dynamic_index_in_dim(got, mine[m], 0, keepdims=False) for m in range(planes)]
        )

    layer_rows = in_order(out_blocks[0], near_out, far_out)
    input_grad = in_order(din_blocks[0], near_din, far_din)
    shape = hidden_in.shape
    heads = 3 * HEAD_DIM
    qkv_grad = jnp.stack(
        [
            qo_grad[:, :heads],
            kv_grad[:, :heads],
            cat(kv_grad[:, 2 * LANES :], kv_grad[:, heads : 2 * LANES]),
        ]
    )
    out_grad = cat(qo_grad[:, 2 * LANES :], qo_grad[:, heads : 2 * LANES]).T
    return (
        layer_rows.reshape(shape),
        input_grad.reshape(shape).astype(F32),
        qkv_grad,
        out_grad,
        gate_up_grad,
        down_grad,
        sums[0:2],
        sums[2:4],
    )


def rope_tables(positions, half_dim):
    exponent = jnp.arange(half_dim, dtype=jnp.float32) * (1.0 / half_dim)
    inverse = jnp.power(rope_base, -exponent)
    angles = positions[:, None] * inverse[None, :]
    return (jnp.cos(angles), jnp.sin(angles))


def rotate(vectors, cosine, sine_table):
    half_dim = vectors.shape[-1] // 2
    first_half = vectors[..., :half_dim]
    second_half = vectors[..., half_dim:]
    return jnp.concatenate(
        [
            first_half * cosine - second_half * sine_table,
            second_half * cosine + first_half * sine_table,
        ],
        axis=-1,
    )


def rotate_back(gradient, cosine, sine_table):
    half_dim = gradient.shape[-1] // 2
    first_half = gradient[..., :half_dim]
    second_half = gradient[..., half_dim:]
    return jnp.concatenate(
        [
            first_half * cosine + second_half * sine_table,
            second_half * cosine - first_half * sine_table,
        ],
        axis=-1,
    )


def normalize(residual_stream, gain_row, bias_row):
    center = residual_stream - jnp.mean(residual_stream, axis=-1, keepdims=True)
    inv_std = lax.rsqrt(jnp.mean(center * center, axis=-1, keepdims=True) + norm_eps)
    scaled = center * inv_std
    return (scaled * gain_row + bias_row, scaled, inv_std)


def normalize_back(upstream, scaled, inv_std, gain_row):
    d_scaled = upstream * gain_row
    d_stream = inv_std * (
        d_scaled
        - jnp.mean(d_scaled, axis=-1, keepdims=True)
        - scaled * jnp.mean(d_scaled * scaled, axis=-1, keepdims=True)
    )
    return (d_stream, jnp.sum(upstream * scaled, axis=(0, 1)), jnp.sum(upstream, axis=(0, 1)))


def split_heads(rows, head_dim):
    return rows.reshape(
        rows.shape[0], rows.shape[1], rows.shape[2] // head_dim, head_dim
    ).transpose(1, 2, 0, 3)


def merge_heads(heads):
    return heads.transpose(2, 0, 1, 3).reshape(
        heads.shape[2], heads.shape[0], heads.shape[1] * heads.shape[3]
    )


def score_grads(
    query_part, grad_part, lse_part, delta_part, key_part, value_part, mask_part, score_scale
):
    scores = (
        jnp.einsum("shqd,shkd->shqk", query_part, key_part, preferred_element_type=jnp.float32)
        * score_scale
    )
    prob_full = jnp.where(mask_part, jnp.exp(scores - lse_part[..., None]), 0.0)
    d_probs = jnp.einsum(
        "shqd,shkd->shqk", grad_part, value_part, preferred_element_type=jnp.float32
    )
    d_scores = (prob_full * (d_probs - delta_part[..., None]) * score_scale).astype(jnp.bfloat16)
    return (d_scores, prob_full.astype(jnp.bfloat16))


def body(
    hidden_in,
    cotangent,
    lengths,
    qkv_weight,
    out_weight,
    gate_up_weight,
    down_weight,
    norm_gain,
    norm_bias,
):
    query_key_value_matrix, output_matrix, gate_up_matrix, down_matrix, gain_rows, bias_rows = (
        lax.all_gather(qkv_weight, "dp", axis=1, tiled=True),
        lax.all_gather(out_weight, "dp", axis=1, tiled=True),
        lax.all_gather(gate_up_weight, "dp", axis=1, tiled=True),
        lax.all_gather(down_weight, "dp", axis=1, tiled=True),
        lax.all_gather(norm_gain, "dp", axis=1, tiled=True),
        lax.all_gather(norm_bias, "dp", axis=1, tiled=True),
    )
    gain_rows = gain_rows.astype(jnp.float32)
    bias_rows = bias_rows.astype(jnp.float32)
    group_size = lax.axis_size("dp")
    group_rank = lax.axis_index("dp")
    model_rank = lax.axis_index("mp")
    local_rows = hidden_in.shape[1]
    slots = local_rows * lax.axis_size("mp")
    seq_total = slots * group_size
    head_dim = HEAD_DIM
    score_scale = head_dim ** (-0.5)
    span = min(group_size, 8)
    block_keys = slots * span
    key_blocks = group_size // span
    own_first = group_rank * slots
    positions = (own_first + jnp.arange(slots, dtype=jnp.int32)).astype(jnp.float32)
    cosine, sine_table = rope_tables(positions, head_dim // 2)
    acc_qkv = jnp.zeros(query_key_value_matrix.shape, jnp.float32)
    acc_out = jnp.zeros(output_matrix.shape, jnp.float32)
    acc_gate_up = jnp.zeros(gate_up_matrix.shape, jnp.float32)
    acc_down = jnp.zeros(down_matrix.shape, jnp.float32)
    acc_gain = jnp.zeros(gain_rows.shape, jnp.float32)
    acc_bias = jnp.zeros(bias_rows.shape, jnp.float32)
    layer_rows = []
    input_rows = []
    for micro_step in range(hidden_in.shape[0]):
        x_rows, grad_rows = (
            lax.all_gather(hidden_in[micro_step], "mp", axis=0, tiled=True),
            lax.all_gather(cotangent[micro_step], "mp", axis=0, tiled=True),
        )
        seq_lengths = lengths[micro_step]

        def allowed_keys(first_row, row_count):
            key_pos = first_row + jnp.arange(row_count, dtype=jnp.int32)
            return (key_pos[None, :] < seq_lengths[:, None])[:, None, None, :]

        projected_rows = jnp.einsum(
            "rsd,cde->rsce", x_rows, query_key_value_matrix, preferred_element_type=jnp.float32
        )
        q_heads = rotate(split_heads(projected_rows[:, :, 0], head_dim), cosine, sine_table).astype(
            jnp.bfloat16
        )
        k_heads = rotate(split_heads(projected_rows[:, :, 1], head_dim), cosine, sine_table).astype(
            jnp.bfloat16
        )
        v_heads = split_heads(projected_rows[:, :, 2], head_dim).astype(jnp.bfloat16)
        head_shape = q_heads.shape
        buffer_shape = (head_shape[0], head_shape[1], seq_total, head_shape[3])
        forward_first_row = jnp.int32(0)
        run_max = jnp.full(head_shape[:3], masked_score, jnp.float32)
        key_part = lax.all_gather(k_heads, "dp", axis=2, tiled=True)
        value_part = lax.all_gather(v_heads, "dp", axis=2, tiled=True)
        forward_row_count = key_part.shape[2]
        forward_key_buffer = key_part
        forward_value_buffer = value_part
        old_max = run_max
        allowed = allowed_keys(forward_first_row, forward_row_count)
        scores = (
            jnp.einsum("shqd,shkd->shqk", q_heads, key_part, preferred_element_type=jnp.float32)
            * score_scale
        )
        scores = jnp.where(allowed, scores, masked_score)
        new_max = jnp.maximum(old_max, jnp.max(scores, axis=-1))
        weights_block = jnp.where(allowed, jnp.exp(scores - new_max[..., None]), 0.0)
        new_sum = jnp.sum(weights_block, axis=-1)
        new_acc = jnp.einsum(
            "shqk,shkd->shqd",
            weights_block.astype(jnp.bfloat16),
            value_part,
            preferred_element_type=jnp.float32,
        )
        run_max = new_max
        key_buffer = forward_key_buffer
        value_buffer = forward_value_buffer
        lse = run_max + jnp.log(new_sum)
        attended = new_acc / new_sum[..., None]
        attended_reduced = merge_heads(attended).astype(jnp.bfloat16)
        residual_branch = lax.psum(
            jnp.einsum(
                "rsf,fd->rsd", attended_reduced, output_matrix, preferred_element_type=jnp.float32
            ).astype(jnp.bfloat16),
            "mp",
        ).astype(jnp.float32)
        attention_normed, scaled_one, inv_std_one = normalize(
            x_rows.astype(jnp.float32) + residual_branch, gain_rows[0], bias_rows[0]
        )
        first_low = attention_normed.astype(jnp.bfloat16)
        gate_up_rows = jnp.einsum(
            "rsd,cdf->rscf", first_low, gate_up_matrix, preferred_element_type=jnp.float32
        )
        gate_part = gate_up_rows[:, :, 0]
        up_part = gate_up_rows[:, :, 1]
        sigmoid_gate = jax.nn.sigmoid(gate_part)
        silu_gate = gate_part * sigmoid_gate
        hidden_rows = (silu_gate * up_part).astype(jnp.bfloat16)
        feedforward_output = lax.psum(
            jnp.einsum(
                "rsf,fd->rsd", hidden_rows, down_matrix, preferred_element_type=jnp.float32
            ).astype(jnp.bfloat16),
            "mp",
        ).astype(jnp.float32)
        output, scaled_two, inv_std_two = normalize(
            attention_normed + feedforward_output, gain_rows[1], bias_rows[1]
        )
        layer_rows.append(
            lax.dynamic_slice_in_dim(output, model_rank * local_rows, local_rows, 0).astype(
                jnp.bfloat16
            )
        )
        d_z2, gain_two, bias_two = normalize_back(
            grad_rows.astype(jnp.float32), scaled_two, inv_std_two, gain_rows[1]
        )
        d_ffn = d_z2.astype(jnp.bfloat16)
        acc_down = acc_down + jnp.einsum(
            "rsf,rsd->fd", hidden_rows, d_ffn, preferred_element_type=jnp.float32
        )
        d_hidden = jnp.einsum("rsd,fd->rsf", d_ffn, down_matrix, preferred_element_type=jnp.float32)
        d_gate = d_hidden * up_part * sigmoid_gate * (1.0 + gate_part * (1.0 - sigmoid_gate))
        d_up = d_hidden * silu_gate
        d_gate_up = jnp.stack([d_gate, d_up], axis=2).astype(jnp.bfloat16)
        acc_gate_up = acc_gate_up + jnp.einsum(
            "rsd,rscf->cdf", first_low, d_gate_up, preferred_element_type=jnp.float32
        )
        d_first = (
            lax.psum(
                jnp.einsum(
                    "rscf,cdf->rsd", d_gate_up, gate_up_matrix, preferred_element_type=jnp.float32
                ).astype(jnp.bfloat16),
                "mp",
            ).astype(jnp.float32)
            + d_z2
        )
        d_z1, gain_one, bias_one = normalize_back(d_first, scaled_one, inv_std_one, gain_rows[0])
        acc_gain = acc_gain + jnp.stack([gain_one, gain_two])
        acc_bias = acc_bias + jnp.stack([bias_one, bias_two])
        d_branch = d_z1.astype(jnp.bfloat16)
        acc_out = acc_out + jnp.einsum(
            "rsf,rsd->fd", attended_reduced, d_branch, preferred_element_type=jnp.float32
        )
        d_attended = split_heads(
            jnp.einsum("rsd,fd->rsf", d_branch, output_matrix, preferred_element_type=jnp.float32),
            head_dim,
        ).astype(jnp.bfloat16)
        delta = jnp.sum(d_attended.astype(jnp.float32) * attended, axis=-1)
        zero_heads = jnp.zeros(head_shape, jnp.float32)

        def query_block(step_index, partial_sums):
            first_row = step_index * block_keys
            key_part = lax.dynamic_slice_in_dim(key_buffer, first_row, block_keys, 2)
            value_part = lax.dynamic_slice_in_dim(value_buffer, first_row, block_keys, 2)
            d_scores, prob_block = score_grads(
                q_heads,
                d_attended,
                lse,
                delta,
                key_part,
                value_part,
                allowed_keys(first_row, block_keys),
                score_scale,
            )
            d_query = partial_sums[0] + jnp.einsum(
                "shqk,shkd->shqd", d_scores, key_part, preferred_element_type=jnp.float32
            )
            key_total = lax.dynamic_update_slice_in_dim(
                partial_sums[1],
                jnp.einsum(
                    "shqk,shqd->shkd", d_scores, q_heads, preferred_element_type=jnp.float32
                ),
                first_row,
                2,
            )
            value_total = lax.dynamic_update_slice_in_dim(
                partial_sums[2],
                jnp.einsum(
                    "shqk,shqd->shkd", prob_block, d_attended, preferred_element_type=jnp.float32
                ),
                first_row,
                2,
            )
            return (d_query, key_total, value_total)

        zero_keys = jnp.zeros(buffer_shape, jnp.float32)
        d_query, key_total, value_total = lax.fori_loop(
            0, key_blocks, query_block, (zero_heads, zero_keys, zero_keys)
        )
        d_key, d_value = (
            lax.psum_scatter(key_total, "dp", scatter_dimension=2, tiled=True),
            lax.psum_scatter(value_total, "dp", scatter_dimension=2, tiled=True),
        )
        d_projected = jnp.stack(
            [
                merge_heads(rotate_back(d_query, cosine, sine_table)),
                merge_heads(rotate_back(d_key, cosine, sine_table)),
                merge_heads(d_value),
            ],
            axis=2,
        ).astype(jnp.bfloat16)
        acc_qkv = acc_qkv + jnp.einsum(
            "rsd,rsce->cde", x_rows, d_projected, preferred_element_type=jnp.float32
        )
        d_input = lax.psum_scatter(
            jnp.einsum(
                "rsce,cde->rsd",
                d_projected,
                query_key_value_matrix,
                preferred_element_type=jnp.float32,
            ).astype(jnp.bfloat16),
            "mp",
            scatter_dimension=0,
            tiled=True,
        ).astype(jnp.float32)
        input_rows.append(
            d_input + lax.dynamic_slice_in_dim(d_z1, model_rank * local_rows, local_rows, 0)
        )
    qkv_grad, out_grad, gate_up_grad, down_grad, gain_grad, bias_grad = (
        lax.psum_scatter(acc_qkv, "dp", scatter_dimension=1, tiled=True),
        lax.psum_scatter(acc_out, "dp", scatter_dimension=1, tiled=True),
        lax.psum_scatter(acc_gate_up, "dp", scatter_dimension=1, tiled=True),
        lax.psum_scatter(acc_down, "dp", scatter_dimension=1, tiled=True),
        lax.psum_scatter(acc_gain, "dp", scatter_dimension=1, tiled=True),
        lax.psum_scatter(acc_bias, "dp", scatter_dimension=1, tiled=True),
    )
    return (
        jnp.stack(layer_rows),
        jnp.stack(input_rows),
        qkv_grad,
        out_grad,
        gate_up_grad,
        down_grad,
        gain_grad,
        bias_grad,
    )


def solution(mesh):
    rows_of = dict(mesh.shape)
    by_plane = rows_of == {"dp": 8, "mp": 4}
    return jax.shard_map(
        plane_body if by_plane else body,
        mesh=mesh,
        in_specs=(
            P(None, ("dp", "mp"), None, None),
            P(None, ("dp", "mp"), None, None),
            P(),
            P(None, "dp", "mp"),
            P("mp", "dp"),
            P(None, "dp", "mp"),
            P("mp", "dp"),
            P(None, "dp"),
            P(None, "dp"),
        ),
        out_specs=(
            P(None, ("dp", "mp"), None, None),
            P(None, ("dp", "mp"), None, None),
            P(None, "dp", "mp"),
            P("mp", "dp"),
            P(None, "dp", "mp"),
            P("mp", "dp"),
            P(None, "dp"),
            P(None, "dp"),
        ),
        check_vma=False,
    )
```

```python
import functools

import jax
import jax.numpy as jnp
from jax import lax
from jax.experimental import pallas as pl
from jax.experimental.pallas import tpu as pltpu
from jax.sharding import PartitionSpec as P

HEAD_DIM = 64

norm_eps = 1e-12
rope_base = 1000.0
masked_score = -1e30

BF = jnp.bfloat16
F32 = jnp.float32
LANES = 128

CORE, XBIT, YBIT = 1, 2, 4
BOTH = XBIT | YBIT


def permute(value, dp_mask, mp_mask=0):
    mp = lax.axis_size("mp")
    count = lax.axis_size("dp") * mp
    pairs = [(i, i ^ (dp_mask((i // mp) & CORE) * mp + mp_mask)) for i in range(count)]
    return lax.ppermute(value, ("dp", "mp"), pairs)


def swap(value, dp_mask=0, mp_mask=0):
    return permute(value, lambda core: dp_mask, mp_mask)


def first_mask(core):
    return XBIT + core * (YBIT - XBIT)


def second_mask(core):
    return YBIT + core * (XBIT - YBIT)


def to_first(value):
    return permute(value, first_mask)


def to_second(value):
    return permute(value, second_mask)


def to_core(value):
    return swap(value, CORE)


def gathered_masks(core):
    first, second = first_mask(core), second_mask(core)
    return (0, first, second, BOTH, CORE, CORE ^ second, CORE ^ first, CORE ^ BOTH)


def kept_masks(core):
    first, second = first_mask(core), second_mask(core)
    return (0, second, first, BOTH), (CORE, CORE ^ first, CORE ^ second, CORE ^ BOTH)


SLOTS = (0, 2, 1, 3)


def add_low(a, b):
    return (a.astype(F32) + b.astype(F32)).astype(BF)


def add_wide(a, b):
    return a.astype(F32) + b.astype(F32)


def fence(*values):
    return lax.optimization_barrier(values)


class Scatter:
    def __init__(self, keep, send, stage=0):
        self.keep, self.go, self.stage = keep, send, stage

    def send(self):
        self.back = (to_core, to_first, to_second)[self.stage](self.go)

    def fold(self):
        back = self.back
        self.stage += 1
        if self.stage == 1:
            self.keep, self.go = add_low(self.keep[:2], back[:2]), add_low(self.keep[2:], back[2:])
        elif self.stage == 2:
            self.go = add_low(self.keep[1], back[1])
            self.keep = add_low(self.keep[0], back[0])

    def total(self):
        return add_low(self.keep, self.back)


class Hop:
    def __init__(self, value, dp_mask=0, mp_mask=0):
        self.go, self.masks = value, (dp_mask, mp_mask)

    def send(self):
        self.back = swap(self.go, *self.masks)

    def fold(self):
        self.got = self.back


class Sum(Hop):
    def fold(self):
        self.got = self.go + self.back


def tick(carry, waits, starts):
    arrived = fence(carry, [w.back for w in waits])
    for w, back in zip(waits, arrived[1]):
        w.back = back
        w.fold()
    starts = starts() if callable(starts) else starts
    ready = fence(arrived[0], [t.go for t in starts])
    for t, go in zip(starts, ready[1]):
        t.go = go
        t.send()
    return ready[0]


def params(limit=60 << 20):
    return pltpu.CompilerParams(vmem_limit_bytes=limit)


def cost(flops, size):
    del flops, size
    return pl.CostEstimate(flops=1, bytes_accessed=1, transcendentals=0)


ANY = pl.BlockSpec(memory_space=pl.ANY)
VM = pl.BlockSpec(memory_space=pltpu.VMEM)


def dot(a, b):
    return lax.dot_general(a, b, (((1,), (0,)), ((), ())), preferred_element_type=F32)


def dot_t(a, b):
    return lax.dot_general(a, b, (((1,), (1,)), ((), ())), preferred_element_type=F32)


def dot_rows(a, b):
    return lax.dot_general(a, b, (((0,), (0,)), ((), ())), preferred_element_type=F32)


def piece_copies(pieces, buffer, sems, plane):
    mine = lax.axis_index("dp")
    masks = gathered_masks(mine & CORE)
    copies = []
    for k, piece in enumerate(pieces):
        rows = buffer.shape[0] // len(pieces)
        start = pl.multiple_of((mine ^ masks[k]) * rows, rows)
        copies.append(
            pltpu.make_async_copy(
                piece.at[pl.ds(plane * rows, rows), :], buffer.at[pl.ds(start, rows), :], sems.at[k]
            )
        )
    return copies


def ffn_copies(pieces, plane, wide, narrow, sems):
    mine = lax.axis_index("dp")
    masks = gathered_masks(mine & CORE)
    inner = wide.shape[1]
    copies = []
    for k, piece in enumerate(pieces):
        for core in range(2):
            rows = piece.shape[2]
            start = pl.multiple_of((mine ^ masks[k] ^ core) * rows, rows)
            source = piece.at[plane, core]
            for i, (target, lanes) in enumerate(
                ((wide, slice(0, inner)), (narrow, slice(inner, piece.shape[3])))
            ):
                copies.append(
                    pltpu.make_async_copy(
                        source.at[:, lanes],
                        target.at[pl.ds(start, rows), :],
                        sems.at[i, 2 * k + core],
                    )
                )
    return copies


def out_copies(buffer, keep, send, sems, rows):
    mine = lax.axis_index("dp")
    copies = []
    for side, (target, masks) in enumerate(zip((keep, send), kept_masks(mine & CORE))):
        for i, mask in enumerate(masks):
            start = pl.multiple_of((mine ^ mask) * rows, rows)
            copies.append(
                pltpu.make_async_copy(
                    buffer.at[pl.ds(start, rows), :], target(i), sems.at[4 * side + i]
                )
            )
    return copies


def chip_copies(buffer, keep, sems, rows):
    mine = lax.axis_index("dp")
    copies = []
    for i, mask in enumerate(kept_masks(mine & CORE)[0]):
        for core in range(2):
            start = pl.multiple_of((mine ^ mask ^ core) * rows, rows)
            copies.append(
                pltpu.make_async_copy(
                    buffer.at[pl.ds(start, rows), :], keep(i, core), sems.at[2 * i + core]
                )
            )
    return copies


def start_all(copies):
    for copy in copies:
        copy.start()


def wait_all(copies):
    for copy in copies:
        copy.wait()


def partner(u):
    lane = lax.broadcasted_iota(jnp.int32, u.shape, 1)
    quarter = HEAD_DIM // 2
    return jnp.where(
        lane % HEAD_DIM < quarter,
        pltpu.roll(u, LANES - quarter, 1),
        pltpu.roll(u, quarter, 1),
    )


def low_lanes(shape):
    return lax.broadcasted_iota(jnp.int32, shape, 1) < HEAD_DIM


def kv_kernel(planes, x_ref, tab_ref, *refs):
    pieces, (kv_ref, w, sems) = refs[:8], refs[8:]
    copies = [piece_copies(pieces, w.at[p], sems.at[p], p) for p in range(planes)]
    for group in copies:
        start_all(group)
    x = x_ref[...]
    for p in range(planes):
        wait_all(copies[p])
        y = dot(x, w[p][:, : 3 * LANES])
        y0, y1, y2 = y[:, :LANES], y[:, LANES : 2 * LANES], y[:, 2 * LANES :]
        base = p * 3 * LANES
        kv_ref[:, base : base + LANES] = (y0 * tab_ref[0] + partner(y0) * tab_ref[1]).astype(BF)
        kv_ref[:, base + LANES : base + 2 * LANES] = (
            y1 * tab_ref[2] + partner(y1) * tab_ref[3]
        ).astype(BF)
        kv_ref[:, base + 2 * LANES : base + 3 * LANES] = y2.astype(BF)


def q_kernel(planes, scale, x_ref, tab_ref, *refs):
    pieces, (q_ref, w, sems) = refs[:8], refs[8:]
    copies = [piece_copies(pieces, w.at[p], sems.at[p], p) for p in range(planes)]
    for group in copies:
        start_all(group)
    x = x_ref[...]
    for p in range(planes):
        wait_all(copies[p])
        y = dot(x, w[p][:, 3 * LANES : 5 * LANES])
        y0, y1 = y[:, :LANES], y[:, LANES:]
        low = low_lanes(y1.shape)
        base = p * 2 * LANES
        q0 = y0 * tab_ref[0] + partner(y0) * tab_ref[1]
        q1 = jnp.where(low, y1 * tab_ref[2] + partner(y1) * tab_ref[3], 0.0)
        q_ref[:, base : base + LANES] = (q0 * scale).astype(BF)
        q_ref[:, base + LANES : base + 2 * LANES] = (q1 * scale).astype(BF)


def attend_kernel(q_ref, bias_ref, *refs):
    pieces = refs[:8]
    att_ref, low_ref, lse_ref, s_ref = refs[8:]
    rows = q_ref.shape[0]
    keys = rows

    def block(k, column):
        return pieces[k][:, column * LANES : (column + 1) * LANES]

    low = low_lanes((rows, LANES))
    lane = lax.broadcasted_iota(jnp.int32, (rows, LANES), 1)
    q0, q1 = q_ref[:, :LANES], q_ref[:, LANES:]
    zero = jnp.zeros_like(q0)
    heads = (
        (jnp.where(low, q0, zero), 0, 2),
        (jnp.where(low, zero, q0), 0, 2),
        (q1, 1, 1),
    )
    stats = jnp.zeros((rows, LANES), F32)
    results = []
    for h, (q, key_column, value_column) in enumerate(heads):
        peak = jnp.full((rows, LANES), -jnp.inf, F32)
        for k in range(8):
            s = dot_t(q, block(k, key_column)) + bias_ref[k : k + 1, :]
            s_ref[:, k * keys : (k + 1) * keys] = s
            for c in range(keys // LANES):
                peak = jnp.maximum(peak, s[:, c * LANES : (c + 1) * LANES])
        top = jnp.max(peak, axis=1, keepdims=True)
        total = jnp.zeros((rows, LANES), F32)
        acc = jnp.zeros((rows, LANES), F32)
        for k in range(8):
            e = jnp.exp(s_ref[:, k * keys : (k + 1) * keys] - top)
            for c in range(keys // LANES):
                total = total + e[:, c * LANES : (c + 1) * LANES]
            acc = acc + dot(e.astype(BF), block(k, value_column))
        total = jnp.sum(total, axis=1, keepdims=True)
        results.append(acc / total)
        stats = jnp.where(lane == h, top + jnp.log(total), stats)
    pair = jnp.where(low, results[0], results[1])
    single = jnp.where(low, 0.0, results[2])
    att_ref[:, :LANES] = single
    att_ref[:, LANES:] = pair
    low_ref[:, :LANES] = single.astype(BF)
    low_ref[:, LANES:] = pair.astype(BF)
    lse_ref[0] = stats.T[:8, :]


def attend_back_kernel(
    scale, q_ref, dat_ref, lse_ref, delta_ref, bias_ref, tab_ref, *refs
):
    pieces = refs[:8]
    keep_ref, send_ref, dq_ref = refs[8:]
    rows = q_ref.shape[0]

    def block(k, column):
        return pieces[k][:, column * LANES : (column + 1) * LANES]

    low = low_lanes((rows, LANES))
    q0, q1 = q_ref[:, :LANES], q_ref[:, LANES:]
    d0, d1 = dat_ref[:, LANES:], dat_ref[:, :LANES]
    zero = jnp.zeros_like(q0)
    heads = (
        (jnp.where(low, q0, zero), jnp.where(low, d0, zero), 0, 2),
        (jnp.where(low, zero, q0), jnp.where(low, zero, d0), 0, 2),
        (q1, d1, 1, 1),
    )
    dq = [jnp.zeros((LANES, rows), F32) for _ in heads]
    for k in range(8):
        side, index = divmod(k, 4)
        target = (keep_ref, send_ref)[side]
        slot = SLOTS[index]
        mask = bias_ref[:, k : k + 1]
        blocks = [block(k, c) for c in range(3)]
        keys_t = [blocks[0].T, blocks[1].T]
        parts = []
        for h, (q, d, key_column, value_column) in enumerate(heads):
            s = dot_t(blocks[key_column], q) + mask
            dp = dot_t(blocks[value_column], d)
            p = jnp.exp(s - lse_ref[0, h : h + 1, :])
            ds = (p * (dp - delta_ref[0, h : h + 1, :])).astype(BF)
            p = p.astype(BF)
            parts.append((dot(ds, q), dot(p, d)))
            dq[h] = dq[h] + dot(keys_t[key_column], ds)
        target[slot, :, :LANES] = (parts[0][0] + parts[1][0]).astype(BF)
        target[slot, :, LANES : 2 * LANES] = (parts[2][0] + parts[2][1]).astype(BF)
        target[slot, :, 2 * LANES :] = (parts[0][1] + parts[1][1]).astype(BF)
    row = lax.broadcasted_iota(jnp.int32, (LANES, rows), 0) < HEAD_DIM
    pair = jnp.where(row, dq[0], dq[1]).T * scale
    single = jnp.where(row, dq[2], 0.0).T * scale
    dq_ref[:, :LANES] = (pair * tab_ref[0] - partner(pair) * tab_ref[1]).astype(BF)
    dq_ref[:, LANES:] = (single * tab_ref[2] - partner(single) * tab_ref[3]).astype(BF)


def center_scale(rows):
    center = rows - jnp.mean(rows, axis=-1, keepdims=True)
    inv = lax.rsqrt(jnp.mean(center * center, axis=-1, keepdims=True) + norm_eps)
    return center * inv, inv


def norm_back(e, scaled, inv):
    return inv * (
        e
        - jnp.mean(e, axis=-1, keepdims=True)
        - scaled * jnp.mean(e * scaled, axis=-1, keepdims=True)
    )


def rows_sum(value):
    return jnp.sum(value, axis=0, keepdims=True)


def mix_kernel(planes, x_ref, att_ref, norm_ref, *refs):
    pieces = refs[:8]
    flow_ref, first_ref, scaled_ref, inv_ref, w, sems = refs[8:]
    copies = [piece_copies(pieces, w.at[p], sems.at[p], p) for p in range(planes)]
    for group in copies:
        start_all(group)
    total = x_ref[...].astype(F32)
    for p in range(planes):
        wait_all(copies[p])
        total = total + dot_t(
            att_ref[:, p * 2 * LANES : (p + 1) * 2 * LANES], w[p][:, 4 * LANES : 6 * LANES]
        )
    scaled, inv = center_scale(total)
    scaled_ref[...] = scaled
    inv_ref[...] = jnp.broadcast_to(inv, inv_ref.shape)
    first = scaled * norm_ref[0:1, :] + norm_ref[2:3, :]
    first_ref[...] = first
    flow_ref[...] = first.astype(BF)


def ffn_kernel(planes, own_ref, other_ref, *refs):
    wide = (refs[:4], refs[4:8])
    ffn_ref, send_ref, wgu, wd, flow, sems = refs[8:]
    half = planes // 2
    rows = own_ref.shape[0]
    copies = [
        ffn_copies(wide[p // half], p % half, wgu.at[p], wd.at[p], sems.at[p])
        for p in range(planes)
    ]
    for group in copies:
        start_all(group)
    flow[:rows, :] = own_ref[...]
    flow[rows:, :] = other_ref[...]
    total = jnp.zeros(flow.shape, F32)
    inner = wd.shape[2]
    for p in range(planes):
        wait_all(copies[p])
        both = dot(flow[...], wgu[p])
        gate, up = both[:, :inner], both[:, inner:]
        hidden = (gate * jax.nn.sigmoid(gate) * up).astype(BF)
        total = total + dot_t(hidden, wd[p])
    ffn_ref[...] = total[:rows]
    send_ref[...] = total[rows:].astype(BF)


def close_kernel(ffn_ref, back_ref, first_ref, cot_ref, norm_ref, out_ref, dz2_ref, dffn_ref, sums_ref):
    gain, bias = norm_ref[1:2, :], norm_ref[3:4, :]
    scaled, inv = center_scale(first_ref[...] + (ffn_ref[...] + back_ref[...].astype(F32)))
    out_ref[...] = (scaled * gain + bias).astype(BF)
    cot = cot_ref[...].astype(F32)
    dz2 = norm_back(cot * gain, scaled, inv)
    dz2_ref[...] = dz2
    dffn_ref[...] = dz2.astype(BF)
    sums_ref[...] = jnp.concatenate(
        [rows_sum(cot * scaled), rows_sum(cot), jnp.zeros((6, cot.shape[1]), F32)], axis=0
    )


def ffn_back_kernel(slab, *refs):
    acc_ref, refs = refs[0], refs[1:]
    flow_own, flow_other, dffn_own, dffn_other = refs[:4]
    pieces, refs = refs[4:8], refs[8:]
    dfirst_ref, send_ref, keep_ref, go_ref, wgu, wd, flow, dffn, both_ref, hidden, grads, sems, out_sems = refs
    rows = flow_own.shape[0]
    count = wgu.shape[0]
    inner = wgu.shape[2] // 2
    copies = []
    for p in range(count):
        group = ffn_copies(
            pieces, p, wgu.at[p], wd.at[:, p * inner : (p + 1) * inner], sems.at[p]
        )
        start_all(group)
        copies.extend(group)
    flow[:rows, :] = flow_own[...]
    flow[rows:, :] = flow_other[...]
    dffn[:rows, :] = dffn_own[...]
    dffn[rows:, :] = dffn_other[...]
    wait_all(copies)
    for p in range(count):
        both = dot(flow[...], wgu[p])
        both_ref[p] = both
        gate, up = both[:, :inner], both[:, inner:]
        hidden[:, p * inner : (p + 1) * inner] = (gate * jax.nn.sigmoid(gate) * up).astype(BF)
    down = dot(dffn[...].T, hidden[...])
    for p in range(count):
        grads[p, :, 2 * inner :] = down[:, p * inner : (p + 1) * inner].astype(BF)
    d_hidden = dot(dffn[...], wd[...])
    flow_t = flow[...].T
    total = acc_ref[...]
    outs = []
    for p in range(count):
        gate, up = both_ref[p][:, :inner], both_ref[p][:, inner:]
        d = d_hidden[:, p * inner : (p + 1) * inner]
        sig = jax.nn.sigmoid(gate)
        d_gate = (d * up * sig * (1.0 + gate * (1.0 - sig))).astype(BF)
        d_up = (d * (gate * sig)).astype(BF)
        both = jnp.concatenate([d_gate, d_up], axis=1)
        grads[p, :, : 2 * inner] = dot(flow_t, both).astype(BF)
        group = chip_copies(
            grads.at[p],
            lambda i, core: (keep_ref, go_ref)[i // 2].at[i % 2, p, core],
            out_sems.at[p],
            slab,
        )
        start_all(group)
        outs.extend(group)
        total = total + dot_t(both, wgu[p])
    dfirst_ref[...] = total
    send_ref[...] = total[rows:].astype(BF)
    wait_all(outs)


def branch_back_kernel(
    planes, dfirst_ref, back_ref, dz2_ref, scaled_ref, inv_ref, norm_ref, two_ref, att_ref, *refs
):
    pieces = refs[:8]
    dz1_ref, dat_ref, delta_ref, sums_ref, w, sems = refs[8:]
    copies = [piece_copies(pieces, w.at[p], sems.at[p], p) for p in range(planes)]
    for group in copies:
        start_all(group)
    dfirst = dfirst_ref[...] + back_ref[...].astype(F32) + dz2_ref[...]
    scaled = scaled_ref[...]
    two = two_ref[...]
    sums_ref[...] = jnp.concatenate(
        [
            rows_sum(dfirst * scaled),
            two[0:1],
            rows_sum(dfirst),
            two[1:2],
            jnp.zeros((4, dfirst.shape[1]), F32),
        ],
        axis=0,
    )
    dz1 = norm_back(dfirst * norm_ref[0:1, :], scaled, inv_ref[:, 0:1])
    dz1_ref[...] = dz1
    d_branch = dz1.astype(BF)
    low = low_lanes((dfirst.shape[0], LANES))
    lane = lax.broadcasted_iota(jnp.int32, (dfirst.shape[0], LANES), 1)
    for p in range(planes):
        wait_all(copies[p])
        d = dot(d_branch, w[p][:, 4 * LANES : 6 * LANES])
        single = jnp.where(low, 0.0, d[:, :LANES]).astype(BF)
        pair = d[:, LANES:].astype(BF)
        dat_ref[:, p * 2 * LANES : p * 2 * LANES + LANES] = single
        dat_ref[:, p * 2 * LANES + LANES : (p + 1) * 2 * LANES] = pair
        both = pair.astype(F32) * att_ref[:, p * 2 * LANES + LANES : (p + 1) * 2 * LANES]
        alone = single.astype(F32) * att_ref[:, p * 2 * LANES : p * 2 * LANES + LANES]
        zero = jnp.zeros_like(both)
        stats = zero
        for h, part in enumerate((jnp.where(low, both, zero), jnp.where(low, zero, both), alone)):
            stats = jnp.where(lane == h, jnp.sum(part, axis=1, keepdims=True), stats)
        delta_ref[p] = stats.T[:8, :]


def query_back_kernel(planes, slab, x_ref, low_dq_ref, high_dq_ref, dz1_ref, low_ref, *refs):
    pieces = refs[:8]
    din_ref, keep_ref, send_ref, w, grads, sems, out_sems = refs[8:]
    half = planes // 2
    copies = [piece_copies(pieces, w.at[p], sems.at[p], p) for p in range(planes)]
    for group in copies:
        start_all(group)
    x_t = x_ref[...].T
    total = dz1_ref[...]
    branch_t = total.astype(BF).T
    outs = []
    for p in range(planes):
        at = (p % half) * 2 * LANES
        d = (low_dq_ref, high_dq_ref)[p // half][:, at : at + 2 * LANES]
        query = dot(x_t, d)
        output = dot(branch_t, low_ref[:, p * 2 * LANES : (p + 1) * 2 * LANES])
        grads[p, :, :LANES] = query[:, :LANES].astype(BF)
        grads[p, :, LANES : 2 * LANES] = (query[:, LANES:] + output[:, :LANES]).astype(BF)
        grads[p, :, 2 * LANES :] = output[:, LANES:].astype(BF)
        group = out_copies(
            grads.at[p],
            lambda i: keep_ref.at[i, p],
            lambda i: send_ref.at[i, p],
            out_sems.at[p],
            slab,
        )
        start_all(group)
        outs.extend(group)
        wait_all(copies[p])
        total = total + dot_t(d, w[p][:, 3 * LANES : 5 * LANES])
    din_ref[...] = total
    wait_all(outs)


def kv_back_kernel(base, count, slab, x_ref, acc_ref, tab_ref, keep_d_ref, back_d_ref, *refs):
    pieces = refs[:8]
    din_ref, keep_ref, send_ref, w, grads, sems, out_sems = refs[8:]
    copies = [piece_copies(pieces, w.at[p], sems.at[p], base + p) for p in range(count)]
    for group in copies:
        start_all(group)
    x_t = x_ref[...].T
    total = acc_ref[...]
    outs = []
    for p in range(count):
        lanes = slice(p * 3 * LANES, (p + 1) * 3 * LANES)
        d = keep_d_ref[:, lanes].astype(F32) + back_d_ref[:, lanes].astype(F32)
        d0, d1, d2 = d[:, :LANES], d[:, LANES : 2 * LANES], d[:, 2 * LANES :]
        d = jnp.concatenate(
            [
                (d0 * tab_ref[0] - partner(d0) * tab_ref[1]).astype(BF),
                (d1 * tab_ref[2] - partner(d1) * tab_ref[3]).astype(BF),
                d2.astype(BF),
            ],
            axis=1,
        )
        grads[p] = dot(x_t, d).astype(BF)
        group = out_copies(
            grads.at[p],
            lambda i: keep_ref.at[i, p],
            lambda i: send_ref.at[i, p],
            out_sems.at[p],
            slab,
        )
        start_all(group)
        outs.extend(group)
        wait_all(copies[p])
        total = total + dot_t(d, w[p][:, : 3 * LANES])
    din_ref[...] = total.astype(din_ref.dtype)
    wait_all(outs)


def sds(shape, dtype):
    return jax.ShapeDtypeStruct(shape, dtype)


def plane_body(
    hidden_in,
    cotangent,
    lengths,
    qkv_weight,
    out_weight,
    gate_up_weight,
    down_weight,
    norm_gain,
    norm_bias,
):
    planes = lax.axis_size("mp")
    pair = planes // 2
    group = lax.axis_size("dp")
    dp, mp = lax.axis_index("dp"), lax.axis_index("mp")
    core = dp & CORE
    part = hidden_in.shape[1]
    width = hidden_in.shape[3]
    rows = part * planes
    slab = qkv_weight.shape[1]
    inner = gate_up_weight.shape[2] // 2
    scale = HEAD_DIM ** (-0.5)
    mine = mp ^ jnp.arange(planes, dtype=jnp.int32)
    others = range(1, planes)

    def blocks_of(array):
        array = array.reshape(array.shape[0], part, width)
        return [lax.dynamic_index_in_dim(array, mine[j], 0, keepdims=False) for j in range(planes)]

    q_w, k_w, v_w = qkv_weight[0], qkv_weight[1], qkv_weight[2]
    o_w, d_w = out_weight.T, down_weight.T
    two = 2 * HEAD_DIM
    own = jnp.concatenate(
        [k_w[:, :two], k_w[:, two:], v_w[:, two:], v_w[:, :two]]
        + [q_w[:, :two], q_w[:, two:], o_w[:, two:], o_w[:, :two]],
        axis=1,
    )
    x_blocks, cot_blocks = blocks_of(hidden_in), blocks_of(cotangent)

    def half_of(index):
        take = lambda w: lax.dynamic_slice_in_dim(w, index * inner, inner, 1)
        return jnp.concatenate([take(gate_up_weight[0]), take(gate_up_weight[1]), take(d_w)], axis=1)

    ffn_mine, ffn_give = half_of(core), half_of(1 - core)
    norm_own = jnp.concatenate([norm_gain, norm_bias, jnp.zeros((12, slab), BF)], axis=0)
    norm_rows = lax.dynamic_update_slice(jnp.zeros((16, width), BF), norm_own, (0, dp * slab))

    z = [swap(own, 0, j) for j in others]
    ffn_get = to_core(ffn_give)
    z, ffn_get, x_blocks = fence(z, ffn_get, x_blocks)
    w_four = jnp.concatenate([own] + z + [norm_rows], axis=0)
    ffn_own = jnp.stack([ffn_mine, ffn_get])
    w_first, w_second = to_first(w_four), to_second(w_four)
    x_got = swap(jnp.stack([x_blocks[1], x_blocks[3]]), 0, 1)
    f_one = swap(ffn_own, 0, 1)
    f_two = [swap(ffn_mine, 0, 2)]
    w_first, w_second, x_got, f_one, f_two, ffn_get, ffn_own, w_four = fence(
        w_first, w_second, x_got, f_one, f_two, ffn_get, ffn_own, w_four
    )
    w_diag = to_second(w_first)
    w_core = [to_core(w_four), to_core(w_first)]
    low = [jnp.stack([ffn_own, f_one])]
    low.append(to_first(low[0]))
    x_far = swap(jnp.stack([x_blocks[2], x_got[1]]), 0, 2)
    w_diag, w_core, w_second, x_far, ffn_get, f_one, low[0] = fence(
        w_diag, w_core, w_second, x_far, ffn_get, f_one, low[0]
    )
    x = jnp.concatenate([x_blocks[0], x_got[0], x_far[0], x_far[1]], axis=0)
    w_core += [to_core(w_second), to_core(w_diag)]
    f_two.append(swap(ffn_get, 0, 2))
    low.append(to_second(low[0]))
    weights = [w_four, w_first, w_second, w_diag] + w_core
    norms = sum(w[planes * slab : planes * slab + 8].astype(F32) for w in weights)

    within = (mine[:, None] * part + jnp.arange(part, dtype=jnp.int32)[None, :]).reshape(rows)
    positions = (dp * rows + within).astype(F32)
    half = HEAD_DIM // 2
    exponent = jnp.arange(half, dtype=F32) * (1.0 / half)
    angles = positions[:, None] * jnp.power(rope_base, -exponent)[None, :]
    cosine, sine = jnp.cos(angles), jnp.sin(angles)
    cos_head = jnp.concatenate([cosine, cosine], axis=1)
    sin_head = jnp.concatenate([-sine, sine], axis=1)
    one, none = jnp.ones_like(cos_head), jnp.zeros_like(cos_head)
    cat = lambda a, b: jnp.concatenate([a, b], axis=1)
    tables = jnp.stack(
        [cat(cos_head, cos_head), cat(sin_head, sin_head), cat(cos_head, one), cat(sin_head, none)]
    )
    length = lax.dynamic_index_in_dim(lengths.reshape(-1), mp, 0, keepdims=False)
    piece_base = (dp ^ jnp.stack([jnp.int32(0) + m for m in gathered_masks(core)])) * rows
    key_pos = piece_base[:, None] + within[None, :]
    bias = jnp.where(key_pos < length, 0.0, masked_score).astype(F32)
    bias_t = bias.T

    dma = pltpu.SemaphoreType.DMA
    w_scratch = [pltpu.VMEM((planes, width, 6 * LANES), BF), dma((planes, 8))]

    def project(kernel, columns, name):
        return pl.pallas_call(
            kernel,
            out_shape=sds((rows, planes * columns), BF),
            in_specs=[VM, VM] + [ANY] * 8,
            out_specs=VM,
            scratch_shapes=w_scratch,
            compiler_params=params(),
            cost_estimate=cost(1, 1),
            name=name,
        )(x, tables, *weights)

    kv = project(functools.partial(kv_kernel, planes), 3 * LANES, "kv_project")
    kv, low, f_one, f_two, bias, bias_t = fence(kv, low, f_one, f_two, bias, bias_t)
    keys = [kv, to_first(kv), to_second(kv)]
    key_core = [to_core(kv)]
    low.append(to_second(low[1]))
    f_three = swap(f_one, 0, 2)
    q = project(functools.partial(q_kernel, planes, scale), 2 * LANES, "q_project")
    q, key_core, keys[1], keys[2], f_three, low[3] = fence(
        q, key_core, keys[1], keys[2], f_three, low[3]
    )
    keys.append(to_second(keys[1]))
    key_core += [to_core(keys[1]), to_core(keys[2])]
    high = [jnp.stack([jnp.stack(f_two), f_three])]
    keys[3], key_core, cot_blocks, high = fence(keys[3], key_core, cot_blocks, high)
    key_core.append(to_core(keys[3]))
    high += [to_first(high[0]), to_second(high[0])]
    cot_got = swap(jnp.stack([cot_blocks[1], cot_blocks[3]]), 0, 1)
    kv_all = keys + key_core

    at_spec = lambda base, columns: pl.BlockSpec((rows, columns), lambda i: (0, i + base))
    seq = rows * group
    att, att_low, lse = pl.pallas_call(
        attend_kernel,
        grid=(planes,),
        out_shape=(
            sds((rows, planes * 2 * LANES), F32),
            sds((rows, planes * 2 * LANES), BF),
            sds((planes, 8, rows), F32),
        ),
        in_specs=[at_spec(0, 2 * LANES), pl.BlockSpec((8, rows), lambda i: (0, 0))]
        + [at_spec(0, 3 * LANES)] * 8,
        out_specs=(
            at_spec(0, 2 * LANES),
            at_spec(0, 2 * LANES),
            pl.BlockSpec((1, 8, rows), lambda i: (i, 0, 0)),
        ),
        scratch_shapes=[pltpu.VMEM((rows, seq), F32)],
        compiler_params=params(),
        cost_estimate=cost(1, 1),
        name="attend",
    )(q, bias, *kv_all)
    act = lambda dtype: sds((rows, width), dtype)
    att_low, high[1], cot_got, cot_blocks = fence(att_low, high[1], cot_got, cot_blocks)
    high.append(to_second(high[1]))
    cot_far = swap(jnp.stack([cot_blocks[2], cot_got[1]]), 0, 2)
    flow, first, scaled, inv = pl.pallas_call(
        functools.partial(mix_kernel, planes),
        out_shape=(act(BF), act(F32), act(F32), sds((rows, LANES), F32)),
        in_specs=[VM] * 3 + [ANY] * 8,
        out_specs=(VM,) * 4,
        scratch_shapes=w_scratch,
        compiler_params=params(),
        cost_estimate=cost(1, 1),
        name="mix",
    )(x, att_low, norms, *weights)
    flow_other = to_core(flow)

    ffn, give = pl.pallas_call(
        functools.partial(ffn_kernel, planes),
        out_shape=(act(F32), act(BF)),
        in_specs=[VM] * 2 + [ANY] * 8,
        out_specs=(VM, VM),
        scratch_shapes=[
            pltpu.VMEM((planes, width, 2 * inner), BF),
            pltpu.VMEM((planes, width, inner), BF),
            pltpu.VMEM((2 * rows, width), BF),
            dma((planes, 2, 8)),
        ],
        compiler_params=params(),
        cost_estimate=cost(1, 1),
        name="ffn",
    )(flow, flow_other, *low, *high)
    ffn, cot_far = fence(ffn, cot_far)
    cot = jnp.concatenate([cot_blocks[0], cot_got[0], cot_far[0], cot_far[1]], axis=0)
    layer_out, dz2, dffn, sums_two = pl.pallas_call(
        close_kernel,
        out_shape=(act(BF), act(F32), act(BF), sds((8, width), F32)),
        in_specs=[VM] * 5,
        out_specs=(VM,) * 4,
        compiler_params=params(),
        cost_estimate=cost(1, 1),
        name="close",
    )(ffn, to_core(give), first, cot, norms)
    dffn_other = to_core(dffn)

    def ffn_back(pieces, acc):
        whole = lambda count: pl.BlockSpec((count * rows, width), lambda i: (0, 0))
        return pl.pallas_call(
            functools.partial(ffn_back_kernel, slab),
            grid=(1,),
            out_shape=(
                sds((2 * rows, width), F32),
                act(BF),
                sds((2, pair, 2, slab, 3 * inner), BF),
                sds((2, pair, 2, slab, 3 * inner), BF),
            ),
            in_specs=[whole(2)] + [whole(1)] * 4 + [ANY] * 4,
            out_specs=(whole(2), whole(1), ANY, ANY),
            scratch_shapes=[
                pltpu.VMEM((pair, width, 2 * inner), BF),
                pltpu.VMEM((width, pair * inner), BF),
                pltpu.VMEM((2 * rows, width), BF),
                pltpu.VMEM((2 * rows, width), BF),
                pltpu.VMEM((pair, 2 * rows, 2 * inner), F32),
                pltpu.VMEM((2 * rows, pair * inner), BF),
                pltpu.VMEM((pair, width, 3 * inner), BF),
                dma((pair, 2, 8)),
                dma((pair, 8)),
            ],
            compiler_params=params(),
            cost_estimate=cost(1, 1),
            name="ffn_back",
        )(acc, flow, flow_other, dffn, dffn_other, *pieces)

    def attend_back(base, q, dat):
        stat = pl.BlockSpec((1, 8, rows), lambda i: (i + base, 0, 0))
        keep_spec = pl.BlockSpec((4, rows, 3 * LANES), lambda i: (0, 0, i))
        return pl.pallas_call(
            functools.partial(attend_back_kernel, scale),
            grid=(pair,),
            out_shape=(
                sds((4, rows, pair * 3 * LANES), BF),
                sds((4, rows, pair * 3 * LANES), BF),
                sds((rows, pair * 2 * LANES), BF),
            ),
            in_specs=[
                at_spec(base, 2 * LANES),
                at_spec(base, 2 * LANES),
                stat,
                stat,
                pl.BlockSpec((rows, 8), lambda i: (0, 0)),
                pl.BlockSpec((4, rows, LANES), lambda i: (0, 0, 0)),
            ]
            + [at_spec(base, 3 * LANES)] * 8,
            out_specs=(keep_spec, keep_spec, at_spec(0, 2 * LANES)),
            compiler_params=params(),
            cost_estimate=cost(1, 1),
            name="attend_back",
        )(q, dat, lse, delta, bias_t, tables, *kv_all)

    out_blocks = [layer_out[j * part : (j + 1) * part] for j in range(planes)]
    near_out = Hop(jnp.stack([out_blocks[1], out_blocks[3]]), 0, 1)
    dfirst, _, keep, go = ffn_back(high, jnp.zeros((2 * rows, width), F32))
    high_sum = Scatter(keep, go, 1)
    dfirst = tick(dfirst, [], [high_sum, near_out])
    dfirst, give, keep, go = ffn_back(low, dfirst)
    low_sum = Scatter(keep, go, 1)
    give_hop = Hop(give, CORE)
    dfirst = tick(dfirst, [near_out], [give_hop, low_sum])
    dfirst = tick(dfirst, [give_hop], [])
    dz1, dat, delta, sums = pl.pallas_call(
        functools.partial(branch_back_kernel, planes),
        grid=(1,),
        out_shape=(
            act(F32),
            sds((rows, planes * 2 * LANES), BF),
            sds((planes, 8, rows), F32),
            sds((8, width), F32),
        ),
        in_specs=[pl.BlockSpec((rows, width), lambda i: (0, 0))] + [VM] * 7 + [ANY] * 8,
        out_specs=(VM,) * 4,
        scratch_shapes=w_scratch,
        compiler_params=params(),
        cost_estimate=cost(1, 1),
        name="branch_back",
    )(dfirst, give_hop.got, dz2, scaled, inv, norms, sums_two, att, *weights)

    stages = [Sum(sums, CORE)]

    def next_sum(dp_mask, mp_mask=0):
        stages.append(Sum(stages[-1].got, dp_mask, mp_mask))
        return stages[-1]

    far_out = Hop(jnp.stack([out_blocks[2], near_out.got[1]]), 0, 2)
    dat = tick(dat, [high_sum], [high_sum, stages[0], far_out])
    keep, send, high_dq = attend_back(pair, q, dat)
    high_keys = Scatter(keep, send)
    dat, high_dq = fence(dat, high_dq)
    dat = tick(
        dat, [stages[0], far_out, low_sum], lambda: [high_keys, low_sum, next_sum(XBIT)]
    )
    keep, send, low_dq = attend_back(0, q, dat)
    low_keys = Scatter(keep, send)
    low_dq = tick(low_dq, [high_keys, stages[1]], lambda: [high_keys, low_keys, next_sum(YBIT)])
    low_dq, high_sum.back, low_sum.back = fence(low_dq, high_sum.back, low_sum.back)
    high_total, low_total = high_sum.total(), low_sum.total()
    far = [Hop(high_total[k], 0, 2 + k) for k in range(2)]
    near = Hop(low_total[1], 0, 1)
    low_dq = tick(low_dq, [], [far[0], near])

    def grads_shape(count):
        return sds((4, count, slab, 3 * LANES), BF)

    din, keep, send = pl.pallas_call(
        functools.partial(query_back_kernel, planes, slab),
        out_shape=(act(F32), grads_shape(planes), grads_shape(planes)),
        in_specs=[VM] * 5 + [ANY] * 8,
        out_specs=(VM, ANY, ANY),
        scratch_shapes=[
            pltpu.VMEM((planes, width, 6 * LANES), BF),
            pltpu.VMEM((planes, width, 3 * LANES), BF),
            dma((planes, 8)),
            dma((planes, 8)),
        ],
        compiler_params=params(),
        cost_estimate=cost(1, 1),
        name="query_back",
    )(x, low_dq, high_dq, dz1, att_low, *weights)
    queries = Scatter(keep, send)
    din = tick(din, [high_keys], [high_keys])
    din = tick(din, [low_keys], [])
    din = tick(din, [stages[2], near], [queries])
    din, high_keys.back = fence(din, high_keys.back)
    din = tick(din, [], [low_keys])

    def kv_back(base, sum_, din, out_type):
        din, keep, send = pl.pallas_call(
            functools.partial(kv_back_kernel, base, pair, slab),
            out_shape=(act(out_type), grads_shape(pair), grads_shape(pair)),
            in_specs=[VM] * 5 + [ANY] * 8,
            out_specs=(VM, ANY, ANY),
            scratch_shapes=[
                pltpu.VMEM((pair, width, 6 * LANES), BF),
                pltpu.VMEM((pair, width, 3 * LANES), BF),
                dma((pair, 8)),
                dma((pair, 8)),
            ],
            compiler_params=params(),
            cost_estimate=cost(1, 1),
            name="kv_back",
        )(x, din, tables, sum_.keep, sum_.back, *weights)
        return din, Scatter(keep, send)

    din, high_w = kv_back(pair, high_keys, din, F32)
    din = tick(din, [low_keys], [low_keys, high_w])
    din = tick(din, [queries, far[0]], [far[1]])
    din = tick(din, [high_w], [])
    din, low_keys.back = fence(din, low_keys.back)
    din = tick(din, [], [queries, high_w])
    din, low_w = kv_back(0, low_keys, din, BF)
    din_blocks = [din[j * part : (j + 1) * part] for j in range(planes)]
    near_din = Hop(jnp.stack([din_blocks[1], din_blocks[3]]), 0, 1)
    carry = tick(din, [far[1]], [low_w, near_din])
    far_din = None

    def more_din():
        nonlocal far_din
        far_din = Hop(jnp.stack([din_blocks[2], near_din.got[1]]), 0, 2)
        return far_din

    carry = tick(carry, [low_w, high_w, near_din], lambda: [low_w, high_w, more_din()])
    carry = tick(carry, [queries], [queries])
    ffn_sum = low_total[0].astype(F32) + near.got.astype(F32)
    ffn_sum = ffn_sum + far[0].got.astype(F32) + far[1].got.astype(F32)
    last_hop = Hop(ffn_sum[1].astype(BF), CORE)
    carry, high_w.back = fence(carry, high_w.back)
    v_high = high_w.total()
    v_hops = [Hop(v_high[k], 0, 2 + k) for k in range(2)]
    carry = tick(carry, [low_w, far_din], [low_w] + v_hops)
    norm_sums = lax.dynamic_slice_in_dim(stages[2].got, dp * slab, slab, 1)
    rider = jnp.pad(norm_sums.astype(BF), ((0, 8), (0, 3 * LANES - slab)))
    carry, queries.back = fence(carry, queries.back)
    q_total = jnp.concatenate(
        [queries.total(), jnp.broadcast_to(rider, (planes,) + rider.shape)], axis=1
    )
    q_hops = [Hop(q_total[j], 0, j) for j in others]
    carry = tick(carry, [], q_hops[:2])
    carry, low_w.back = fence(carry, low_w.back)
    v_low = low_w.total()
    v_near = Hop(v_low[1], 0, 1)
    carry = tick(carry, [q_hops[0]] + v_hops[:1], [v_near, q_hops[2], last_hop])
    carry = tick(carry, [v_near, last_hop] + v_hops[1:] + q_hops[1:], [])
    mine_sum, other_sum = ffn_sum[0], last_hop.got.astype(F32)
    even, odd = jnp.where(core == 0, mine_sum, other_sum), jnp.where(core == 0, other_sum, mine_sum)
    join = lambda k: cat(even[:, k * inner : (k + 1) * inner], odd[:, k * inner : (k + 1) * inner])
    gate_up_grad = jnp.stack([join(0), join(1)])
    down_grad = join(2).T
    wide = lambda values: sum(value.astype(F32) for value in values)
    q_all = wide([q_total[0]] + [hop.got for hop in q_hops])
    qo_grad, sums = q_all[:slab], q_all[slab:, :slab]
    kv_grad = wide([v_low[0]] + [hop.got for hop in [v_near] + v_hops])

    def in_order(own, near_hop, far_hop):
        got = jnp.stack([own, near_hop.got[0], far_hop.got[0], far_hop.got[1]])
        return jnp.stack(
            [lax.dynamic_index_in_dim(got, mine[m], 0, keepdims=False) for m in range(planes)]
        )

    layer_rows = in_order(out_blocks[0], near_out, far_out)
    input_grad = in_order(din_blocks[0], near_din, far_din)
    shape = hidden_in.shape
    heads = 3 * HEAD_DIM
    qkv_grad = jnp.stack(
        [
            qo_grad[:, :heads],
            kv_grad[:, :heads],
            cat(kv_grad[:, 2 * LANES :], kv_grad[:, heads : 2 * LANES]),
        ]
    )
    out_grad = cat(qo_grad[:, 2 * LANES :], qo_grad[:, heads : 2 * LANES]).T
    return (
        layer_rows.reshape(shape),
        input_grad.reshape(shape).astype(F32),
        qkv_grad,
        out_grad,
        gate_up_grad,
        down_grad,
        sums[0:2],
        sums[2:4],
    )


def rope_tables(positions, half_dim):
    exponent = jnp.arange(half_dim, dtype=jnp.float32) * (1.0 / half_dim)
    inverse = jnp.power(rope_base, -exponent)
    angles = positions[:, None] * inverse[None, :]
    return (jnp.cos(angles), jnp.sin(angles))


def rotate(vectors, cosine, sine_table):
    half_dim = vectors.shape[-1] // 2
    first_half = vectors[..., :half_dim]
    second_half = vectors[..., half_dim:]
    return jnp.concatenate(
        [
            first_half * cosine - second_half * sine_table,
            second_half * cosine + first_half * sine_table,
        ],
        axis=-1,
    )


def rotate_back(gradient, cosine, sine_table):
    half_dim = gradient.shape[-1] // 2
    first_half = gradient[..., :half_dim]
    second_half = gradient[..., half_dim:]
    return jnp.concatenate(
        [
            first_half * cosine + second_half * sine_table,
            second_half * cosine - first_half * sine_table,
        ],
        axis=-1,
    )


def normalize(residual_stream, gain_row, bias_row):
    center = residual_stream - jnp.mean(residual_stream, axis=-1, keepdims=True)
    inv_std = lax.rsqrt(jnp.mean(center * center, axis=-1, keepdims=True) + norm_eps)
    scaled = center * inv_std
    return (scaled * gain_row + bias_row, scaled, inv_std)


def normalize_back(upstream, scaled, inv_std, gain_row):
    d_scaled = upstream * gain_row
    d_stream = inv_std * (
        d_scaled
        - jnp.mean(d_scaled, axis=-1, keepdims=True)
        - scaled * jnp.mean(d_scaled * scaled, axis=-1, keepdims=True)
    )
    return (d_stream, jnp.sum(upstream * scaled, axis=(0, 1)), jnp.sum(upstream, axis=(0, 1)))


def split_heads(rows, head_dim):
    return rows.reshape(
        rows.shape[0], rows.shape[1], rows.shape[2] // head_dim, head_dim
    ).transpose(1, 2, 0, 3)


def merge_heads(heads):
    return heads.transpose(2, 0, 1, 3).reshape(
        heads.shape[2], heads.shape[0], heads.shape[1] * heads.shape[3]
    )


def score_grads(
    query_part, grad_part, lse_part, delta_part, key_part, value_part, mask_part, score_scale
):
    scores = (
        jnp.einsum("shqd,shkd->shqk", query_part, key_part, preferred_element_type=jnp.float32)
        * score_scale
    )
    prob_full = jnp.where(mask_part, jnp.exp(scores - lse_part[..., None]), 0.0)
    d_probs = jnp.einsum(
        "shqd,shkd->shqk", grad_part, value_part, preferred_element_type=jnp.float32
    )
    d_scores = (prob_full * (d_probs - delta_part[..., None]) * score_scale).astype(jnp.bfloat16)
    return (d_scores, prob_full.astype(jnp.bfloat16))


def body(
    hidden_in,
    cotangent,
    lengths,
    qkv_weight,
    out_weight,
    gate_up_weight,
    down_weight,
    norm_gain,
    norm_bias,
):
    query_key_value_matrix, output_matrix, gate_up_matrix, down_matrix, gain_rows, bias_rows = (
        lax.all_gather(qkv_weight, "dp", axis=1, tiled=True),
        lax.all_gather(out_weight, "dp", axis=1, tiled=True),
        lax.all_gather(gate_up_weight, "dp", axis=1, tiled=True),
        lax.all_gather(down_weight, "dp", axis=1, tiled=True),
        lax.all_gather(norm_gain, "dp", axis=1, tiled=True),
        lax.all_gather(norm_bias, "dp", axis=1, tiled=True),
    )
    gain_rows = gain_rows.astype(jnp.float32)
    bias_rows = bias_rows.astype(jnp.float32)
    group_size = lax.axis_size("dp")
    group_rank = lax.axis_index("dp")
    model_rank = lax.axis_index("mp")
    local_rows = hidden_in.shape[1]
    slots = local_rows * lax.axis_size("mp")
    seq_total = slots * group_size
    head_dim = HEAD_DIM
    score_scale = head_dim ** (-0.5)
    span = min(group_size, 8)
    block_keys = slots * span
    key_blocks = group_size // span
    own_first = group_rank * slots
    positions = (own_first + jnp.arange(slots, dtype=jnp.int32)).astype(jnp.float32)
    cosine, sine_table = rope_tables(positions, head_dim // 2)
    acc_qkv = jnp.zeros(query_key_value_matrix.shape, jnp.float32)
    acc_out = jnp.zeros(output_matrix.shape, jnp.float32)
    acc_gate_up = jnp.zeros(gate_up_matrix.shape, jnp.float32)
    acc_down = jnp.zeros(down_matrix.shape, jnp.float32)
    acc_gain = jnp.zeros(gain_rows.shape, jnp.float32)
    acc_bias = jnp.zeros(bias_rows.shape, jnp.float32)
    layer_rows = []
    input_rows = []
    for micro_step in range(hidden_in.shape[0]):
        x_rows, grad_rows = (
            lax.all_gather(hidden_in[micro_step], "mp", axis=0, tiled=True),
            lax.all_gather(cotangent[micro_step], "mp", axis=0, tiled=True),
        )
        seq_lengths = lengths[micro_step]

        def allowed_keys(first_row, row_count):
            key_pos = first_row + jnp.arange(row_count, dtype=jnp.int32)
            return (key_pos[None, :] < seq_lengths[:, None])[:, None, None, :]

        projected_rows = jnp.einsum(
            "rsd,cde->rsce", x_rows, query_key_value_matrix, preferred_element_type=jnp.float32
        )
        q_heads = rotate(split_heads(projected_rows[:, :, 0], head_dim), cosine, sine_table).astype(
            jnp.bfloat16
        )
        k_heads = rotate(split_heads(projected_rows[:, :, 1], head_dim), cosine, sine_table).astype(
            jnp.bfloat16
        )
        v_heads = split_heads(projected_rows[:, :, 2], head_dim).astype(jnp.bfloat16)
        head_shape = q_heads.shape
        buffer_shape = (head_shape[0], head_shape[1], seq_total, head_shape[3])
        forward_first_row = jnp.int32(0)
        run_max = jnp.full(head_shape[:3], masked_score, jnp.float32)
        key_part = lax.all_gather(k_heads, "dp", axis=2, tiled=True)
        value_part = lax.all_gather(v_heads, "dp", axis=2, tiled=True)
        forward_row_count = key_part.shape[2]
        forward_key_buffer = key_part
        forward_value_buffer = value_part
        old_max = run_max
        allowed = allowed_keys(forward_first_row, forward_row_count)
        scores = (
            jnp.einsum("shqd,shkd->shqk", q_heads, key_part, preferred_element_type=jnp.float32)
            * score_scale
        )
        scores = jnp.where(allowed, scores, masked_score)
        new_max = jnp.maximum(old_max, jnp.max(scores, axis=-1))
        weights_block = jnp.where(allowed, jnp.exp(scores - new_max[..., None]), 0.0)
        new_sum = jnp.sum(weights_block, axis=-1)
        new_acc = jnp.einsum(
            "shqk,shkd->shqd",
            weights_block.astype(jnp.bfloat16),
            value_part,
            preferred_element_type=jnp.float32,
        )
        run_max = new_max
        key_buffer = forward_key_buffer
        value_buffer = forward_value_buffer
        lse = run_max + jnp.log(new_sum)
        attended = new_acc / new_sum[..., None]
        attended_reduced = merge_heads(attended).astype(jnp.bfloat16)
        residual_branch = lax.psum(
            jnp.einsum(
                "rsf,fd->rsd", attended_reduced, output_matrix, preferred_element_type=jnp.float32
            ).astype(jnp.bfloat16),
            "mp",
        ).astype(jnp.float32)
        attention_normed, scaled_one, inv_std_one = normalize(
            x_rows.astype(jnp.float32) + residual_branch, gain_rows[0], bias_rows[0]
        )
        first_low = attention_normed.astype(jnp.bfloat16)
        gate_up_rows = jnp.einsum(
            "rsd,cdf->rscf", first_low, gate_up_matrix, preferred_element_type=jnp.float32
        )
        gate_part = gate_up_rows[:, :, 0]
        up_part = gate_up_rows[:, :, 1]
        sigmoid_gate = jax.nn.sigmoid(gate_part)
        silu_gate = gate_part * sigmoid_gate
        hidden_rows = (silu_gate * up_part).astype(jnp.bfloat16)
        feedforward_output = lax.psum(
            jnp.einsum(
                "rsf,fd->rsd", hidden_rows, down_matrix, preferred_element_type=jnp.float32
            ).astype(jnp.bfloat16),
            "mp",
        ).astype(jnp.float32)
        output, scaled_two, inv_std_two = normalize(
            attention_normed + feedforward_output, gain_rows[1], bias_rows[1]
        )
        layer_rows.append(
            lax.dynamic_slice_in_dim(output, model_rank * local_rows, local_rows, 0).astype(
                jnp.bfloat16
            )
        )
        d_z2, gain_two, bias_two = normalize_back(
            grad_rows.astype(jnp.float32), scaled_two, inv_std_two, gain_rows[1]
        )
        d_ffn = d_z2.astype(jnp.bfloat16)
        acc_down = acc_down + jnp.einsum(
            "rsf,rsd->fd", hidden_rows, d_ffn, preferred_element_type=jnp.float32
        )
        d_hidden = jnp.einsum("rsd,fd->rsf", d_ffn, down_matrix, preferred_element_type=jnp.float32)
        d_gate = d_hidden * up_part * sigmoid_gate * (1.0 + gate_part * (1.0 - sigmoid_gate))
        d_up = d_hidden * silu_gate
        d_gate_up = jnp.stack([d_gate, d_up], axis=2).astype(jnp.bfloat16)
        acc_gate_up = acc_gate_up + jnp.einsum(
            "rsd,rscf->cdf", first_low, d_gate_up, preferred_element_type=jnp.float32
        )
        d_first = (
            lax.psum(
                jnp.einsum(
                    "rscf,cdf->rsd", d_gate_up, gate_up_matrix, preferred_element_type=jnp.float32
                ).astype(jnp.bfloat16),
                "mp",
            ).astype(jnp.float32)
            + d_z2
        )
        d_z1, gain_one, bias_one = normalize_back(d_first, scaled_one, inv_std_one, gain_rows[0])
        acc_gain = acc_gain + jnp.stack([gain_one, gain_two])
        acc_bias = acc_bias + jnp.stack([bias_one, bias_two])
        d_branch = d_z1.astype(jnp.bfloat16)
        acc_out = acc_out + jnp.einsum(
            "rsf,rsd->fd", attended_reduced, d_branch, preferred_element_type=jnp.float32
        )
        d_attended = split_heads(
            jnp.einsum("rsd,fd->rsf", d_branch, output_matrix, preferred_element_type=jnp.float32),
            head_dim,
        ).astype(jnp.bfloat16)
        delta = jnp.sum(d_attended.astype(jnp.float32) * attended, axis=-1)
        zero_heads = jnp.zeros(head_shape, jnp.float32)

        def query_block(step_index, partial_sums):
            first_row = step_index * block_keys
            key_part = lax.dynamic_slice_in_dim(key_buffer, first_row, block_keys, 2)
            value_part = lax.dynamic_slice_in_dim(value_buffer, first_row, block_keys, 2)
            d_scores, prob_block = score_grads(
                q_heads,
                d_attended,
                lse,
                delta,
                key_part,
                value_part,
                allowed_keys(first_row, block_keys),
                score_scale,
            )
            d_query = partial_sums[0] + jnp.einsum(
                "shqk,shkd->shqd", d_scores, key_part, preferred_element_type=jnp.float32
            )
            key_total = lax.dynamic_update_slice_in_dim(
                partial_sums[1],
                jnp.einsum(
                    "shqk,shqd->shkd", d_scores, q_heads, preferred_element_type=jnp.float32
                ),
                first_row,
                2,
            )
            value_total = lax.dynamic_update_slice_in_dim(
                partial_sums[2],
                jnp.einsum(
                    "shqk,shqd->shkd", prob_block, d_attended, preferred_element_type=jnp.float32
                ),
                first_row,
                2,
            )
            return (d_query, key_total, value_total)

        zero_keys = jnp.zeros(buffer_shape, jnp.float32)
        d_query, key_total, value_total = lax.fori_loop(
            0, key_blocks, query_block, (zero_heads, zero_keys, zero_keys)
        )
        d_key, d_value = (
            lax.psum_scatter(key_total, "dp", scatter_dimension=2, tiled=True),
            lax.psum_scatter(value_total, "dp", scatter_dimension=2, tiled=True),
        )
        d_projected = jnp.stack(
            [
                merge_heads(rotate_back(d_query, cosine, sine_table)),
                merge_heads(rotate_back(d_key, cosine, sine_table)),
                merge_heads(d_value),
            ],
            axis=2,
        ).astype(jnp.bfloat16)
        acc_qkv = acc_qkv + jnp.einsum(
            "rsd,rsce->cde", x_rows, d_projected, preferred_element_type=jnp.float32
        )
        d_input = lax.psum_scatter(
            jnp.einsum(
                "rsce,cde->rsd",
                d_projected,
                query_key_value_matrix,
                preferred_element_type=jnp.float32,
            ).astype(jnp.bfloat16),
            "mp",
            scatter_dimension=0,
            tiled=True,
        ).astype(jnp.float32)
        input_rows.append(
            d_input + lax.dynamic_slice_in_dim(d_z1, model_rank * local_rows, local_rows, 0)
        )
    qkv_grad, out_grad, gate_up_grad, down_grad, gain_grad, bias_grad = (
        lax.psum_scatter(acc_qkv, "dp", scatter_dimension=1, tiled=True),
        lax.psum_scatter(acc_out, "dp", scatter_dimension=1, tiled=True),
        lax.psum_scatter(acc_gate_up, "dp", scatter_dimension=1, tiled=True),
        lax.psum_scatter(acc_down, "dp", scatter_dimension=1, tiled=True),
        lax.psum_scatter(acc_gain, "dp", scatter_dimension=1, tiled=True),
        lax.psum_scatter(acc_bias, "dp", scatter_dimension=1, tiled=True),
    )
    return (
        jnp.stack(layer_rows),
        jnp.stack(input_rows),
        qkv_grad,
        out_grad,
        gate_up_grad,
        down_grad,
        gain_grad,
        bias_grad,
    )


def solution(mesh):
    rows_of = dict(mesh.shape)
    by_plane = rows_of == {"dp": 8, "mp": 4}
    return jax.shard_map(
        plane_body if by_plane else body,
        mesh=mesh,
        in_specs=(
            P(None, ("dp", "mp"), None, None),
            P(None, ("dp", "mp"), None, None),
            P(),
            P(None, "dp", "mp"),
            P("mp", "dp"),
            P(None, "dp", "mp"),
            P("mp", "dp"),
            P(None, "dp"),
            P(None, "dp"),
        ),
        out_specs=(
            P(None, ("dp", "mp"), None, None),
            P(None, ("dp", "mp"), None, None),
            P(None, "dp", "mp"),
            P("mp", "dp"),
            P(None, "dp", "mp"),
            P("mp", "dp"),
            P(None, "dp"),
            P(None, "dp"),
        ),
        check_vma=False,
    )
```

```python
import functools

import jax
import jax.numpy as jnp
from jax import lax
from jax.experimental import pallas as pl
from jax.experimental.pallas import tpu as pltpu
from jax.sharding import PartitionSpec as P

HEAD_DIM = 64

norm_eps = 1e-12
rope_base = 1000.0
masked_score = -1e30

BF = jnp.bfloat16
F32 = jnp.float32
LANES = 128

CORE, XBIT, YBIT = 1, 2, 4
BOTH = XBIT | YBIT


def permute(value, dp_mask, mp_mask=0):
    mp = lax.axis_size("mp")
    count = lax.axis_size("dp") * mp
    pairs = [(i, i ^ (dp_mask((i // mp) & CORE) * mp + mp_mask)) for i in range(count)]
    return lax.ppermute(value, ("dp", "mp"), pairs)


def swap(value, dp_mask=0, mp_mask=0):
    return permute(value, lambda core: dp_mask, mp_mask)


def first_mask(core):
    return XBIT + core * (YBIT - XBIT)


def second_mask(core):
    return YBIT + core * (XBIT - YBIT)


def to_first(value):
    return permute(value, first_mask)


def to_second(value):
    return permute(value, second_mask)


def to_core(value):
    return swap(value, CORE)


def gathered_masks(core):
    first, second = first_mask(core), second_mask(core)
    return (0, first, second, BOTH, CORE, CORE ^ second, CORE ^ first, CORE ^ BOTH)


def kept_masks(core):
    first, second = first_mask(core), second_mask(core)
    return (0, second, first, BOTH), (CORE, CORE ^ first, CORE ^ second, CORE ^ BOTH)


SLOTS = (0, 2, 1, 3)


def add_low(a, b):
    return (a.astype(F32) + b.astype(F32)).astype(BF)


def add_wide(a, b):
    return a.astype(F32) + b.astype(F32)


def fence(*values):
    return lax.optimization_barrier(values)


class Scatter:
    def __init__(self, keep, send, stage=0):
        self.keep, self.go, self.stage = keep, send, stage

    def send(self):
        self.back = (to_core, to_first, to_second)[self.stage](self.go)

    def fold(self):
        back = self.back
        self.stage += 1
        if self.stage == 1:
            self.keep, self.go = add_low(self.keep[:2], back[:2]), add_low(self.keep[2:], back[2:])
        elif self.stage == 2:
            self.go = add_low(self.keep[1], back[1])
            self.keep = add_low(self.keep[0], back[0])

    def total(self):
        return add_low(self.keep, self.back)


class Hop:
    def __init__(self, value, dp_mask=0, mp_mask=0):
        self.go, self.masks = value, (dp_mask, mp_mask)

    def send(self):
        self.back = swap(self.go, *self.masks)

    def fold(self):
        self.got = self.back


class Sum(Hop):
    def fold(self):
        self.got = self.go + self.back


def tick(carry, waits, starts):
    arrived = fence(carry, [w.back for w in waits])
    for w, back in zip(waits, arrived[1]):
        w.back = back
        w.fold()
    starts = starts() if callable(starts) else starts
    ready = fence(arrived[0], [t.go for t in starts])
    for t, go in zip(starts, ready[1]):
        t.go = go
        t.send()
    return ready[0]


def params(limit=60 << 20):
    return pltpu.CompilerParams(vmem_limit_bytes=limit)


def cost(flops, size):
    del flops, size
    return pl.CostEstimate(flops=1, bytes_accessed=1, transcendentals=0)


ANY = pl.BlockSpec(memory_space=pl.ANY)
VM = pl.BlockSpec(memory_space=pltpu.VMEM)


def dot(a, b):
    return lax.dot_general(a, b, (((1,), (0,)), ((), ())), preferred_element_type=F32)


def dot_t(a, b):
    return lax.dot_general(a, b, (((1,), (1,)), ((), ())), preferred_element_type=F32)


def dot_rows(a, b):
    return lax.dot_general(a, b, (((0,), (0,)), ((), ())), preferred_element_type=F32)


def piece_copies(pieces, buffer, sems, plane):
    mine = lax.axis_index("dp")
    masks = gathered_masks(mine & CORE)
    copies = []
    for k, piece in enumerate(pieces):
        rows = buffer.shape[0] // len(pieces)
        start = pl.multiple_of((mine ^ masks[k]) * rows, rows)
        copies.append(
            pltpu.make_async_copy(
                piece.at[pl.ds(plane * rows, rows), :], buffer.at[pl.ds(start, rows), :], sems.at[k]
            )
        )
    return copies


def ffn_copies(pieces, plane, wide, narrow, sems):
    mine = lax.axis_index("dp")
    masks = gathered_masks(mine & CORE)
    inner = wide.shape[1]
    copies = []
    for k, piece in enumerate(pieces):
        for core in range(2):
            rows = piece.shape[2]
            start = pl.multiple_of((mine ^ masks[k] ^ core) * rows, rows)
            source = piece.at[plane, core]
            for i, (target, lanes) in enumerate(
                ((wide, slice(0, inner)), (narrow, slice(inner, piece.shape[3])))
            ):
                copies.append(
                    pltpu.make_async_copy(
                        source.at[:, lanes],
                        target.at[pl.ds(start, rows), :],
                        sems.at[i, 2 * k + core],
                    )
                )
    return copies


def out_copies(buffer, keep, send, sems, rows):
    mine = lax.axis_index("dp")
    copies = []
    for side, (target, masks) in enumerate(zip((keep, send), kept_masks(mine & CORE))):
        for i, mask in enumerate(masks):
            start = pl.multiple_of((mine ^ mask) * rows, rows)
            copies.append(
                pltpu.make_async_copy(
                    buffer.at[pl.ds(start, rows), :], target(i), sems.at[4 * side + i]
                )
            )
    return copies


def chip_copies(buffer, keep, sems, rows):
    mine = lax.axis_index("dp")
    copies = []
    for i, mask in enumerate(kept_masks(mine & CORE)[0]):
        for core in range(2):
            start = pl.multiple_of((mine ^ mask ^ core) * rows, rows)
            copies.append(
                pltpu.make_async_copy(
                    buffer.at[pl.ds(start, rows), :], keep(i, core), sems.at[2 * i + core]
                )
            )
    return copies


def start_all(copies):
    for copy in copies:
        copy.start()


def wait_all(copies):
    for copy in copies:
        copy.wait()


def partner(u):
    lane = lax.broadcasted_iota(jnp.int32, u.shape, 1)
    quarter = HEAD_DIM // 2
    return jnp.where(
        lane % HEAD_DIM < quarter,
        pltpu.roll(u, LANES - quarter, 1),
        pltpu.roll(u, quarter, 1),
    )


def low_lanes(shape):
    return lax.broadcasted_iota(jnp.int32, shape, 1) < HEAD_DIM


def kv_kernel(planes, x_ref, tab_ref, *refs):
    pieces, (kv_ref, w, sems) = refs[:8], refs[8:]
    copies = [piece_copies(pieces, w.at[p], sems.at[p], p) for p in range(planes)]
    for group in copies:
        start_all(group)
    x = x_ref[...]
    for p in range(planes):
        wait_all(copies[p])
        y = dot(x, w[p][:, : 3 * LANES])
        y0, y1, y2 = y[:, :LANES], y[:, LANES : 2 * LANES], y[:, 2 * LANES :]
        base = p * 3 * LANES
        kv_ref[:, base : base + LANES] = (y0 * tab_ref[0] + partner(y0) * tab_ref[1]).astype(BF)
        kv_ref[:, base + LANES : base + 2 * LANES] = (
            y1 * tab_ref[2] + partner(y1) * tab_ref[3]
        ).astype(BF)
        kv_ref[:, base + 2 * LANES : base + 3 * LANES] = y2.astype(BF)


def q_kernel(planes, scale, x_ref, tab_ref, *refs):
    pieces, (q_ref, w, sems) = refs[:8], refs[8:]
    copies = [piece_copies(pieces, w.at[p], sems.at[p], p) for p in range(planes)]
    for group in copies:
        start_all(group)
    x = x_ref[...]
    for p in range(planes):
        wait_all(copies[p])
        y = dot(x, w[p][:, 3 * LANES : 5 * LANES])
        y0, y1 = y[:, :LANES], y[:, LANES:]
        low = low_lanes(y1.shape)
        base = p * 2 * LANES
        q0 = y0 * tab_ref[0] + partner(y0) * tab_ref[1]
        q1 = jnp.where(low, y1 * tab_ref[2] + partner(y1) * tab_ref[3], 0.0)
        q_ref[:, base : base + LANES] = (q0 * scale).astype(BF)
        q_ref[:, base + LANES : base + 2 * LANES] = (q1 * scale).astype(BF)


def attend_kernel(q_ref, bias_ref, *refs):
    pieces = refs[:8]
    att_ref, low_ref, lse_ref, s_ref = refs[8:]
    rows = q_ref.shape[0]
    keys = rows

    def block(k, column):
        return pieces[k][:, column * LANES : (column + 1) * LANES]

    low = low_lanes((rows, LANES))
    lane = lax.broadcasted_iota(jnp.int32, (rows, LANES), 1)
    q0, q1 = q_ref[:, :LANES], q_ref[:, LANES:]
    zero = jnp.zeros_like(q0)
    heads = (
        (jnp.where(low, q0, zero), 0, 2),
        (jnp.where(low, zero, q0), 0, 2),
        (q1, 1, 1),
    )
    stats = jnp.zeros((rows, LANES), F32)
    results = []
    for h, (q, key_column, value_column) in enumerate(heads):
        peak = jnp.full((rows, LANES), -jnp.inf, F32)
        for k in range(8):
            s = dot_t(q, block(k, key_column)) + bias_ref[k : k + 1, :]
            s_ref[:, k * keys : (k + 1) * keys] = s
            for c in range(keys // LANES):
                peak = jnp.maximum(peak, s[:, c * LANES : (c + 1) * LANES])
        top = jnp.max(peak, axis=1, keepdims=True)
        total = jnp.zeros((rows, LANES), F32)
        acc = jnp.zeros((rows, LANES), F32)
        for k in range(8):
            e = jnp.exp(s_ref[:, k * keys : (k + 1) * keys] - top)
            for c in range(keys // LANES):
                total = total + e[:, c * LANES : (c + 1) * LANES]
            acc = acc + dot(e.astype(BF), block(k, value_column))
        total = jnp.sum(total, axis=1, keepdims=True)
        results.append(acc / total)
        stats = jnp.where(lane == h, top + jnp.log(total), stats)
    pair = jnp.where(low, results[0], results[1])
    single = jnp.where(low, 0.0, results[2])
    att_ref[:, :LANES] = single
    att_ref[:, LANES:] = pair
    low_ref[:, :LANES] = single.astype(BF)
    low_ref[:, LANES:] = pair.astype(BF)
    lse_ref[0] = stats.T[:8, :]


def attend_back_kernel(
    scale, q_ref, dat_ref, lse_ref, delta_ref, bias_ref, tab_ref, *refs
):
    pieces = refs[:8]
    keep_ref, send_ref, dq_ref = refs[8:]
    rows = q_ref.shape[0]

    def block(k, column):
        return pieces[k][:, column * LANES : (column + 1) * LANES]

    low = low_lanes((rows, LANES))
    q0, q1 = q_ref[:, :LANES], q_ref[:, LANES:]
    d0, d1 = dat_ref[:, LANES:], dat_ref[:, :LANES]
    zero = jnp.zeros_like(q0)
    heads = (
        (jnp.where(low, q0, zero), jnp.where(low, d0, zero), 0, 2),
        (jnp.where(low, zero, q0), jnp.where(low, zero, d0), 0, 2),
        (q1, d1, 1, 1),
    )
    dq = [jnp.zeros((LANES, rows), F32) for _ in heads]
    for k in range(8):
        side, index = divmod(k, 4)
        target = (keep_ref, send_ref)[side]
        slot = SLOTS[index]
        mask = bias_ref[:, k : k + 1]
        blocks = [block(k, c) for c in range(3)]
        keys_t = [blocks[0].T, blocks[1].T]
        parts = []
        for h, (q, d, key_column, value_column) in enumerate(heads):
            s = dot_t(blocks[key_column], q) + mask
            dp = dot_t(blocks[value_column], d)
            p = jnp.exp(s - lse_ref[0, h : h + 1, :])
            ds = (p * (dp - delta_ref[0, h : h + 1, :])).astype(BF)
            p = p.astype(BF)
            parts.append((dot(ds, q), dot(p, d)))
            dq[h] = dq[h] + dot(keys_t[key_column], ds)
        target[slot, :, :LANES] = (parts[0][0] + parts[1][0]).astype(BF)
        target[slot, :, LANES : 2 * LANES] = (parts[2][0] + parts[2][1]).astype(BF)
        target[slot, :, 2 * LANES :] = (parts[0][1] + parts[1][1]).astype(BF)
    row = lax.broadcasted_iota(jnp.int32, (LANES, rows), 0) < HEAD_DIM
    pair = jnp.where(row, dq[0], dq[1]).T * scale
    single = jnp.where(row, dq[2], 0.0).T * scale
    dq_ref[:, :LANES] = (pair * tab_ref[0] - partner(pair) * tab_ref[1]).astype(BF)
    dq_ref[:, LANES:] = (single * tab_ref[2] - partner(single) * tab_ref[3]).astype(BF)


def center_scale(rows):
    center = rows - jnp.mean(rows, axis=-1, keepdims=True)
    inv = lax.rsqrt(jnp.mean(center * center, axis=-1, keepdims=True) + norm_eps)
    return center * inv, inv


def norm_back(e, scaled, inv):
    return inv * (
        e
        - jnp.mean(e, axis=-1, keepdims=True)
        - scaled * jnp.mean(e * scaled, axis=-1, keepdims=True)
    )


def rows_sum(value):
    return jnp.sum(value, axis=0, keepdims=True)


def mix_kernel(planes, x_ref, att_ref, norm_ref, *refs):
    pieces = refs[:8]
    flow_ref, first_ref, scaled_ref, inv_ref, w, sems = refs[8:]
    copies = [piece_copies(pieces, w.at[p], sems.at[p], p) for p in range(planes)]
    for group in copies:
        start_all(group)
    total = x_ref[...].astype(F32)
    for p in range(planes):
        wait_all(copies[p])
        total = total + dot_t(
            att_ref[:, p * 2 * LANES : (p + 1) * 2 * LANES], w[p][:, 4 * LANES : 6 * LANES]
        )
    scaled, inv = center_scale(total)
    scaled_ref[...] = scaled
    inv_ref[...] = jnp.broadcast_to(inv, inv_ref.shape)
    first = scaled * norm_ref[0:1, :] + norm_ref[2:3, :]
    first_ref[...] = first
    flow_ref[...] = first.astype(BF)


def ffn_kernel(planes, own_ref, other_ref, *refs):
    wide = (refs[:4], refs[4:8])
    ffn_ref, send_ref, wgu, wd, flow, sems = refs[8:]
    half = planes // 2
    rows = own_ref.shape[0]
    copies = [
        ffn_copies(wide[p // half], p % half, wgu.at[p], wd.at[p], sems.at[p])
        for p in range(planes)
    ]
    for group in copies:
        start_all(group)
    flow[:rows, :] = own_ref[...]
    flow[rows:, :] = other_ref[...]
    total = jnp.zeros(flow.shape, F32)
    inner = wd.shape[2]
    for p in range(planes):
        wait_all(copies[p])
        both = dot(flow[...], wgu[p])
        gate, up = both[:, :inner], both[:, inner:]
        hidden = (gate * jax.nn.sigmoid(gate) * up).astype(BF)
        total = total + dot_t(hidden, wd[p])
    ffn_ref[...] = total[:rows]
    send_ref[...] = total[rows:].astype(BF)


def close_kernel(ffn_ref, back_ref, first_ref, cot_ref, norm_ref, out_ref, dz2_ref, dffn_ref, sums_ref):
    gain, bias = norm_ref[1:2, :], norm_ref[3:4, :]
    scaled, inv = center_scale(first_ref[...] + (ffn_ref[...] + back_ref[...].astype(F32)))
    out_ref[...] = (scaled * gain + bias).astype(BF)
    cot = cot_ref[...].astype(F32)
    dz2 = norm_back(cot * gain, scaled, inv)
    dz2_ref[...] = dz2
    dffn_ref[...] = dz2.astype(BF)
    sums_ref[...] = jnp.concatenate(
        [rows_sum(cot * scaled), rows_sum(cot), jnp.zeros((6, cot.shape[1]), F32)], axis=0
    )


def ffn_back_kernel(slab, *refs):
    acc_ref, refs = refs[0], refs[1:]
    flow_own, flow_other, dffn_own, dffn_other = refs[:4]
    pieces, refs = refs[4:8], refs[8:]
    dfirst_ref, send_ref, keep_ref, go_ref, wgu, wd, flow, dffn, both_ref, hidden, grads, sems, out_sems = refs
    rows = flow_own.shape[0]
    count = wgu.shape[0]
    inner = wgu.shape[2] // 2
    copies = []
    for p in range(count):
        group = ffn_copies(
            pieces, p, wgu.at[p], wd.at[:, p * inner : (p + 1) * inner], sems.at[p]
        )
        start_all(group)
        copies.extend(group)
    flow[:rows, :] = flow_own[...]
    flow[rows:, :] = flow_other[...]
    dffn[:rows, :] = dffn_own[...]
    dffn[rows:, :] = dffn_other[...]
    wait_all(copies)
    for p in range(count):
        both = dot(flow[...], wgu[p])
        both_ref[p] = both
        gate, up = both[:, :inner], both[:, inner:]
        hidden[:, p * inner : (p + 1) * inner] = (gate * jax.nn.sigmoid(gate) * up).astype(BF)
    down = dot(dffn[...].T, hidden[...])
    for p in range(count):
        grads[p, :, 2 * inner :] = down[:, p * inner : (p + 1) * inner].astype(BF)
    d_hidden = dot(dffn[...], wd[...])
    flow_t = flow[...].T
    total = acc_ref[...]
    outs = []
    for p in range(count):
        gate, up = both_ref[p][:, :inner], both_ref[p][:, inner:]
        d = d_hidden[:, p * inner : (p + 1) * inner]
        sig = jax.nn.sigmoid(gate)
        d_gate = (d * up * sig * (1.0 + gate * (1.0 - sig))).astype(BF)
        d_up = (d * (gate * sig)).astype(BF)
        both = jnp.concatenate([d_gate, d_up], axis=1)
        grads[p, :, : 2 * inner] = dot(flow_t, both).astype(BF)
        group = chip_copies(
            grads.at[p],
            lambda i, core: (keep_ref, go_ref)[i // 2].at[i % 2, p, core],
            out_sems.at[p],
            slab,
        )
        start_all(group)
        outs.extend(group)
        total = total + dot_t(both, wgu[p])
    dfirst_ref[...] = total
    send_ref[...] = total[rows:].astype(BF)
    wait_all(outs)


def branch_back_kernel(
    planes, dfirst_ref, back_ref, dz2_ref, scaled_ref, inv_ref, norm_ref, two_ref, att_ref, *refs
):
    pieces = refs[:8]
    dz1_ref, dat_ref, delta_ref, sums_ref, w, sems = refs[8:]
    copies = [piece_copies(pieces, w.at[p], sems.at[p], p) for p in range(planes)]
    for group in copies:
        start_all(group)
    dfirst = dfirst_ref[...] + back_ref[...].astype(F32) + dz2_ref[...]
    scaled = scaled_ref[...]
    two = two_ref[...]
    sums_ref[...] = jnp.concatenate(
        [
            rows_sum(dfirst * scaled),
            two[0:1],
            rows_sum(dfirst),
            two[1:2],
            jnp.zeros((4, dfirst.shape[1]), F32),
        ],
        axis=0,
    )
    dz1 = norm_back(dfirst * norm_ref[0:1, :], scaled, inv_ref[:, 0:1])
    dz1_ref[...] = dz1
    d_branch = dz1.astype(BF)
    low = low_lanes((dfirst.shape[0], LANES))
    lane = lax.broadcasted_iota(jnp.int32, (dfirst.shape[0], LANES), 1)
    for p in range(planes):
        wait_all(copies[p])
        d = dot(d_branch, w[p][:, 4 * LANES : 6 * LANES])
        single = jnp.where(low, 0.0, d[:, :LANES]).astype(BF)
        pair = d[:, LANES:].astype(BF)
        dat_ref[:, p * 2 * LANES : p * 2 * LANES + LANES] = single
        dat_ref[:, p * 2 * LANES + LANES : (p + 1) * 2 * LANES] = pair
        both = pair.astype(F32) * att_ref[:, p * 2 * LANES + LANES : (p + 1) * 2 * LANES]
        alone = single.astype(F32) * att_ref[:, p * 2 * LANES : p * 2 * LANES + LANES]
        zero = jnp.zeros_like(both)
        stats = zero
        for h, part in enumerate((jnp.where(low, both, zero), jnp.where(low, zero, both), alone)):
            stats = jnp.where(lane == h, jnp.sum(part, axis=1, keepdims=True), stats)
        delta_ref[p] = stats.T[:8, :]


def query_back_kernel(planes, slab, x_ref, low_dq_ref, high_dq_ref, dz1_ref, low_ref, *refs):
    pieces = refs[:8]
    din_ref, keep_ref, send_ref, w, grads, sems, out_sems = refs[8:]
    half = planes // 2
    copies = [piece_copies(pieces, w.at[p], sems.at[p], p) for p in range(planes)]
    for group in copies:
        start_all(group)
    x_t = x_ref[...].T
    total = dz1_ref[...]
    branch_t = total.astype(BF).T
    outs = []
    for p in range(planes):
        at = (p % half) * 2 * LANES
        d = (low_dq_ref, high_dq_ref)[p // half][:, at : at + 2 * LANES]
        query = dot(x_t, d)
        output = dot(branch_t, low_ref[:, p * 2 * LANES : (p + 1) * 2 * LANES])
        grads[p, :, :LANES] = query[:, :LANES].astype(BF)
        grads[p, :, LANES : 2 * LANES] = (query[:, LANES:] + output[:, :LANES]).astype(BF)
        grads[p, :, 2 * LANES :] = output[:, LANES:].astype(BF)
        group = out_copies(
            grads.at[p],
            lambda i: keep_ref.at[i, p],
            lambda i: send_ref.at[i, p],
            out_sems.at[p],
            slab,
        )
        start_all(group)
        outs.extend(group)
        wait_all(copies[p])
        total = total + dot_t(d, w[p][:, 3 * LANES : 5 * LANES])
    din_ref[...] = total
    wait_all(outs)


def kv_back_kernel(base, count, slab, x_ref, acc_ref, tab_ref, keep_d_ref, back_d_ref, *refs):
    pieces = refs[:8]
    din_ref, keep_ref, send_ref, w, grads, sems, out_sems = refs[8:]
    copies = [piece_copies(pieces, w.at[p], sems.at[p], base + p) for p in range(count)]
    for group in copies:
        start_all(group)
    x_t = x_ref[...].T
    total = acc_ref[...]
    outs = []
    for p in range(count):
        lanes = slice(p * 3 * LANES, (p + 1) * 3 * LANES)
        d = keep_d_ref[:, lanes].astype(F32) + back_d_ref[:, lanes].astype(F32)
        d0, d1, d2 = d[:, :LANES], d[:, LANES : 2 * LANES], d[:, 2 * LANES :]
        d = jnp.concatenate(
            [
                (d0 * tab_ref[0] - partner(d0) * tab_ref[1]).astype(BF),
                (d1 * tab_ref[2] - partner(d1) * tab_ref[3]).astype(BF),
                d2.astype(BF),
            ],
            axis=1,
        )
        grads[p] = dot(x_t, d).astype(BF)
        group = out_copies(
            grads.at[p],
            lambda i: keep_ref.at[i, p],
            lambda i: send_ref.at[i, p],
            out_sems.at[p],
            slab,
        )
        start_all(group)
        outs.extend(group)
        wait_all(copies[p])
        total = total + dot_t(d, w[p][:, : 3 * LANES])
    din_ref[...] = total.astype(din_ref.dtype)
    wait_all(outs)


def sds(shape, dtype):
    return jax.ShapeDtypeStruct(shape, dtype)


def plane_body(
    hidden_in,
    cotangent,
    lengths,
    qkv_weight,
    out_weight,
    gate_up_weight,
    down_weight,
    norm_gain,
    norm_bias,
):
    planes = lax.axis_size("mp")
    pair = planes // 2
    group = lax.axis_size("dp")
    dp, mp = lax.axis_index("dp"), lax.axis_index("mp")
    core = dp & CORE
    part = hidden_in.shape[1]
    width = hidden_in.shape[3]
    rows = part * planes
    slab = qkv_weight.shape[1]
    inner = gate_up_weight.shape[2] // 2
    scale = HEAD_DIM ** (-0.5)
    mine = mp ^ jnp.arange(planes, dtype=jnp.int32)
    others = range(1, planes)

    def blocks_of(array):
        array = array.reshape(array.shape[0], part, width)
        return [lax.dynamic_index_in_dim(array, mine[j], 0, keepdims=False) for j in range(planes)]

    q_w, k_w, v_w = qkv_weight[0], qkv_weight[1], qkv_weight[2]
    o_w, d_w = out_weight.T, down_weight.T
    two = 2 * HEAD_DIM
    own = jnp.concatenate(
        [k_w[:, :two], k_w[:, two:], v_w[:, two:], v_w[:, :two]]
        + [q_w[:, :two], q_w[:, two:], o_w[:, two:], o_w[:, :two]],
        axis=1,
    )
    x_blocks, cot_blocks = blocks_of(hidden_in), blocks_of(cotangent)

    def half_of(index):
        take = lambda w: lax.dynamic_slice_in_dim(w, index * inner, inner, 1)
        return jnp.concatenate([take(gate_up_weight[0]), take(gate_up_weight[1]), take(d_w)], axis=1)

    ffn_mine, ffn_give = half_of(core), half_of(1 - core)
    norm_own = jnp.concatenate([norm_gain, norm_bias, jnp.zeros((12, slab), BF)], axis=0)
    norm_rows = lax.dynamic_update_slice(jnp.zeros((16, width), BF), norm_own, (0, dp * slab))

    z = [swap(own, 0, j) for j in others]
    ffn_get = to_core(ffn_give)
    z, ffn_get, x_blocks = fence(z, ffn_get, x_blocks)
    w_four = jnp.concatenate([own] + z + [norm_rows], axis=0)
    ffn_own = jnp.stack([ffn_mine, ffn_get])
    w_first, w_second = to_first(w_four), to_second(w_four)
    x_got = swap(jnp.stack([x_blocks[1], x_blocks[3]]), 0, 1)
    f_one = swap(ffn_own, 0, 1)
    f_two = [swap(ffn_mine, 0, 2)]
    w_first, w_second, x_got, f_one, f_two, ffn_get, ffn_own, w_four = fence(
        w_first, w_second, x_got, f_one, f_two, ffn_get, ffn_own, w_four
    )
    w_diag = to_second(w_first)
    w_core = [to_core(w_four), to_core(w_first)]
    low = [jnp.stack([ffn_own, f_one])]
    low.append(to_first(low[0]))
    x_far = swap(jnp.stack([x_blocks[2], x_got[1]]), 0, 2)
    w_diag, w_core, w_second, x_far, ffn_get, f_one, low[0] = fence(
        w_diag, w_core, w_second, x_far, ffn_get, f_one, low[0]
    )
    x = jnp.concatenate([x_blocks[0], x_got[0], x_far[0], x_far[1]], axis=0)
    w_core += [to_core(w_second), to_core(w_diag)]
    f_two.append(swap(ffn_get, 0, 2))
    low.append(to_second(low[0]))
    weights = [w_four, w_first, w_second, w_diag] + w_core
    norms = sum(w[planes * slab : planes * slab + 8].astype(F32) for w in weights)

    within = (mine[:, None] * part + jnp.arange(part, dtype=jnp.int32)[None, :]).reshape(rows)
    positions = (dp * rows + within).astype(F32)
    half = HEAD_DIM // 2
    exponent = jnp.arange(half, dtype=F32) * (1.0 / half)
    angles = positions[:, None] * jnp.power(rope_base, -exponent)[None, :]
    cosine, sine = jnp.cos(angles), jnp.sin(angles)
    cos_head = jnp.concatenate([cosine, cosine], axis=1)
    sin_head = jnp.concatenate([-sine, sine], axis=1)
    one, none = jnp.ones_like(cos_head), jnp.zeros_like(cos_head)
    cat = lambda a, b: jnp.concatenate([a, b], axis=1)
    tables = jnp.stack(
        [cat(cos_head, cos_head), cat(sin_head, sin_head), cat(cos_head, one), cat(sin_head, none)]
    )
    length = lax.dynamic_index_in_dim(lengths.reshape(-1), mp, 0, keepdims=False)
    piece_base = (dp ^ jnp.stack([jnp.int32(0) + m for m in gathered_masks(core)])) * rows
    key_pos = piece_base[:, None] + within[None, :]
    bias = jnp.where(key_pos < length, 0.0, masked_score).astype(F32)
    bias_t = bias.T

    dma = pltpu.SemaphoreType.DMA
    w_scratch = [pltpu.VMEM((planes, width, 6 * LANES), BF), dma((planes, 8))]

    def project(kernel, columns, name):
        return pl.pallas_call(
            kernel,
            out_shape=sds((rows, planes * columns), BF),
            in_specs=[VM, VM] + [ANY] * 8,
            out_specs=VM,
            scratch_shapes=w_scratch,
            compiler_params=params(),
            cost_estimate=cost(1, 1),
            name=name,
        )(x, tables, *weights)

    kv = project(functools.partial(kv_kernel, planes), 3 * LANES, "kv_project")
    kv, low, f_one, f_two, bias, bias_t = fence(kv, low, f_one, f_two, bias, bias_t)
    keys = [kv, to_first(kv), to_second(kv)]
    key_core = [to_core(kv)]
    low.append(to_second(low[1]))
    f_three = swap(f_one, 0, 2)
    q = project(functools.partial(q_kernel, planes, scale), 2 * LANES, "q_project")
    q, key_core, keys[1], keys[2], f_three, low[3] = fence(
        q, key_core, keys[1], keys[2], f_three, low[3]
    )
    keys.append(to_second(keys[1]))
    key_core += [to_core(keys[1]), to_core(keys[2])]
    high = [jnp.stack([jnp.stack(f_two), f_three])]
    keys[3], key_core, cot_blocks, high = fence(keys[3], key_core, cot_blocks, high)
    key_core.append(to_core(keys[3]))
    high += [to_first(high[0]), to_second(high[0])]
    cot_got = swap(jnp.stack([cot_blocks[1], cot_blocks[3]]), 0, 1)
    kv_all = keys + key_core

    at_spec = lambda base, columns: pl.BlockSpec((rows, columns), lambda i: (0, i + base))
    seq = rows * group
    att, att_low, lse = pl.pallas_call(
        attend_kernel,
        grid=(planes,),
        out_shape=(
            sds((rows, planes * 2 * LANES), F32),
            sds((rows, planes * 2 * LANES), BF),
            sds((planes, 8, rows), F32),
        ),
        in_specs=[at_spec(0, 2 * LANES), pl.BlockSpec((8, rows), lambda i: (0, 0))]
        + [at_spec(0, 3 * LANES)] * 8,
        out_specs=(
            at_spec(0, 2 * LANES),
            at_spec(0, 2 * LANES),
            pl.BlockSpec((1, 8, rows), lambda i: (i, 0, 0)),
        ),
        scratch_shapes=[pltpu.VMEM((rows, seq), F32)],
        compiler_params=params(),
        cost_estimate=cost(1, 1),
        name="attend",
    )(q, bias, *kv_all)
    act = lambda dtype: sds((rows, width), dtype)
    att_low, high[1], cot_got, cot_blocks = fence(att_low, high[1], cot_got, cot_blocks)
    high.append(to_second(high[1]))
    cot_far = swap(jnp.stack([cot_blocks[2], cot_got[1]]), 0, 2)
    flow, first, scaled, inv = pl.pallas_call(
        functools.partial(mix_kernel, planes),
        out_shape=(act(BF), act(F32), act(F32), sds((rows, LANES), F32)),
        in_specs=[VM] * 3 + [ANY] * 8,
        out_specs=(VM,) * 4,
        scratch_shapes=w_scratch,
        compiler_params=params(),
        cost_estimate=cost(1, 1),
        name="mix",
    )(x, att_low, norms, *weights)
    flow_other = to_core(flow)

    ffn, give = pl.pallas_call(
        functools.partial(ffn_kernel, planes),
        out_shape=(act(F32), act(BF)),
        in_specs=[VM] * 2 + [ANY] * 8,
        out_specs=(VM, VM),
        scratch_shapes=[
            pltpu.VMEM((planes, width, 2 * inner), BF),
            pltpu.VMEM((planes, width, inner), BF),
            pltpu.VMEM((2 * rows, width), BF),
            dma((planes, 2, 8)),
        ],
        compiler_params=params(),
        cost_estimate=cost(1, 1),
        name="ffn",
    )(flow, flow_other, *low, *high)
    ffn, cot_far = fence(ffn, cot_far)
    cot = jnp.concatenate([cot_blocks[0], cot_got[0], cot_far[0], cot_far[1]], axis=0)
    layer_out, dz2, dffn, sums_two = pl.pallas_call(
        close_kernel,
        out_shape=(act(BF), act(F32), act(BF), sds((8, width), F32)),
        in_specs=[VM] * 5,
        out_specs=(VM,) * 4,
        compiler_params=params(),
        cost_estimate=cost(1, 1),
        name="close",
    )(ffn, to_core(give), first, cot, norms)
    dffn_other = to_core(dffn)

    def ffn_back(pieces, acc):
        whole = lambda count: pl.BlockSpec((count * rows, width), lambda i: (0, 0))
        return pl.pallas_call(
            functools.partial(ffn_back_kernel, slab),
            grid=(1,),
            out_shape=(
                sds((2 * rows, width), F32),
                act(BF),
                sds((2, pair, 2, slab, 3 * inner), BF),
                sds((2, pair, 2, slab, 3 * inner), BF),
            ),
            in_specs=[whole(2)] + [whole(1)] * 4 + [ANY] * 4,
            out_specs=(whole(2), whole(1), ANY, ANY),
            scratch_shapes=[
                pltpu.VMEM((pair, width, 2 * inner), BF),
                pltpu.VMEM((width, pair * inner), BF),
                pltpu.VMEM((2 * rows, width), BF),
                pltpu.VMEM((2 * rows, width), BF),
                pltpu.VMEM((pair, 2 * rows, 2 * inner), F32),
                pltpu.VMEM((2 * rows, pair * inner), BF),
                pltpu.VMEM((pair, width, 3 * inner), BF),
                dma((pair, 2, 8)),
                dma((pair, 8)),
            ],
            compiler_params=params(),
            cost_estimate=cost(1, 1),
            name="ffn_back",
        )(acc, flow, flow_other, dffn, dffn_other, *pieces)

    def attend_back(base, q, dat):
        stat = pl.BlockSpec((1, 8, rows), lambda i: (i + base, 0, 0))
        keep_spec = pl.BlockSpec((4, rows, 3 * LANES), lambda i: (0, 0, i))
        return pl.pallas_call(
            functools.partial(attend_back_kernel, scale),
            grid=(pair,),
            out_shape=(
                sds((4, rows, pair * 3 * LANES), BF),
                sds((4, rows, pair * 3 * LANES), BF),
                sds((rows, pair * 2 * LANES), BF),
            ),
            in_specs=[
                at_spec(base, 2 * LANES),
                at_spec(base, 2 * LANES),
                stat,
                stat,
                pl.BlockSpec((rows, 8), lambda i: (0, 0)),
                pl.BlockSpec((4, rows, LANES), lambda i: (0, 0, 0)),
            ]
            + [at_spec(base, 3 * LANES)] * 8,
            out_specs=(keep_spec, keep_spec, at_spec(0, 2 * LANES)),
            compiler_params=params(),
            cost_estimate=cost(1, 1),
            name="attend_back",
        )(q, dat, lse, delta, bias_t, tables, *kv_all)

    out_blocks = [layer_out[j * part : (j + 1) * part] for j in range(planes)]
    near_out = Hop(jnp.stack([out_blocks[1], out_blocks[3]]), 0, 1)
    dfirst, _, keep, go = ffn_back(high, jnp.zeros((2 * rows, width), F32))
    high_sum = Scatter(keep, go, 1)
    dfirst = tick(dfirst, [], [high_sum, near_out])
    dfirst, give, keep, go = ffn_back(low, dfirst)
    low_sum = Scatter(keep, go, 1)
    give_hop = Hop(give, CORE)
    dfirst = tick(dfirst, [near_out], [give_hop, low_sum])
    dfirst = tick(dfirst, [give_hop], [])
    dz1, dat, delta, sums = pl.pallas_call(
        functools.partial(branch_back_kernel, planes),
        grid=(1,),
        out_shape=(
            act(F32),
            sds((rows, planes * 2 * LANES), BF),
            sds((planes, 8, rows), F32),
            sds((8, width), F32),
        ),
        in_specs=[pl.BlockSpec((rows, width), lambda i: (0, 0))] + [VM] * 7 + [ANY] * 8,
        out_specs=(VM,) * 4,
        scratch_shapes=w_scratch,
        compiler_params=params(),
        cost_estimate=cost(1, 1),
        name="branch_back",
    )(dfirst, give_hop.got, dz2, scaled, inv, norms, sums_two, att, *weights)

    stages = [Sum(sums, CORE)]

    def next_sum(dp_mask, mp_mask=0):
        stages.append(Sum(stages[-1].got, dp_mask, mp_mask))
        return stages[-1]

    far_out = Hop(jnp.stack([out_blocks[2], near_out.got[1]]), 0, 2)
    dat = tick(dat, [high_sum], [high_sum, stages[0], far_out])
    keep, send, high_dq = attend_back(pair, q, dat)
    high_keys = Scatter(keep, send)
    dat, high_dq = fence(dat, high_dq)
    dat = tick(
        dat, [stages[0], far_out, low_sum], lambda: [high_keys, low_sum, next_sum(XBIT)]
    )
    keep, send, low_dq = attend_back(0, q, dat)
    low_keys = Scatter(keep, send)
    low_dq = tick(low_dq, [high_keys, stages[1]], lambda: [high_keys, low_keys, next_sum(YBIT)])
    low_dq, high_sum.back, low_sum.back = fence(low_dq, high_sum.back, low_sum.back)
    high_total, low_total = high_sum.total(), low_sum.total()
    far = [Hop(high_total[k], 0, 2 + k) for k in range(2)]
    near = Hop(low_total[1], 0, 1)
    low_dq = tick(low_dq, [], [far[0], near])

    def grads_shape(count):
        return sds((4, count, slab, 3 * LANES), BF)

    din, keep, send = pl.pallas_call(
        functools.partial(query_back_kernel, planes, slab),
        out_shape=(act(F32), grads_shape(planes), grads_shape(planes)),
        in_specs=[VM] * 5 + [ANY] * 8,
        out_specs=(VM, ANY, ANY),
        scratch_shapes=[
            pltpu.VMEM((planes, width, 6 * LANES), BF),
            pltpu.VMEM((planes, width, 3 * LANES), BF),
            dma((planes, 8)),
            dma((planes, 8)),
        ],
        compiler_params=params(),
        cost_estimate=cost(1, 1),
        name="query_back",
    )(x, low_dq, high_dq, dz1, att_low, *weights)
    queries = Scatter(keep, send)
    din = tick(din, [high_keys], [high_keys])
    din = tick(din, [low_keys, stages[2], near], [queries])
    din, high_keys.back = fence(din, high_keys.back)
    din = tick(din, [], [low_keys])

    def kv_back(base, sum_, din, out_type):
        din, keep, send = pl.pallas_call(
            functools.partial(kv_back_kernel, base, pair, slab),
            out_shape=(act(out_type), grads_shape(pair), grads_shape(pair)),
            in_specs=[VM] * 5 + [ANY] * 8,
            out_specs=(VM, ANY, ANY),
            scratch_shapes=[
                pltpu.VMEM((pair, width, 6 * LANES), BF),
                pltpu.VMEM((pair, width, 3 * LANES), BF),
                dma((pair, 8)),
                dma((pair, 8)),
            ],
            compiler_params=params(),
            cost_estimate=cost(1, 1),
            name="kv_back",
        )(x, din, tables, sum_.keep, sum_.back, *weights)
        return din, Scatter(keep, send)

    din, high_w = kv_back(pair, high_keys, din, F32)
    din = tick(din, [low_keys], [low_keys, high_w])
    din = tick(din, [queries, far[0]], [far[1]])
    din = tick(din, [high_w], [])
    din, low_keys.back = fence(din, low_keys.back)
    din = tick(din, [], [queries, high_w])
    din, low_w = kv_back(0, low_keys, din, BF)
    din_blocks = [din[j * part : (j + 1) * part] for j in range(planes)]
    near_din = Hop(jnp.stack([din_blocks[1], din_blocks[3]]), 0, 1)
    carry = tick(din, [far[1]], [low_w, near_din])
    carry = tick(carry, [low_w, high_w, near_din], [low_w, high_w])
    far_din = Hop(jnp.stack([din_blocks[2], near_din.got[1]]), 0, 2)
    ffn_sum = low_total[0].astype(F32) + near.got.astype(F32)
    ffn_sum = ffn_sum + far[0].got.astype(F32) + far[1].got.astype(F32)
    last_hop = Hop(ffn_sum[1].astype(BF), CORE)
    carry = tick(carry, [queries], [queries, far_din, last_hop])
    carry, high_w.back = fence(carry, high_w.back)
    v_high = high_w.total()
    v_hops = [Hop(v_high[k], 0, 2 + k) for k in range(2)]
    carry = tick(carry, [low_w, far_din, last_hop], [low_w] + v_hops)
    norm_sums = lax.dynamic_slice_in_dim(stages[2].got, dp * slab, slab, 1)
    rider = jnp.pad(norm_sums.astype(BF), ((0, 8), (0, 3 * LANES - slab)))
    carry, queries.back = fence(carry, queries.back)
    q_total = jnp.concatenate(
        [queries.total(), jnp.broadcast_to(rider, (planes,) + rider.shape)], axis=1
    )
    q_hops = [Hop(q_total[j], 0, j) for j in others]
    carry = tick(carry, [], q_hops[:2])
    mine_sum, other_sum = ffn_sum[0], last_hop.got.astype(F32)
    even, odd = jnp.where(core == 0, mine_sum, other_sum), jnp.where(core == 0, other_sum, mine_sum)
    join = lambda k: cat(even[:, k * inner : (k + 1) * inner], odd[:, k * inner : (k + 1) * inner])
    gate_up_grad = jnp.stack([join(0), join(1)])
    down_grad = join(2).T
    carry, gate_up_grad, down_grad = fence(carry, gate_up_grad, down_grad)
    carry, low_w.back = fence(carry, low_w.back)
    v_low = low_w.total()
    v_near = Hop(v_low[1], 0, 1)
    carry = tick(carry, [q_hops[0]] + v_hops[:1], [v_near, q_hops[2]])
    carry = tick(carry, [v_near] + v_hops[1:] + q_hops[1:], [])
    wide = lambda values: sum(value.astype(F32) for value in values)
    q_all = wide([q_total[0]] + [hop.got for hop in q_hops])
    qo_grad, sums = q_all[:slab], q_all[slab:, :slab]
    kv_grad = wide([v_low[0]] + [hop.got for hop in [v_near] + v_hops])

    def in_order(own, near_hop, far_hop):
        got = jnp.stack([own, near_hop.got[0], far_hop.got[0], far_hop.got[1]])
        return jnp.stack(
            [lax.dynamic_index_in_dim(got, mine[m], 0, keepdims=False) for m in range(planes)]
        )

    layer_rows = in_order(out_blocks[0], near_out, far_out)
    input_grad = in_order(din_blocks[0], near_din, far_din)
    shape = hidden_in.shape
    heads = 3 * HEAD_DIM
    qkv_grad = jnp.stack(
        [
            qo_grad[:, :heads],
            kv_grad[:, :heads],
            cat(kv_grad[:, 2 * LANES :], kv_grad[:, heads : 2 * LANES]),
        ]
    )
    out_grad = cat(qo_grad[:, 2 * LANES :], qo_grad[:, heads : 2 * LANES]).T
    return (
        layer_rows.reshape(shape),
        input_grad.reshape(shape).astype(F32),
        qkv_grad,
        out_grad,
        gate_up_grad,
        down_grad,
        sums[0:2],
        sums[2:4],
    )


def rope_tables(positions, half_dim):
    exponent = jnp.arange(half_dim, dtype=jnp.float32) * (1.0 / half_dim)
    inverse = jnp.power(rope_base, -exponent)
    angles = positions[:, None] * inverse[None, :]
    return (jnp.cos(angles), jnp.sin(angles))


def rotate(vectors, cosine, sine_table):
    half_dim = vectors.shape[-1] // 2
    first_half = vectors[..., :half_dim]
    second_half = vectors[..., half_dim:]
    return jnp.concatenate(
        [
            first_half * cosine - second_half * sine_table,
            second_half * cosine + first_half * sine_table,
        ],
        axis=-1,
    )


def rotate_back(gradient, cosine, sine_table):
    half_dim = gradient.shape[-1] // 2
    first_half = gradient[..., :half_dim]
    second_half = gradient[..., half_dim:]
    return jnp.concatenate(
        [
            first_half * cosine + second_half * sine_table,
            second_half * cosine - first_half * sine_table,
        ],
        axis=-1,
    )


def normalize(residual_stream, gain_row, bias_row):
    center = residual_stream - jnp.mean(residual_stream, axis=-1, keepdims=True)
    inv_std = lax.rsqrt(jnp.mean(center * center, axis=-1, keepdims=True) + norm_eps)
    scaled = center * inv_std
    return (scaled * gain_row + bias_row, scaled, inv_std)


def normalize_back(upstream, scaled, inv_std, gain_row):
    d_scaled = upstream * gain_row
    d_stream = inv_std * (
        d_scaled
        - jnp.mean(d_scaled, axis=-1, keepdims=True)
        - scaled * jnp.mean(d_scaled * scaled, axis=-1, keepdims=True)
    )
    return (d_stream, jnp.sum(upstream * scaled, axis=(0, 1)), jnp.sum(upstream, axis=(0, 1)))


def split_heads(rows, head_dim):
    return rows.reshape(
        rows.shape[0], rows.shape[1], rows.shape[2] // head_dim, head_dim
    ).transpose(1, 2, 0, 3)


def merge_heads(heads):
    return heads.transpose(2, 0, 1, 3).reshape(
        heads.shape[2], heads.shape[0], heads.shape[1] * heads.shape[3]
    )


def score_grads(
    query_part, grad_part, lse_part, delta_part, key_part, value_part, mask_part, score_scale
):
    scores = (
        jnp.einsum("shqd,shkd->shqk", query_part, key_part, preferred_element_type=jnp.float32)
        * score_scale
    )
    prob_full = jnp.where(mask_part, jnp.exp(scores - lse_part[..., None]), 0.0)
    d_probs = jnp.einsum(
        "shqd,shkd->shqk", grad_part, value_part, preferred_element_type=jnp.float32
    )
    d_scores = (prob_full * (d_probs - delta_part[..., None]) * score_scale).astype(jnp.bfloat16)
    return (d_scores, prob_full.astype(jnp.bfloat16))


def body(
    hidden_in,
    cotangent,
    lengths,
    qkv_weight,
    out_weight,
    gate_up_weight,
    down_weight,
    norm_gain,
    norm_bias,
):
    query_key_value_matrix, output_matrix, gate_up_matrix, down_matrix, gain_rows, bias_rows = (
        lax.all_gather(qkv_weight, "dp", axis=1, tiled=True),
        lax.all_gather(out_weight, "dp", axis=1, tiled=True),
        lax.all_gather(gate_up_weight, "dp", axis=1, tiled=True),
        lax.all_gather(down_weight, "dp", axis=1, tiled=True),
        lax.all_gather(norm_gain, "dp", axis=1, tiled=True),
        lax.all_gather(norm_bias, "dp", axis=1, tiled=True),
    )
    gain_rows = gain_rows.astype(jnp.float32)
    bias_rows = bias_rows.astype(jnp.float32)
    group_size = lax.axis_size("dp")
    group_rank = lax.axis_index("dp")
    model_rank = lax.axis_index("mp")
    local_rows = hidden_in.shape[1]
    slots = local_rows * lax.axis_size("mp")
    seq_total = slots * group_size
    head_dim = HEAD_DIM
    score_scale = head_dim ** (-0.5)
    span = min(group_size, 8)
    block_keys = slots * span
    key_blocks = group_size // span
    own_first = group_rank * slots
    positions = (own_first + jnp.arange(slots, dtype=jnp.int32)).astype(jnp.float32)
    cosine, sine_table = rope_tables(positions, head_dim // 2)
    acc_qkv = jnp.zeros(query_key_value_matrix.shape, jnp.float32)
    acc_out = jnp.zeros(output_matrix.shape, jnp.float32)
    acc_gate_up = jnp.zeros(gate_up_matrix.shape, jnp.float32)
    acc_down = jnp.zeros(down_matrix.shape, jnp.float32)
    acc_gain = jnp.zeros(gain_rows.shape, jnp.float32)
    acc_bias = jnp.zeros(bias_rows.shape, jnp.float32)
    layer_rows = []
    input_rows = []
    for micro_step in range(hidden_in.shape[0]):
        x_rows, grad_rows = (
            lax.all_gather(hidden_in[micro_step], "mp", axis=0, tiled=True),
            lax.all_gather(cotangent[micro_step], "mp", axis=0, tiled=True),
        )
        seq_lengths = lengths[micro_step]

        def allowed_keys(first_row, row_count):
            key_pos = first_row + jnp.arange(row_count, dtype=jnp.int32)
            return (key_pos[None, :] < seq_lengths[:, None])[:, None, None, :]

        projected_rows = jnp.einsum(
            "rsd,cde->rsce", x_rows, query_key_value_matrix, preferred_element_type=jnp.float32
        )
        q_heads = rotate(split_heads(projected_rows[:, :, 0], head_dim), cosine, sine_table).astype(
            jnp.bfloat16
        )
        k_heads = rotate(split_heads(projected_rows[:, :, 1], head_dim), cosine, sine_table).astype(
            jnp.bfloat16
        )
        v_heads = split_heads(projected_rows[:, :, 2], head_dim).astype(jnp.bfloat16)
        head_shape = q_heads.shape
        buffer_shape = (head_shape[0], head_shape[1], seq_total, head_shape[3])
        forward_first_row = jnp.int32(0)
        run_max = jnp.full(head_shape[:3], masked_score, jnp.float32)
        key_part = lax.all_gather(k_heads, "dp", axis=2, tiled=True)
        value_part = lax.all_gather(v_heads, "dp", axis=2, tiled=True)
        forward_row_count = key_part.shape[2]
        forward_key_buffer = key_part
        forward_value_buffer = value_part
        old_max = run_max
        allowed = allowed_keys(forward_first_row, forward_row_count)
        scores = (
            jnp.einsum("shqd,shkd->shqk", q_heads, key_part, preferred_element_type=jnp.float32)
            * score_scale
        )
        scores = jnp.where(allowed, scores, masked_score)
        new_max = jnp.maximum(old_max, jnp.max(scores, axis=-1))
        weights_block = jnp.where(allowed, jnp.exp(scores - new_max[..., None]), 0.0)
        new_sum = jnp.sum(weights_block, axis=-1)
        new_acc = jnp.einsum(
            "shqk,shkd->shqd",
            weights_block.astype(jnp.bfloat16),
            value_part,
            preferred_element_type=jnp.float32,
        )
        run_max = new_max
        key_buffer = forward_key_buffer
        value_buffer = forward_value_buffer
        lse = run_max + jnp.log(new_sum)
        attended = new_acc / new_sum[..., None]
        attended_reduced = merge_heads(attended).astype(jnp.bfloat16)
        residual_branch = lax.psum(
            jnp.einsum(
                "rsf,fd->rsd", attended_reduced, output_matrix, preferred_element_type=jnp.float32
            ).astype(jnp.bfloat16),
            "mp",
        ).astype(jnp.float32)
        attention_normed, scaled_one, inv_std_one = normalize(
            x_rows.astype(jnp.float32) + residual_branch, gain_rows[0], bias_rows[0]
        )
        first_low = attention_normed.astype(jnp.bfloat16)
        gate_up_rows = jnp.einsum(
            "rsd,cdf->rscf", first_low, gate_up_matrix, preferred_element_type=jnp.float32
        )
        gate_part = gate_up_rows[:, :, 0]
        up_part = gate_up_rows[:, :, 1]
        sigmoid_gate = jax.nn.sigmoid(gate_part)
        silu_gate = gate_part * sigmoid_gate
        hidden_rows = (silu_gate * up_part).astype(jnp.bfloat16)
        feedforward_output = lax.psum(
            jnp.einsum(
                "rsf,fd->rsd", hidden_rows, down_matrix, preferred_element_type=jnp.float32
            ).astype(jnp.bfloat16),
            "mp",
        ).astype(jnp.float32)
        output, scaled_two, inv_std_two = normalize(
            attention_normed + feedforward_output, gain_rows[1], bias_rows[1]
        )
        layer_rows.append(
            lax.dynamic_slice_in_dim(output, model_rank * local_rows, local_rows, 0).astype(
                jnp.bfloat16
            )
        )
        d_z2, gain_two, bias_two = normalize_back(
            grad_rows.astype(jnp.float32), scaled_two, inv_std_two, gain_rows[1]
        )
        d_ffn = d_z2.astype(jnp.bfloat16)
        acc_down = acc_down + jnp.einsum(
            "rsf,rsd->fd", hidden_rows, d_ffn, preferred_element_type=jnp.float32
        )
        d_hidden = jnp.einsum("rsd,fd->rsf", d_ffn, down_matrix, preferred_element_type=jnp.float32)
        d_gate = d_hidden * up_part * sigmoid_gate * (1.0 + gate_part * (1.0 - sigmoid_gate))
        d_up = d_hidden * silu_gate
        d_gate_up = jnp.stack([d_gate, d_up], axis=2).astype(jnp.bfloat16)
        acc_gate_up = acc_gate_up + jnp.einsum(
            "rsd,rscf->cdf", first_low, d_gate_up, preferred_element_type=jnp.float32
        )
        d_first = (
            lax.psum(
                jnp.einsum(
                    "rscf,cdf->rsd", d_gate_up, gate_up_matrix, preferred_element_type=jnp.float32
                ).astype(jnp.bfloat16),
                "mp",
            ).astype(jnp.float32)
            + d_z2
        )
        d_z1, gain_one, bias_one = normalize_back(d_first, scaled_one, inv_std_one, gain_rows[0])
        acc_gain = acc_gain + jnp.stack([gain_one, gain_two])
        acc_bias = acc_bias + jnp.stack([bias_one, bias_two])
        d_branch = d_z1.astype(jnp.bfloat16)
        acc_out = acc_out + jnp.einsum(
            "rsf,rsd->fd", attended_reduced, d_branch, preferred_element_type=jnp.float32
        )
        d_attended = split_heads(
            jnp.einsum("rsd,fd->rsf", d_branch, output_matrix, preferred_element_type=jnp.float32),
            head_dim,
        ).astype(jnp.bfloat16)
        delta = jnp.sum(d_attended.astype(jnp.float32) * attended, axis=-1)
        zero_heads = jnp.zeros(head_shape, jnp.float32)

        def query_block(step_index, partial_sums):
            first_row = step_index * block_keys
            key_part = lax.dynamic_slice_in_dim(key_buffer, first_row, block_keys, 2)
            value_part = lax.dynamic_slice_in_dim(value_buffer, first_row, block_keys, 2)
            d_scores, prob_block = score_grads(
                q_heads,
                d_attended,
                lse,
                delta,
                key_part,
                value_part,
                allowed_keys(first_row, block_keys),
                score_scale,
            )
            d_query = partial_sums[0] + jnp.einsum(
                "shqk,shkd->shqd", d_scores, key_part, preferred_element_type=jnp.float32
            )
            key_total = lax.dynamic_update_slice_in_dim(
                partial_sums[1],
                jnp.einsum(
                    "shqk,shqd->shkd", d_scores, q_heads, preferred_element_type=jnp.float32
                ),
                first_row,
                2,
            )
            value_total = lax.dynamic_update_slice_in_dim(
                partial_sums[2],
                jnp.einsum(
                    "shqk,shqd->shkd", prob_block, d_attended, preferred_element_type=jnp.float32
                ),
                first_row,
                2,
            )
            return (d_query, key_total, value_total)

        zero_keys = jnp.zeros(buffer_shape, jnp.float32)
        d_query, key_total, value_total = lax.fori_loop(
            0, key_blocks, query_block, (zero_heads, zero_keys, zero_keys)
        )
        d_key, d_value = (
            lax.psum_scatter(key_total, "dp", scatter_dimension=2, tiled=True),
            lax.psum_scatter(value_total, "dp", scatter_dimension=2, tiled=True),
        )
        d_projected = jnp.stack(
            [
                merge_heads(rotate_back(d_query, cosine, sine_table)),
                merge_heads(rotate_back(d_key, cosine, sine_table)),
                merge_heads(d_value),
            ],
            axis=2,
        ).astype(jnp.bfloat16)
        acc_qkv = acc_qkv + jnp.einsum(
            "rsd,rsce->cde", x_rows, d_projected, preferred_element_type=jnp.float32
        )
        d_input = lax.psum_scatter(
            jnp.einsum(
                "rsce,cde->rsd",
                d_projected,
                query_key_value_matrix,
                preferred_element_type=jnp.float32,
            ).astype(jnp.bfloat16),
            "mp",
            scatter_dimension=0,
            tiled=True,
        ).astype(jnp.float32)
        input_rows.append(
            d_input + lax.dynamic_slice_in_dim(d_z1, model_rank * local_rows, local_rows, 0)
        )
    qkv_grad, out_grad, gate_up_grad, down_grad, gain_grad, bias_grad = (
        lax.psum_scatter(acc_qkv, "dp", scatter_dimension=1, tiled=True),
        lax.psum_scatter(acc_out, "dp", scatter_dimension=1, tiled=True),
        lax.psum_scatter(acc_gate_up, "dp", scatter_dimension=1, tiled=True),
        lax.psum_scatter(acc_down, "dp", scatter_dimension=1, tiled=True),
        lax.psum_scatter(acc_gain, "dp", scatter_dimension=1, tiled=True),
        lax.psum_scatter(acc_bias, "dp", scatter_dimension=1, tiled=True),
    )
    return (
        jnp.stack(layer_rows),
        jnp.stack(input_rows),
        qkv_grad,
        out_grad,
        gate_up_grad,
        down_grad,
        gain_grad,
        bias_grad,
    )


def solution(mesh):
    rows_of = dict(mesh.shape)
    by_plane = rows_of == {"dp": 8, "mp": 4}
    return jax.shard_map(
        plane_body if by_plane else body,
        mesh=mesh,
        in_specs=(
            P(None, ("dp", "mp"), None, None),
            P(None, ("dp", "mp"), None, None),
            P(),
            P(None, "dp", "mp"),
            P("mp", "dp"),
            P(None, "dp", "mp"),
            P("mp", "dp"),
            P(None, "dp"),
            P(None, "dp"),
        ),
        out_specs=(
            P(None, ("dp", "mp"), None, None),
            P(None, ("dp", "mp"), None, None),
            P(None, "dp", "mp"),
            P("mp", "dp"),
            P(None, "dp", "mp"),
            P("mp", "dp"),
            P(None, "dp"),
            P(None, "dp"),
        ),
        check_vma=False,
    )
```
